256 devices in a mesh: seq: 64 (over z, y, x_lo), mp: 4 (over x_hi, core).
Axes of the slice: x: 4 (x_hi: 2, x_lo: 2; x = x_hi * 2 + x_lo), y: 4, z: 8, core: 2. Of those that a mesh axis runs over, the one named last changes fastest.
Arguments:
- inputs: bfloat16 [32, 4, 2048], replicated, may hold values from -3 to 3
- w_qkv: bfloat16 [3, 2048, 2048], P(None, None, 'mp'), may hold values from -0.125 to 0.125
- w_out: bfloat16 [2048, 2048], P('mp'), may hold values from -0.125 to 0.125
- w_gate_up: bfloat16 [2, 2048, 4096], P(None, None, 'mp'), may hold values from -0.125 to 0.125
- w_down: bfloat16 [4096, 2048], P('mp'), may hold values from -0.09375 to 0.09375
- cache_keys: bfloat16 [32, 8192, 2048], P(None, 'seq', 'mp'), may hold values from -256 to 256
- cache_values: bfloat16 [32, 8192, 2048], P(None, 'seq', 'mp'), may hold values from -6 to 6
- lengths: int32 [32], replicated, may hold values from 1 to 8192, as said below
Outputs:
- hidden: bfloat16 [32, 4, 2048], P(None, None, 'mp')
- queries: bfloat16 [32, 4, 2048], P(None, None, 'mp')
- new_keys: bfloat16 [32, 4, 2048], P(None, None, 'mp')
- new_values: bfloat16 [32, 4, 2048], P(None, None, 'mp')
The draws below stay inside these ranges and needn't reach their ends.
Inputs may be any that keep to these rules, and one draw needn't show every extreme that they name: `lengths`: half of the 32 requests hold 1 to 512 cached positions, the others 8192 - 8192 // 8 to 8192; one request holds exactly 8192.
All inputs are finite; a program needn't handle non-finite values.
Results may differ from the reference program's by a relative error of at most 0.015.
The reference program's roundings to bfloat16 on the way count: a program that leaves them out, or rounds other values in their place, can miss the bound.
Values may be sent and summed in bfloat16 or wider, within the bound.
No kernel may reach another device: no remote copies, remote signals or barrier semaphores. Data moves between devices by JAX's collectives and lax.ppermute only.
A program may use at most 128 MiB of HBM per device.

```python
import jax
import jax.numpy as jnp
from jax import lax

D = 2048
H = 16
DH = 128
FF = 4096
STEPS = 4
REQS = 32
CACHE = 8192


def draw_cache_keys(key, part):
    normal_key = jax.random.fold_in(key, 0)
    full_shape = (REQS, CACHE, H * DH)
    return jnp.clip(2.5 * jax.random.normal(normal_key, full_shape, jnp.float32), -15.0, 15.0).astype(jnp.bfloat16)


def draw_lengths(key, part):
    short_key, long_key, order_key = jax.random.split(key, 3)
    short_lens = jax.random.randint(short_key, (REQS,), 1, CACHE // 16 + 1)
    long_lens = jax.random.randint(long_key, (REQS,), CACHE - CACHE // 8, CACHE + 1)
    ranking = jax.random.permutation(order_key, REQS)
    chosen = jnp.where(ranking < REQS // 2, long_lens, short_lens)
    return jnp.where(ranking == 0, CACHE, chosen).astype(jnp.int32)


def steps_of(rng, dims, shards, smallest, top_value):
    level, own = 1.0, jax.random.fold_in(rng, 6)
    for position, shards_of in shards:
        heights = jnp.exp(jax.random.uniform(jax.random.fold_in(own, position), (shards_of,), jnp.float32, smallest / len(shards), top_value / len(shards)))
        level = level * jnp.repeat(heights, dims[position] // shards_of).reshape([-1 if axis == position else 1 for axis in range(len(dims))])
    return level


def scatter_about(key, extent, deviation, reach, cuts=(), kind=jnp.bfloat16):
    drawn = deviation * jax.random.normal(key, extent, jnp.float32)
    if cuts:
        drawn = drawn * steps_of(key, extent, cuts, -0.22, 0.18)
    return jnp.clip(drawn, -reach, reach).astype(kind)


def setup_inputs(seed: int = 0) -> dict:
    key_list = jax.random.split(jax.random.key(seed), 9)
    inputs = scatter_about(key_list[0], (REQS, STEPS, D), 0.5, 3.0)
    w_qkv = scatter_about(key_list[1], (3, D, H * DH), D ** -0.5, 0.125, ((2, 4),))
    w_out = scatter_about(key_list[2], (H * DH, D), (H * DH) ** -0.5, 0.125, ((0, 4),))
    w_gate_up = scatter_about(key_list[3], (2, D, FF), D ** -0.5, 0.125, ((2, 4),))
    w_down = scatter_about(key_list[4], (FF, D), FF ** -0.5, 0.09375, ((0, 4),))
    cache_keys = draw_cache_keys(jax.random.fold_in(key_list[8], 71), 0)
    cache_values = scatter_about(key_list[6], (REQS, CACHE, H * DH), 1.0, 6.0, ((1, 64), (2, 4)))
    lengths = draw_lengths(jax.random.fold_in(key_list[8], 71), 0)
    return dict(inputs=inputs, w_qkv=w_qkv, w_out=w_out, w_gate_up=w_gate_up, w_down=w_down, cache_keys=cache_keys, cache_values=cache_values, lengths=lengths)


neg_fill = -1e+30
norm_eps = 1e-05
rope_base = 10000.0

def layer_norm(values):
    average = lax.optimization_barrier(jnp.mean(values, axis=-1, keepdims=True))
    centred = values - average
    variance = lax.optimization_barrier(jnp.mean(centred * centred, axis=-1, keepdims=True))
    return centred * lax.rsqrt(variance + norm_eps)

def rotate(values, positions):
    head_dim = values.shape[-1]
    half_dim = head_dim // 2
    inverse = rope_base ** (-2.0 * jnp.arange(half_dim, dtype=jnp.float32) / head_dim)
    angles = positions.astype(jnp.float32)[..., None] * inverse
    angles = jnp.concatenate([angles, angles], axis=-1)[..., None, :]
    turned = jnp.concatenate([-values[..., half_dim:], values[..., :half_dim]], axis=-1)
    return values * jnp.cos(angles) + turned * jnp.sin(angles)

def project(inputs, w_qkv, lengths):
    batch_rows, step_count, model_width = inputs.shape
    normed = layer_norm(inputs.astype(jnp.float32)).astype(jnp.bfloat16)
    flat_rows = normed.reshape(batch_rows * step_count, model_width)
    triple = jnp.einsum('rd,jdk->jrk', flat_rows.astype(jnp.float32), w_qkv.astype(jnp.float32))
    triple = triple.reshape(3, batch_rows, step_count, -1, DH)
    positions = lengths[:, None] + jnp.arange(step_count, dtype=jnp.int32)[None, :]
    queries = rotate(triple[0], positions).astype(jnp.bfloat16)
    new_keys = rotate(triple[1], positions).astype(jnp.bfloat16)
    return (queries, new_keys, triple[2].astype(jnp.bfloat16))

def reference(inputs, w_qkv, w_out, w_gate_up, w_down, cache_keys, cache_values, lengths):
    batch_rows, step_count, model_width = inputs.shape
    queries, new_keys, new_values = project(inputs, w_qkv, lengths)
    head_count = queries.shape[2]
    step_ids = jnp.arange(step_count, dtype=jnp.int32)
    places = jnp.arange(CACHE + step_count, dtype=jnp.int32)

    def one_request(packed):
        query_rows, keys_old, values_old, keys_new, values_new, length_now = packed
        keys_all = jnp.concatenate([keys_old.reshape(CACHE, head_count, DH), keys_new], axis=0).astype(jnp.float32)
        values_all = jnp.concatenate([values_old.reshape(CACHE, head_count, DH), values_new], axis=0).astype(jnp.float32)
        scores = jnp.einsum('thd,khd->thk', query_rows.astype(jnp.float32), keys_all) * DH ** (-0.5)
        live = jnp.where(places[None, :] < CACHE, places[None, :] < length_now, places[None, :] - CACHE <= step_ids[:, None])[:, None, :]
        highest = lax.optimization_barrier(jnp.max(jnp.where(live, scores, neg_fill), axis=-1))
        weights = jnp.where(live, jnp.exp(scores - highest[..., None]), 0.0)
        totals = lax.optimization_barrier(jnp.sum(weights, axis=-1))
        rounded = lax.optimization_barrier(weights.astype(jnp.bfloat16)).astype(jnp.float32)
        summed = jnp.einsum('thk,khd->thd', rounded, values_all)
        return (summed / totals[..., None]).astype(jnp.bfloat16).reshape(step_count, head_count * DH)
    context = lax.map(one_request, (queries, cache_keys, cache_values, new_keys, new_values, lengths))
    flat_count = batch_rows * step_count
    middle = inputs.reshape(flat_count, model_width).astype(jnp.float32) + jnp.dot(context.reshape(flat_count, -1), w_out, preferred_element_type=jnp.float32)
    normed = layer_norm(middle).astype(jnp.bfloat16)
    gate_up = jnp.einsum('rd,jdf->jrf', normed.astype(jnp.float32), w_gate_up.astype(jnp.float32))
    active = (jax.nn.silu(gate_up[0]) * gate_up[1]).astype(jnp.bfloat16)
    hidden = (middle + jnp.dot(active, w_down, preferred_element_type=jnp.float32)).astype(jnp.bfloat16)
    head_width = head_count * DH
    return (hidden.reshape(batch_rows, step_count, model_width), queries.reshape(batch_rows, step_count, head_width), new_keys.reshape(batch_rows, step_count, head_width), new_values.reshape(batch_rows, step_count, head_width))
```

```python
import functools

import jax
import jax.numpy as jnp
import numpy as np
from jax import lax
from jax.experimental import pallas as pl
from jax.experimental.pallas import tpu as pltpu
from jax.sharding import PartitionSpec as P

DH = 128
NEG = -1e30
EPS = 1e-05
SCALE = DH ** (-0.5)
F32 = jnp.float32
BF16 = jnp.bfloat16


def norm_rows(x):
    centred = x - jnp.mean(x, axis=-1, keepdims=True)
    variance = jnp.mean(centred * centred, axis=-1, keepdims=True)
    return centred * lax.rsqrt(variance + EPS)


def split3(v):
    a = v.astype(BF16).astype(F32)
    rest = v - a
    b = rest.astype(BF16).astype(F32)
    return a, b, rest - b


def local_kernel(
    reqs, steps, block, width,
    len_ref, x_hbm, w_hbm, ck_hbm, cv_hbm, freq_ref,
    q_out, k_out, v_out, part_out, fresh_out,
    x_v, w_v, ck_v, cv_v, xs, q16, k16, v16, flat, sem_x, sem_w, sem_c,
):
    heads = width // DH
    rows = reqs * steps
    seq = lax.axis_index("seq")
    copy_x = pltpu.make_async_copy(x_hbm, x_v, sem_x)
    copy_x.start()
    copies_w = [pltpu.make_async_copy(w_hbm.at[j], w_v.at[j], sem_w.at[j]) for j in range(3)]
    copies_k = [
        pltpu.make_async_copy(ck_hbm.at[pl.ds(g, reqs // 2)], ck_v.at[pl.ds(g, reqs // 2)], sem_c.at[i])
        for i, g in enumerate((0, reqs // 2))
    ]
    copies_v = [
        pltpu.make_async_copy(cv_hbm.at[pl.ds(g, reqs // 2)], cv_v.at[pl.ds(g, reqs // 2)], sem_c.at[2 + i])
        for i, g in enumerate((0, reqs // 2))
    ]
    copies_w[0].start()
    copies_k[0].start()
    copies_v[0].start()
    copies_k[1].start()
    copies_v[1].start()
    copies_w[1].start()
    copies_w[2].start()

    row_ids = lax.broadcasted_iota(jnp.int32, (rows, DH), 0)
    for r in range(reqs):
        flat[pl.ds(r * steps, steps), :] = jnp.full((steps, DH), len_ref[r], jnp.int32).astype(F32)
    angles = (flat[...] + (row_ids % steps).astype(F32)) * freq_ref[0:1, :]
    lane = lax.broadcasted_iota(jnp.int32, (rows, DH), 1)
    cosine = jnp.cos(angles)
    sine = jnp.sin(angles)
    sine = jnp.where(lane < DH // 2, -sine, sine)

    copy_x.wait()
    for r in range(reqs):
        xs[pl.ds(r * steps, steps), :] = x_v[r].astype(F32)
    normed = norm_rows(xs[...]).astype(BF16)

    def turned(part, head):
        v = part[:, head * DH : (head + 1) * DH]
        return (v * cosine + pltpu.roll(v, DH // 2, 1) * sine).astype(BF16).astype(F32)

    def emit(j, rotated, out, store):
        copies_w[j].wait()
        part = jnp.dot(normed, w_v[j], preferred_element_type=F32)
        for h in range(heads):
            v = turned(part, h) if rotated else part[:, h * DH : (h + 1) * DH].astype(BF16).astype(F32)
            store[pl.ds(h, rows, stride=heads), :] = v
            flat[...] = v
            for r in range(reqs):
                out[r, :, h * DH : (h + 1) * DH] = flat[pl.ds(r * steps, steps), :].astype(BF16)

    emit(0, True, q_out, q16)

    tall = steps * heads
    row_head = lax.broadcasted_iota(jnp.int32, (tall, DH), 0) % heads
    lane16 = lax.broadcasted_iota(jnp.int32, (tall, DH), 1)
    for r in range(reqs):
        if r % (reqs // 2) == 0:
            copies_k[r // (reqs // 2)].wait()
            copies_v[r // (reqs // 2)].wait()
        q = q16[r * tall : (r + 1) * tall, :]
        spread = jnp.concatenate([jnp.where(row_head == h, q, 0.0).astype(BF16) for h in range(heads)], axis=1)
        scores = lax.dot_general(spread, ck_v[r], (((1,), (1,)), ((), ())), preferred_element_type=F32) * SCALE
        live = lane16 < len_ref[r] - seq * block
        highest = jnp.max(jnp.where(live, scores, NEG), axis=-1, keepdims=True)
        weights = jnp.where(live, jnp.exp(scores - highest), 0.0)
        total = jnp.sum(weights, axis=-1, keepdims=True)
        wide = jnp.dot(weights.astype(BF16), cv_v[r], preferred_element_type=F32)
        o = wide[:, 0:DH]
        for h in range(1, heads):
            o = jnp.where(row_head == h, wide[:, h * DH : (h + 1) * DH], o)
        pieces = split3(jnp.broadcast_to(highest, o.shape)) + split3(jnp.broadcast_to(total, o.shape))
        stats = pieces[5]
        for i in range(4, -1, -1):
            stats = jnp.where(lane16 == i, pieces[i], stats)
        half = tall // 2
        for i in range(2):
            part_out[2 * r + i, 0:half, :] = o[i * half : (i + 1) * half].astype(BF16)
            part_out[2 * r + i, half : 2 * half, :] = stats[i * half : (i + 1) * half].astype(BF16)

    emit(1, True, k_out, k16)
    emit(2, False, v_out, v16)

    half = tall // 2
    q = q16[pl.ds(seq * half, half), :]
    step = (seq % 2) * 2 + lax.broadcasted_iota(jnp.int32, (half, 1), 0) // heads
    base = (seq // 2) * tall
    scores = []
    values = []
    for s in range(steps):
        key = k16[pl.ds(base + s * heads, heads), :]
        value = v16[pl.ds(base + s * heads, heads), :]
        key = jnp.concatenate([key, key], axis=0)
        values.append(jnp.concatenate([value, value], axis=0))
        scores.append(jnp.sum(q * key, axis=-1, keepdims=True) * SCALE)
    highest = scores[0]
    for s in range(1, steps):
        highest = jnp.maximum(highest, jnp.where(s <= step, scores[s], NEG))
    total = jnp.zeros_like(highest)
    o = jnp.zeros((half, DH), F32)
    for s in range(steps):
        weight = jnp.where(s <= step, jnp.exp(scores[s] - highest), 0.0)
        total = total + weight
        o = o + weight.astype(BF16).astype(F32) * values[s]
    fresh_out[0] = o
    fresh_out[1] = jnp.broadcast_to(highest, o.shape)
    fresh_out[2] = jnp.broadcast_to(total, o.shape)


def merge_kernel(got_ref, fresh_ref, w_ref, out_ref, ctx_s):
    half = fresh_ref.shape[1]
    heads = half // 2
    stats = got_ref[:, half : 2 * half, :].astype(F32)
    highest = (stats[:, :, 0:1] + stats[:, :, 1:2]) + stats[:, :, 2:3]
    total = (stats[:, :, 3:4] + stats[:, :, 4:5]) + stats[:, :, 5:6]
    fresh_high = fresh_ref[1][:, 0:1]
    top = jnp.maximum(jnp.max(highest, axis=0), fresh_high)
    factor = jnp.exp(highest - top[None])
    fresh_factor = jnp.exp(fresh_high - top)
    whole = jnp.sum(factor * total, axis=0) + fresh_factor * fresh_ref[2][:, 0:1]
    o = jnp.sum(factor * got_ref[:, 0:half, :].astype(F32), axis=0) + fresh_factor * fresh_ref[0]
    ctx_s[...] = o / whole
    ctx = jnp.concatenate([ctx_s[pl.ds(h, 2, stride=heads), :] for h in range(heads)], axis=1)
    out_ref[...] = jnp.dot(ctx.astype(BF16), w_ref[...], preferred_element_type=F32)


def mlp_kernel(x_ref, a_ref, b_ref, c_ref, d_ref, gu_ref, wd_ref, o0, o1, o2, o3, mid_s, down_s):
    seq = lax.axis_index("seq")
    me = lax.axis_index("mp")
    parts = down_s.shape[0]
    cols = down_s.shape[2]
    x = x_ref[seq // 2].astype(F32)
    x = jnp.where(seq % 2 == 0, x[0:2], x[2:4])
    middle = x + ((a_ref[...] + b_ref[...]) + (c_ref[...] + d_ref[...]))
    normed = norm_rows(middle).astype(BF16)
    gate = jnp.dot(normed, gu_ref[0], preferred_element_type=F32)
    up = jnp.dot(normed, gu_ref[1], preferred_element_type=F32)
    active = ((gate / (1.0 + jnp.exp(-gate))) * up).astype(BF16)
    down = jnp.dot(active, wd_ref[...], preferred_element_type=F32)
    for p in range(parts):
        mid_s[p] = middle[:, p * cols : (p + 1) * cols]
        down_s[p] = down[:, p * cols : (p + 1) * cols]
    o0[...] = down_s[me] + mid_s[me]
    o1[...] = down_s[me ^ 1]
    o2[...] = down_s[me ^ 2]
    o3[...] = down_s[me ^ 3]


def to_others(values, axis):
    size = lax.axis_size(axis)
    return [
        lax.ppermute(v, axis, [(i, i ^ k) for i in range(size)]) for k, v in zip(range(1, size), values)
    ]


def per_device(inputs, w_qkv, w_out, w_gate_up, w_down, cache_keys, cache_values, lengths):
    reqs, steps, model = inputs.shape
    block = cache_keys.shape[1]
    width = cache_keys.shape[2]
    heads = width // DH
    rows = reqs * steps
    tall = steps * heads
    n_seq = lax.axis_size("seq")
    n_mp = lax.axis_size("mp")
    assert rows == 2 * n_seq and steps == 4 and n_mp == 4 and tall == 16
    half_dim = DH // 2
    freq = np.float32(10000.0) ** (np.float32(-2.0) * np.arange(half_dim, dtype=np.float32) / np.float32(DH))
    freq = np.broadcast_to(np.concatenate([freq, freq]).astype(np.float32), (8, DH))
    in_hbm = functools.partial(pltpu.with_memory_space_constraint, memory_space=pltpu.HBM)
    any_space = pl.BlockSpec(memory_space=pltpu.HBM)
    vmem = pl.BlockSpec(memory_space=pltpu.VMEM)
    smem = pl.BlockSpec(memory_space=pltpu.SMEM)
    piece = jax.ShapeDtypeStruct((reqs, steps, width), BF16)
    queries, new_keys, new_values, part, fresh = pl.pallas_call(
        functools.partial(local_kernel, reqs, steps, block, width),
        out_shape=(
            piece, piece, piece,
            jax.ShapeDtypeStruct((n_seq, tall, DH), BF16),
            jax.ShapeDtypeStruct((3, tall // 2, DH), F32),
        ),
        in_specs=[smem, any_space, any_space, any_space, any_space, vmem],
        out_specs=(vmem,) * 5,
        scratch_shapes=[
            pltpu.VMEM(inputs.shape, BF16),
            pltpu.VMEM(w_qkv.shape, BF16),
            pltpu.VMEM(cache_keys.shape, BF16),
            pltpu.VMEM(cache_values.shape, BF16),
            pltpu.VMEM((rows, model), F32),
            pltpu.VMEM((rows * heads, DH), F32),
            pltpu.VMEM((rows * heads, DH), F32),
            pltpu.VMEM((rows * heads, DH), F32),
            pltpu.VMEM((rows, DH), F32),
            pltpu.SemaphoreType.DMA,
            pltpu.SemaphoreType.DMA((3,)),
            pltpu.SemaphoreType.DMA((4,)),
        ],
        compiler_params=pltpu.CompilerParams(vmem_limit_bytes=32 << 20),
        name="local_attention",
    )(lengths, *(in_hbm(a) for a in (inputs, w_qkv, cache_keys, cache_values)), jnp.asarray(freq))

    got = lax.all_to_all(part, "seq", 0, 0)

    mine = pl.pallas_call(
        merge_kernel,
        out_shape=jax.ShapeDtypeStruct((2, model), F32),
        in_specs=[vmem, vmem, vmem],
        out_specs=vmem,
        scratch_shapes=[pltpu.VMEM((tall // 2, DH), F32)],
        compiler_params=pltpu.CompilerParams(vmem_limit_bytes=8 << 20),
        name="merge_project",
    )(got, fresh, w_out)
    others = to_others([mine] * 3, "mp")

    cols = model // n_mp
    chunk = jax.ShapeDtypeStruct((2, cols), F32)
    own, *rest = pl.pallas_call(
        mlp_kernel,
        out_shape=(chunk,) * 4,
        in_specs=[vmem] * 7,
        out_specs=(vmem,) * 4,
        scratch_shapes=[pltpu.VMEM((n_mp, 2, cols), F32)] * 2,
        compiler_params=pltpu.CompilerParams(vmem_limit_bytes=20 << 20),
        name="mlp",
    )(inputs, mine, *others, w_gate_up, w_down)
    back = to_others(rest, "mp")
    hidden = ((own + back[0]) + (back[1] + back[2])).astype(BF16)
    hidden = lax.all_to_all(jnp.broadcast_to(hidden[None], (n_seq, 2, cols)), "seq", 0, 0)
    return (hidden.reshape(reqs, steps, cols), queries, new_keys, new_values)


def solution(mesh):
    placed = (
        P(),
        P(None, None, "mp"),
        P("mp", None),
        P(None, None, "mp"),
        P("mp", None),
        P(None, "seq", "mp"),
        P(None, "seq", "mp"),
        P(),
    )
    return jax.shard_map(
        per_device,
        mesh=mesh,
        in_specs=placed,
        out_specs=(P(None, None, "mp"),) * 4,
        check_vma=False,
    )
```

```python
import functools

import jax
import jax.numpy as jnp
import numpy as np
from jax import lax
from jax.experimental import pallas as pl
from jax.experimental.pallas import tpu as pltpu
from jax.sharding import PartitionSpec as P

DH = 128
NEG = -1e30
EPS = 1e-05
SCALE = DH ** (-0.5)
F32 = jnp.float32
BF16 = jnp.bfloat16


def norm_rows(x):
    centred = x - jnp.mean(x, axis=-1, keepdims=True)
    variance = jnp.mean(centred * centred, axis=-1, keepdims=True)
    return centred * lax.rsqrt(variance + EPS)


def split3(v):
    a = v.astype(BF16).astype(F32)
    rest = v - a
    b = rest.astype(BF16).astype(F32)
    return a, b, rest - b


def frequencies():
    half = DH // 2
    values = np.float32(10000.0) ** (np.float32(-2.0) * np.arange(half, dtype=np.float32) / np.float32(DH))
    lane = lax.broadcasted_iota(jnp.int32, (8, DH), 1) % half
    freq = jnp.full((8, DH), float(values[0]), F32)
    for i in range(1, half):
        freq = jnp.where(lane == i, float(values[i]), freq)
    return freq


def turn(v, cosine, sine):
    return v * cosine + pltpu.roll(v, DH // 2, 1) * sine


def rounded(v):
    return v.astype(BF16).astype(F32)


def cached_kernel(
    group, reqs, steps, block, width,
    len_hbm, x_hbm, w_hbm, ck_hbm, cv_hbm,
    part_out, q_rows, q_own, normed_out, cos_out, sin_out,
    len_s, x_v, w_v, ck_v, cv_v, xs, q16, sem_l, sem_x, sem_w, sem_k, sem_v,
):
    heads = width // DH
    rows = reqs * steps
    seq = lax.axis_index("seq")
    copy_l = pltpu.make_async_copy(len_hbm, len_s, sem_l)
    copy_l.start()
    copy_x = pltpu.make_async_copy(x_hbm, x_v, sem_x)
    copy_x.start()
    copy_w = pltpu.make_async_copy(w_hbm.at[0], w_v, sem_w)
    copy_w.start()
    count = reqs // group
    copies = []
    for g in range(count):
        span = pl.ds(g * group, group)
        copies.append((
            pltpu.make_async_copy(ck_hbm.at[span], ck_v.at[span], sem_k.at[g]),
            pltpu.make_async_copy(cv_hbm.at[span], cv_v.at[span], sem_v.at[g]),
        ))
        copies[g][0].start()
        copies[g][1].start()

    copy_l.wait()
    freq = frequencies()
    step_of = (lax.broadcasted_iota(jnp.int32, (8, DH), 0) % steps).astype(F32)
    lane8 = lax.broadcasted_iota(jnp.int32, (8, DH), 1)
    upper = lax.broadcasted_iota(jnp.int32, (8, DH), 0) >= steps
    for r in range(0, reqs, 2):
        place = jnp.where(upper, len_s[r + 1], len_s[r]).astype(F32) + step_of
        angles = place * freq
        cos_out[r * steps : (r + 2) * steps, :] = jnp.cos(angles)
        sine = jnp.sin(angles)
        sin_out[r * steps : (r + 2) * steps, :] = jnp.where(lane8 < DH // 2, -sine, sine)

    copy_x.wait()
    for r in range(reqs):
        xs[pl.ds(r * steps, steps), :] = x_v[r].astype(F32)
    normed_out[...] = norm_rows(xs[...]).astype(BF16)

    copy_w.wait()
    part = jnp.dot(normed_out[...], w_v[...], preferred_element_type=F32)
    for h in range(heads):
        q = turn(part[:, h * DH : (h + 1) * DH], cos_out[...], sin_out[...]).astype(BF16)
        q_rows[:, h * DH : (h + 1) * DH] = q
        q16[pl.ds(h, rows, stride=heads), :] = q.astype(F32)

    tall = steps * heads
    half = tall // 2
    q_own[...] = q16[pl.ds(seq * half, half), :]
    lane = lax.broadcasted_iota(jnp.int32, (tall, DH), 1)
    many_head = lax.broadcasted_iota(jnp.int32, (group * tall, DH), 0) % heads
    many_lane = lax.broadcasted_iota(jnp.int32, (group * tall, DH), 1)
    for g in range(count):
        q = q16[g * group * tall : (g + 1) * group * tall, :]
        spread = jnp.concatenate([jnp.where(many_head == h, q, 0.0).astype(BF16) for h in range(heads)], axis=1)
        copies[g][0].wait()
        scores = []
        for i in range(group):
            r = g * group + i
            score = lax.dot_general(
                spread[i * tall : (i + 1) * tall], ck_v[r], (((1,), (1,)), ((), ())), preferred_element_type=F32
            )
            scores.append(jnp.where(lane < len_s[r] - seq * block, score * SCALE, NEG))
        scores = jnp.concatenate(scores, axis=0)
        highest = jnp.max(scores, axis=-1, keepdims=True)
        weights = jnp.where(scores == NEG, 0.0, jnp.exp(scores - highest))
        total = jnp.sum(weights, axis=-1, keepdims=True)
        weights = weights.astype(BF16)
        copies[g][1].wait()
        pieces = split3(jnp.broadcast_to(highest, scores.shape)) + split3(jnp.broadcast_to(total, scores.shape))
        stats = pieces[5]
        for i in range(4, -1, -1):
            stats = jnp.where(many_lane == i, pieces[i], stats)
        stats = stats.astype(BF16)
        for i in range(group):
            r = g * group + i
            wide = jnp.dot(weights[i * tall : (i + 1) * tall], cv_v[r], preferred_element_type=F32)
            o = wide[:, 0:DH]
            for h in range(1, heads):
                o = jnp.where(many_head[0:tall] == h, wide[:, h * DH : (h + 1) * DH], o)
            for j in range(2):
                part_out[2 * r + j, 0:half, :] = o[j * half : (j + 1) * half].astype(BF16)
                part_out[2 * r + j, half : 2 * half, :] = stats[i * tall + j * half : i * tall + (j + 1) * half]


def fresh_kernel(
    reqs, steps, width,
    w_hbm, proj_hbm, q_rows, q_own, normed, cosine, sine,
    q_out, k_out, v_out, fresh_out, proj_out,
    w_v, k16, v16, sem_w, sem_p,
):
    heads = width // DH
    rows = reqs * steps
    tall = steps * heads
    half = tall // 2
    seq = lax.axis_index("seq")
    copies = [pltpu.make_async_copy(w_hbm.at[1 + j], w_v.at[j], sem_w.at[j]) for j in range(2)]
    for c in copies:
        c.start()
    copy_p = pltpu.make_async_copy(proj_hbm, proj_out, sem_p)
    copy_p.start()

    def emit(store, out):
        for h in range(heads):
            v = store[pl.ds(h, rows, stride=heads), :]
            out[:, :, h * DH : (h + 1) * DH] = v.reshape(reqs, steps, DH).astype(BF16)

    q_out[...] = q_rows[...].reshape(q_out.shape)
    for j, store, out in ((0, k16, k_out), (1, v16, v_out)):
        copies[j].wait()
        part = jnp.dot(normed[...], w_v[j], preferred_element_type=F32)
        for h in range(heads):
            v = part[:, h * DH : (h + 1) * DH]
            v = turn(v, cosine[...], sine[...]) if j == 0 else v
            store[pl.ds(h, rows, stride=heads), :] = rounded(v)
        emit(store, out)

    q = q_own[...]
    step = (seq % 2) * 2 + lax.broadcasted_iota(jnp.int32, (half, 1), 0) // heads
    base = (seq // 2) * tall
    scores = []
    values = []
    for s in range(steps):
        key = k16[pl.ds(base + s * heads, heads), :]
        value = v16[pl.ds(base + s * heads, heads), :]
        key = jnp.concatenate([key, key], axis=0)
        values.append(jnp.concatenate([value, value], axis=0))
        scores.append(jnp.sum(q * key, axis=-1, keepdims=True) * SCALE)
    highest = scores[0]
    for s in range(1, steps):
        highest = jnp.maximum(highest, jnp.where(s <= step, scores[s], NEG))
    total = jnp.zeros_like(highest)
    o = jnp.zeros((half, DH), F32)
    for s in range(steps):
        weight = jnp.where(s <= step, jnp.exp(scores[s] - highest), 0.0)
        total = total + weight
        o = o + rounded(weight) * values[s]
    fresh_out[0] = o
    fresh_out[1] = jnp.broadcast_to(highest, o.shape)
    fresh_out[2] = jnp.broadcast_to(total, o.shape)
    copy_p.wait()


def merge_kernel(got_ref, fresh_ref, w_ref, out_ref, ctx_s):
    half = fresh_ref.shape[1]
    heads = half // 2
    stats = got_ref[:, half : 2 * half, :].astype(F32)
    highest = (stats[:, :, 0:1] + stats[:, :, 1:2]) + stats[:, :, 2:3]
    total = (stats[:, :, 3:4] + stats[:, :, 4:5]) + stats[:, :, 5:6]
    fresh_high = fresh_ref[1][:, 0:1]
    top = jnp.maximum(jnp.max(highest, axis=0), fresh_high)
    factor = jnp.exp(highest - top[None])
    fresh_factor = jnp.exp(fresh_high - top)
    whole = jnp.sum(factor * total, axis=0) + fresh_factor * fresh_ref[2][:, 0:1]
    o = jnp.sum(factor * got_ref[:, 0:half, :].astype(F32), axis=0) + fresh_factor * fresh_ref[0]
    ctx_s[...] = o / whole
    ctx = jnp.concatenate([ctx_s[pl.ds(h, 2, stride=heads), :] for h in range(heads)], axis=1)
    out_ref[...] = jnp.dot(ctx.astype(BF16), w_ref[...], preferred_element_type=F32)


def mlp_kernel(
    x_hbm, gu_hbm, wd_hbm, a_ref, b_ref, c_ref, d_ref,
    o0, o1, o2, o3,
    x_v, gu_v, wd_v, mid_s, down_s, sem_x, sem_g, sem_d,
):
    seq = lax.axis_index("seq")
    me = lax.axis_index("mp")
    parts = down_s.shape[0]
    cols = down_s.shape[2]
    model = gu_v.shape[1]
    inner = wd_v.shape[0]
    pieces = sem_g.shape[1]
    copy_x = pltpu.make_async_copy(x_hbm.at[seq // 2], x_v, sem_x)
    copy_x.start()
    copies_g = []
    for p in range(pieces):
        span = pl.ds(p * (model // pieces), model // pieces)
        for j in range(2):
            copies_g.append(pltpu.make_async_copy(gu_hbm.at[j, span], gu_v.at[j, span], sem_g.at[j, p]))
            copies_g[-1].start()
    copies_d = []
    for p in range(pieces):
        span = pl.ds(p * (inner // pieces), inner // pieces)
        copies_d.append(pltpu.make_async_copy(wd_hbm.at[span], wd_v.at[span], sem_d.at[p]))
        copies_d[-1].start()
    others = (a_ref[...] + b_ref[...]) + (c_ref[...] + d_ref[...])
    copy_x.wait()
    x = x_v[...].astype(F32)
    middle = jnp.where(seq % 2 == 0, x[0:2], x[2:4]) + others
    normed = norm_rows(middle).astype(BF16)
    gate_up = [None, None]
    for p in range(pieces):
        lo, hi = p * (model // pieces), (p + 1) * (model // pieces)
        for j in range(2):
            copies_g[2 * p + j].wait()
            term = jnp.dot(normed[:, lo:hi], gu_v[j, lo:hi, :], preferred_element_type=F32)
            gate_up[j] = term if p == 0 else gate_up[j] + term
    gate, up = gate_up
    active = ((gate / (1.0 + jnp.exp(-gate))) * up).astype(BF16)
    down = None
    for p in range(pieces):
        lo, hi = p * (inner // pieces), (p + 1) * (inner // pieces)
        copies_d[p].wait()
        term = jnp.dot(active[:, lo:hi], wd_v[lo:hi, :], preferred_element_type=F32)
        down = term if p == 0 else down + term
    for p in range(parts):
        mid_s[p] = middle[:, p * cols : (p + 1) * cols]
        down_s[p] = down[:, p * cols : (p + 1) * cols]
    o0[...] = down_s[me] + mid_s[me]
    o1[...] = down_s[me ^ 1]
    o2[...] = down_s[me ^ 2]
    o3[...] = down_s[me ^ 3]


def to_others(values, axis):
    size = lax.axis_size(axis)
    return [
        lax.ppermute(v, axis, [(i, i ^ k) for i in range(size)]) for k, v in zip(range(1, size), values)
    ]


def per_device(inputs, w_qkv, w_out, w_gate_up, w_down, cache_keys, cache_values, lengths):
    reqs, steps, model = inputs.shape
    block = cache_keys.shape[1]
    width = cache_keys.shape[2]
    heads = width // DH
    rows = reqs * steps
    tall = steps * heads
    n_seq = lax.axis_size("seq")
    n_mp = lax.axis_size("mp")
    assert rows == 2 * n_seq and steps == 4 and n_mp == 4 and tall == 16
    group = min(8, reqs)
    in_hbm = functools.partial(pltpu.with_memory_space_constraint, memory_space=pltpu.HBM)
    any_space = pl.BlockSpec(memory_space=pltpu.HBM)
    vmem = pl.BlockSpec(memory_space=pltpu.VMEM)
    w_qkv_hbm = in_hbm(w_qkv)
    part, q_rows, q_own, normed, cosine, sine = pl.pallas_call(
        functools.partial(cached_kernel, group, reqs, steps, block, width),
        out_shape=(
            jax.ShapeDtypeStruct((n_seq, tall, DH), BF16),
            jax.ShapeDtypeStruct((rows, width), BF16),
            jax.ShapeDtypeStruct((tall // 2, DH), F32),
            jax.ShapeDtypeStruct((rows, model), BF16),
            jax.ShapeDtypeStruct((rows, DH), F32),
            jax.ShapeDtypeStruct((rows, DH), F32),
        ),
        in_specs=[any_space] * 5,
        out_specs=(vmem,) * 6,
        scratch_shapes=[
            pltpu.SMEM((reqs,), jnp.int32),
            pltpu.VMEM(inputs.shape, BF16),
            pltpu.VMEM((model, width), BF16),
            pltpu.VMEM(cache_keys.shape, BF16),
            pltpu.VMEM(cache_values.shape, BF16),
            pltpu.VMEM((rows, model), F32),
            pltpu.VMEM((rows * heads, DH), F32),
            pltpu.SemaphoreType.DMA,
            pltpu.SemaphoreType.DMA,
            pltpu.SemaphoreType.DMA,
            pltpu.SemaphoreType.DMA((reqs // group,)),
            pltpu.SemaphoreType.DMA((reqs // group,)),
        ],
        compiler_params=pltpu.CompilerParams(vmem_limit_bytes=48 << 20),
        name="cached_attention",
    )(in_hbm(lengths), in_hbm(inputs), w_qkv_hbm, in_hbm(cache_keys), in_hbm(cache_values))

    piece = jax.ShapeDtypeStruct((reqs, steps, width), BF16)
    queries, new_keys, new_values, fresh, w_proj = pl.pallas_call(
        functools.partial(fresh_kernel, reqs, steps, width),
        out_shape=(
            piece, piece, piece,
            jax.ShapeDtypeStruct((3, tall // 2, DH), F32),
            jax.ShapeDtypeStruct(w_out.shape, BF16),
        ),
        in_specs=[any_space] * 2 + [vmem] * 5,
        out_specs=(vmem,) * 5,
        scratch_shapes=[
            pltpu.VMEM((2, model, width), BF16),
            pltpu.VMEM((rows * heads, DH), F32),
            pltpu.VMEM((rows * heads, DH), F32),
            pltpu.SemaphoreType.DMA((2,)),
            pltpu.SemaphoreType.DMA,
        ],
        compiler_params=pltpu.CompilerParams(vmem_limit_bytes=16 << 20),
        name="new_tokens",
    )(w_qkv_hbm, in_hbm(w_out), q_rows, q_own, normed, cosine, sine)

    got = lax.all_to_all(part, "seq", 0, 0)

    mine = pl.pallas_call(
        merge_kernel,
        out_shape=jax.ShapeDtypeStruct((2, model), F32),
        in_specs=[vmem, vmem, vmem],
        out_specs=vmem,
        scratch_shapes=[pltpu.VMEM((tall // 2, DH), F32)],
        compiler_params=pltpu.CompilerParams(vmem_limit_bytes=8 << 20),
        name="merge_project",
    )(got, fresh, w_proj)
    others = to_others([mine] * 3, "mp")

    cols = model // n_mp
    chunk = jax.ShapeDtypeStruct((2, cols), F32)
    own, *rest = pl.pallas_call(
        mlp_kernel,
        out_shape=(chunk,) * 4,
        in_specs=[any_space] * 3 + [vmem] * 4,
        out_specs=(vmem,) * 4,
        scratch_shapes=[
            pltpu.VMEM((steps, model), BF16),
            pltpu.VMEM(w_gate_up.shape, BF16),
            pltpu.VMEM(w_down.shape, BF16),
            pltpu.VMEM((n_mp, 2, cols), F32),
            pltpu.VMEM((n_mp, 2, cols), F32),
            pltpu.SemaphoreType.DMA,
            pltpu.SemaphoreType.DMA((2, 4)),
            pltpu.SemaphoreType.DMA((4,)),
        ],
        compiler_params=pltpu.CompilerParams(vmem_limit_bytes=20 << 20),
        name="mlp",
    )(in_hbm(inputs), in_hbm(w_gate_up), in_hbm(w_down), mine, *others)
    back = to_others(rest, "mp")
    hidden = ((own + back[0]) + (back[1] + back[2])).astype(BF16)
    hidden = lax.all_to_all(jnp.broadcast_to(hidden[None], (n_seq, 2, cols)), "seq", 0, 0)
    return (hidden.reshape(reqs, steps, cols), queries, new_keys, new_values)


def solution(mesh):
    placed = (
        P(),
        P(None, None, "mp"),
        P("mp", None),
        P(None, None, "mp"),
        P("mp", None),
        P(None, "seq", "mp"),
        P(None, "seq", "mp"),
        P(),
    )
    return jax.shard_map(
        per_device,
        mesh=mesh,
        in_specs=placed,
        out_specs=(P(None, None, "mp"),) * 4,
        check_vma=False,
    )
```

```python
import functools

import jax
import jax.numpy as jnp
import numpy as np
from jax import lax
from jax.experimental import pallas as pl
from jax.experimental.pallas import tpu as pltpu
from jax.sharding import PartitionSpec as P

DH = 128
NEG = -1e30
EPS = 1e-05
SCALE = DH ** (-0.5)
F32 = jnp.float32
BF16 = jnp.bfloat16
FIRST = 2
LIMIT = 48


def norm_rows(x):
    centred = x - jnp.mean(x, axis=-1, keepdims=True)
    variance = jnp.mean(centred * centred, axis=-1, keepdims=True)
    return centred * lax.rsqrt(variance + EPS)


def split3(v):
    a = v.astype(BF16).astype(F32)
    rest = v - a
    b = rest.astype(BF16).astype(F32)
    return a, b, rest - b


def frequencies():
    half = DH // 2
    values = np.float32(10000.0) ** (np.float32(-2.0) * np.arange(half, dtype=np.float32) / np.float32(DH))
    lane = lax.broadcasted_iota(jnp.int32, (8, DH), 1) % half
    freq = jnp.full((8, DH), float(values[0]), F32)
    for i in range(1, half):
        freq = jnp.where(lane == i, float(values[i]), freq)
    return freq


def turn(v, cosine, sine):
    return v * cosine + pltpu.roll(v, DH // 2, 1) * sine


def rounded(v):
    return v.astype(BF16).astype(F32)


def cached_kernel(
    group, reqs, steps, block, width,
    len_hbm, x_hbm, w_hbm, ck_hbm, cv_hbm,
    part_out, q_rows, q_own, normed_out, cos_out, sin_out,
    len_s, x_v, w_v, ck_v, cv_v, xs, q16, sem_l, sem_x, sem_w, sem_k, sem_v,
):
    heads = width // DH
    rows = reqs * steps
    seq = lax.axis_index("seq")
    copy_l = pltpu.make_async_copy(len_hbm, len_s, sem_l)
    copy_l.start()
    copy_x = pltpu.make_async_copy(x_hbm, x_v, sem_x)
    copy_x.start()
    copy_w = pltpu.make_async_copy(w_hbm.at[0], w_v, sem_w)
    copy_w.start()
    count = reqs // group
    copies = []
    for g in range(count):
        span = pl.ds(g * group, group)
        copies.append(pltpu.make_async_copy(ck_hbm.at[span], ck_v.at[span], sem_k.at[g]))
        copies.append(pltpu.make_async_copy(cv_hbm.at[span], cv_v.at[span], sem_v.at[g]))
    for c in copies[:FIRST]:
        c.start()
    waiting = copies[FIRST:]

    def fetch(number):
        for _ in range(min(number, len(waiting))):
            waiting.pop(0).start()

    copy_l.wait()
    freq = frequencies()
    step_of = (lax.broadcasted_iota(jnp.int32, (8, DH), 0) % steps).astype(F32)
    lane8 = lax.broadcasted_iota(jnp.int32, (8, DH), 1)
    upper = lax.broadcasted_iota(jnp.int32, (8, DH), 0) >= steps
    for r in range(0, reqs, 2):
        place = jnp.where(upper, len_s[r + 1], len_s[r]).astype(F32) + step_of
        angles = place * freq
        cos_out[r * steps : (r + 2) * steps, :] = jnp.cos(angles)
        sine = jnp.sin(angles)
        sin_out[r * steps : (r + 2) * steps, :] = jnp.where(lane8 < DH // 2, -sine, sine)

    copy_x.wait()
    fetch(1)
    for r in range(reqs):
        xs[pl.ds(r * steps, steps), :] = x_v[r].astype(F32)
    normed_out[...] = norm_rows(xs[...]).astype(BF16)

    copy_w.wait()
    fetch(2)
    part = jnp.dot(normed_out[...], w_v[...], preferred_element_type=F32)
    for h in range(heads):
        q = turn(part[:, h * DH : (h + 1) * DH], cos_out[...], sin_out[...]).astype(BF16)
        q_rows[:, h * DH : (h + 1) * DH] = q
        q16[pl.ds(h, rows, stride=heads), :] = q.astype(F32)

    tall = steps * heads
    half = tall // 2
    q_own[...] = q16[pl.ds(seq * half, half), :]
    lane = lax.broadcasted_iota(jnp.int32, (tall, DH), 1)
    many_head = lax.broadcasted_iota(jnp.int32, (group * tall, DH), 0) % heads
    many_lane = lax.broadcasted_iota(jnp.int32, (group * tall, DH), 1)
    for g in range(count):
        q = q16[g * group * tall : (g + 1) * group * tall, :]
        spread = jnp.concatenate([jnp.where(many_head == h, q, 0.0).astype(BF16) for h in range(heads)], axis=1)
        copies[2 * g].wait()
        fetch(1)
        scores = []
        for i in range(group):
            r = g * group + i
            score = lax.dot_general(
                spread[i * tall : (i + 1) * tall], ck_v[r], (((1,), (1,)), ((), ())), preferred_element_type=F32
            )
            scores.append(jnp.where(lane < len_s[r] - seq * block, score * SCALE, NEG))
        scores = jnp.concatenate(scores, axis=0)
        highest = jnp.max(scores, axis=-1, keepdims=True)
        weights = jnp.where(scores == NEG, 0.0, jnp.exp(scores - highest))
        total = jnp.sum(weights, axis=-1, keepdims=True)
        weights = weights.astype(BF16)
        copies[2 * g + 1].wait()
        fetch(1)
        pieces = split3(jnp.broadcast_to(highest, scores.shape)) + split3(jnp.broadcast_to(total, scores.shape))
        stats = pieces[5]
        for i in range(4, -1, -1):
            stats = jnp.where(many_lane == i, pieces[i], stats)
        stats = stats.astype(BF16)
        for i in range(group):
            r = g * group + i
            wide = jnp.dot(weights[i * tall : (i + 1) * tall], cv_v[r], preferred_element_type=F32)
            o = wide[:, 0:DH]
            for h in range(1, heads):
                o = jnp.where(many_head[0:tall] == h, wide[:, h * DH : (h + 1) * DH], o)
            for j in range(2):
                part_out[2 * r + j, 0:half, :] = o[j * half : (j + 1) * half].astype(BF16)
                part_out[2 * r + j, half : 2 * half, :] = stats[i * tall + j * half : i * tall + (j + 1) * half]


def merge_kernel(
    steps,
    got_ref, q_own, normed, cosine, sine, w_qkv, w_ref,
    out_ref,
    k16, v16, ctx_s,
):
    half = q_own.shape[0]
    heads = half // 2
    tall = 2 * half
    seq = lax.axis_index("seq")

    block = pl.multiple_of((seq // 4) * 8, 8)
    rows = normed[pl.ds(block, 8), :]
    keys = jnp.dot(rows, w_qkv[1], preferred_element_type=F32)
    values = jnp.dot(rows, w_qkv[2], preferred_element_type=F32)
    turns = (cosine[pl.ds(block, 8), :], sine[pl.ds(block, 8), :])
    for h in range(heads):
        span = slice(h * DH, (h + 1) * DH)
        k16[pl.ds(h, 8, stride=heads), :] = rounded(turn(keys[:, span], *turns))
        v16[pl.ds(h, 8, stride=heads), :] = rounded(values[:, span])
    q = q_own[...]
    step = (seq % 2) * 2 + lax.broadcasted_iota(jnp.int32, (half, 1), 0) // heads
    base = pl.multiple_of(((seq // 2) % 2) * tall, tall)
    scores = []
    values = []
    for s in range(steps):
        key = k16[pl.ds(base + s * heads, heads), :]
        value = v16[pl.ds(base + s * heads, heads), :]
        key = jnp.concatenate([key, key], axis=0)
        values.append(jnp.concatenate([value, value], axis=0))
        scores.append(jnp.sum(q * key, axis=-1, keepdims=True) * SCALE)
    fresh_high = scores[0]
    for s in range(1, steps):
        fresh_high = jnp.maximum(fresh_high, jnp.where(s <= step, scores[s], NEG))
    fresh_total = jnp.zeros_like(fresh_high)
    fresh = jnp.zeros((half, DH), F32)
    for s in range(steps):
        weight = jnp.where(s <= step, jnp.exp(scores[s] - fresh_high), 0.0)
        fresh_total = fresh_total + weight
        fresh = fresh + rounded(weight) * values[s]

    stats = got_ref[:, half : 2 * half, :].astype(F32)
    highest = (stats[:, :, 0:1] + stats[:, :, 1:2]) + stats[:, :, 2:3]
    total = (stats[:, :, 3:4] + stats[:, :, 4:5]) + stats[:, :, 5:6]
    top = jnp.maximum(jnp.max(highest, axis=0), fresh_high)
    factor = jnp.exp(highest - top[None])
    fresh_factor = jnp.exp(fresh_high - top)
    whole = jnp.sum(factor * total, axis=0) + fresh_factor * fresh_total
    o = jnp.sum(factor * got_ref[:, 0:half, :].astype(F32), axis=0) + fresh_factor * fresh
    ctx_s[...] = o / whole
    ctx = jnp.concatenate([ctx_s[pl.ds(h, 2, stride=heads), :] for h in range(heads)], axis=1)
    out_ref[...] = jnp.dot(ctx.astype(BF16), w_ref[...], preferred_element_type=F32)


def outputs_kernel(
    after_hbm, w_hbm, q_rows, normed, cosine, sine,
    q_out, k_out, v_out,
    w_v, sem_w,
):
    reqs, steps, width = q_out.shape
    copies = [pltpu.make_async_copy(w_hbm.at[1 + j], w_v.at[j], sem_w.at[j]) for j in range(2)]
    for c in copies:
        c.start()
    q_out[...] = q_rows[...].reshape(q_out.shape)
    for j, out in enumerate((k_out, v_out)):
        copies[j].wait()
        part = jnp.dot(normed[...], w_v[j], preferred_element_type=F32)
        for h in range(width // DH):
            v = part[:, h * DH : (h + 1) * DH]
            v = turn(v, cosine[...], sine[...]) if j == 0 else v
            out[:, :, h * DH : (h + 1) * DH] = v.reshape(reqs, steps, DH).astype(BF16)


def mlp_kernel(x_ref, gu_ref, wd_ref, a_ref, b_ref, c_ref, d_ref, o0, o1, o2, o3, mid_s, down_s):
    seq = lax.axis_index("seq")
    me = lax.axis_index("mp")
    parts = down_s.shape[0]
    cols = down_s.shape[2]
    x = x_ref[seq // 2].astype(F32)
    x = jnp.where(seq % 2 == 0, x[0:2], x[2:4])
    middle = x + ((a_ref[...] + b_ref[...]) + (c_ref[...] + d_ref[...]))
    normed = norm_rows(middle).astype(BF16)
    gate = jnp.dot(normed, gu_ref[0], preferred_element_type=F32)
    up = jnp.dot(normed, gu_ref[1], preferred_element_type=F32)
    active = ((gate / (1.0 + jnp.exp(-gate))) * up).astype(BF16)
    down = jnp.dot(active, wd_ref[...], preferred_element_type=F32)
    for p in range(parts):
        mid_s[p] = middle[:, p * cols : (p + 1) * cols]
        down_s[p] = down[:, p * cols : (p + 1) * cols]
    o0[...] = down_s[me] + mid_s[me]
    o1[...] = down_s[me ^ 1]
    o2[...] = down_s[me ^ 2]
    o3[...] = down_s[me ^ 3]


def to_others(values, axis):
    size = lax.axis_size(axis)
    got = [None] * (size - 1)
    for k in range(size - 1, 0, -1):
        got[k - 1] = lax.ppermute(values[k - 1], axis, [(i, i ^ k) for i in range(size)])
    return got


def per_device(inputs, w_qkv, w_out, w_gate_up, w_down, cache_keys, cache_values, lengths):
    reqs, steps, model = inputs.shape
    block = cache_keys.shape[1]
    width = cache_keys.shape[2]
    heads = width // DH
    rows = reqs * steps
    tall = steps * heads
    n_seq = lax.axis_size("seq")
    n_mp = lax.axis_size("mp")
    assert rows == 2 * n_seq and steps == 4 and n_mp == 4 and tall == 16
    group = min(16, reqs)
    in_hbm = functools.partial(pltpu.with_memory_space_constraint, memory_space=pltpu.HBM)
    any_space = pl.BlockSpec(memory_space=pltpu.HBM)
    vmem = pl.BlockSpec(memory_space=pltpu.VMEM)
    part, q_rows, q_own, normed, cosine, sine = pl.pallas_call(
        functools.partial(cached_kernel, group, reqs, steps, block, width),
        out_shape=(
            jax.ShapeDtypeStruct((n_seq, tall, DH), BF16),
            jax.ShapeDtypeStruct((rows, width), BF16),
            jax.ShapeDtypeStruct((tall // 2, DH), F32),
            jax.ShapeDtypeStruct((rows, model), BF16),
            jax.ShapeDtypeStruct((rows, DH), F32),
            jax.ShapeDtypeStruct((rows, DH), F32),
        ),
        in_specs=[any_space] * 5,
        out_specs=(vmem,) * 6,
        scratch_shapes=[
            pltpu.SMEM((reqs,), jnp.int32),
            pltpu.VMEM(inputs.shape, BF16),
            pltpu.VMEM((model, width), BF16),
            pltpu.VMEM(cache_keys.shape, BF16),
            pltpu.VMEM(cache_values.shape, BF16),
            pltpu.VMEM((rows, model), F32),
            pltpu.VMEM((rows * heads, DH), F32),
            pltpu.SemaphoreType.DMA,
            pltpu.SemaphoreType.DMA,
            pltpu.SemaphoreType.DMA,
            pltpu.SemaphoreType.DMA((reqs // group,)),
            pltpu.SemaphoreType.DMA((reqs // group,)),
        ],
        compiler_params=pltpu.CompilerParams(vmem_limit_bytes=LIMIT << 20),
        name="cached_attention",
    )(in_hbm(lengths), in_hbm(inputs), in_hbm(w_qkv), in_hbm(cache_keys), in_hbm(cache_values))

    got = lax.all_to_all(part, "seq", 0, 0)

    mine = pl.pallas_call(
        functools.partial(merge_kernel, steps),
        out_shape=jax.ShapeDtypeStruct((2, model), F32),
        in_specs=[vmem] * 7,
        out_specs=vmem,
        scratch_shapes=[
            pltpu.VMEM((8 * heads, DH), F32),
            pltpu.VMEM((8 * heads, DH), F32),
            pltpu.VMEM((tall // 2, DH), F32),
        ],
        compiler_params=pltpu.CompilerParams(vmem_limit_bytes=8 << 20),
        name="merge_project",
    )(got, q_own, normed, cosine, sine, w_qkv, w_out)
    others = to_others([mine] * 3, "mp")

    piece = jax.ShapeDtypeStruct((reqs, steps, width), BF16)
    queries, new_keys, new_values = pl.pallas_call(
        outputs_kernel,
        out_shape=(piece,) * 3,
        in_specs=[any_space] * 2 + [vmem] * 4,
        out_specs=(vmem,) * 3,
        scratch_shapes=[pltpu.VMEM((2, model, width), BF16), pltpu.SemaphoreType.DMA((2,))],
        compiler_params=pltpu.CompilerParams(vmem_limit_bytes=12 << 20),
        name="projections",
    )(mine, in_hbm(w_qkv), q_rows, normed, cosine, sine)

    cols = model // n_mp
    chunk = jax.ShapeDtypeStruct((2, cols), F32)
    own, *rest = pl.pallas_call(
        mlp_kernel,
        out_shape=(chunk,) * 4,
        in_specs=[vmem] * 7,
        out_specs=(vmem,) * 4,
        scratch_shapes=[pltpu.VMEM((n_mp, 2, cols), F32)] * 2,
        compiler_params=pltpu.CompilerParams(vmem_limit_bytes=8 << 20),
        name="mlp",
    )(inputs, w_gate_up, w_down, mine, *others)
    back = to_others(rest, "mp")
    hidden = ((own + back[0]) + (back[1] + back[2])).astype(BF16)
    hidden = lax.all_to_all(jnp.broadcast_to(hidden[None], (n_seq, 2, cols)), "seq", 0, 0)
    return (hidden.reshape(reqs, steps, cols), queries, new_keys, new_values)


def solution(mesh):
    placed = (
        P(),
        P(None, None, "mp"),
        P("mp", None),
        P(None, None, "mp"),
        P("mp", None),
        P(None, "seq", "mp"),
        P(None, "seq", "mp"),
        P(),
    )
    return jax.shard_map(
        per_device,
        mesh=mesh,
        in_specs=placed,
        out_specs=(P(None, None, "mp"),) * 4,
        check_vma=False,
    )
```

```python
import functools

import jax
import jax.numpy as jnp
import numpy as np
from jax import lax
from jax.experimental import pallas as pl
from jax.experimental.pallas import tpu as pltpu
from jax.sharding import PartitionSpec as P

DH = 128
NEG = -1e30
EPS = 1e-05
SCALE = DH ** (-0.5)
F32 = jnp.float32
BF16 = jnp.bfloat16
FIRST = 2
LIMIT = 48


def norm_rows(x):
    centred = x - jnp.mean(x, axis=-1, keepdims=True)
    variance = jnp.mean(centred * centred, axis=-1, keepdims=True)
    return centred * lax.rsqrt(variance + EPS)


def split3(v):
    a = v.astype(BF16).astype(F32)
    rest = v - a
    b = rest.astype(BF16).astype(F32)
    return a, b, rest - b


def frequencies():
    half = DH // 2
    values = np.float32(10000.0) ** (np.float32(-2.0) * np.arange(half, dtype=np.float32) / np.float32(DH))
    lane = lax.broadcasted_iota(jnp.int32, (8, DH), 1) % half
    freq = jnp.full((8, DH), float(values[0]), F32)
    for i in range(1, half):
        freq = jnp.where(lane == i, float(values[i]), freq)
    return freq


def turn(v, cosine, sine):
    return v * cosine + pltpu.roll(v, DH // 2, 1) * sine


def rounded(v):
    return v.astype(BF16).astype(F32)


def cached_kernel(
    group, reqs, steps, block, width,
    len_hbm, x_hbm, w_hbm, ck_hbm, cv_hbm,
    part_out, q_rows, q_own, normed_out, cos_out, sin_out,
    len_s, x_v, w_v, ck_v, cv_v, xs, q16, sem_l, sem_x, sem_w, sem_k, sem_v,
):
    heads = width // DH
    rows = reqs * steps
    seq = lax.axis_index("seq")
    copy_l = pltpu.make_async_copy(len_hbm, len_s, sem_l)
    copy_l.start()
    copy_x = pltpu.make_async_copy(x_hbm, x_v, sem_x)
    copy_x.start()
    copy_w = pltpu.make_async_copy(w_hbm.at[0], w_v, sem_w)
    copy_w.start()
    count = reqs // group
    copies = []
    for g in range(count):
        span = pl.ds(g * group, group)
        copies.append(pltpu.make_async_copy(ck_hbm.at[span], ck_v.at[span], sem_k.at[g]))
        copies.append(pltpu.make_async_copy(cv_hbm.at[span], cv_v.at[span], sem_v.at[g]))
    for c in copies[:FIRST]:
        c.start()
    waiting = copies[FIRST:]

    def fetch(number):
        for _ in range(min(number, len(waiting))):
            waiting.pop(0).start()

    copy_l.wait()
    freq = frequencies()
    step_of = (lax.broadcasted_iota(jnp.int32, (8, DH), 0) % steps).astype(F32)
    lane8 = lax.broadcasted_iota(jnp.int32, (8, DH), 1)
    upper = lax.broadcasted_iota(jnp.int32, (8, DH), 0) >= steps
    for r in range(0, reqs, 2):
        place = jnp.where(upper, len_s[r + 1], len_s[r]).astype(F32) + step_of
        angles = place * freq
        cos_out[r * steps : (r + 2) * steps, :] = jnp.cos(angles)
        sine = jnp.sin(angles)
        sin_out[r * steps : (r + 2) * steps, :] = jnp.where(lane8 < DH // 2, -sine, sine)

    copy_x.wait()
    fetch(1)
    for r in range(reqs):
        xs[pl.ds(r * steps, steps), :] = x_v[r].astype(F32)
    normed_out[...] = norm_rows(xs[...]).astype(BF16)

    copy_w.wait()
    fetch(2)
    part = jnp.dot(normed_out[...], w_v[...], preferred_element_type=F32)
    for h in range(heads):
        q = turn(part[:, h * DH : (h + 1) * DH], cos_out[...], sin_out[...]).astype(BF16)
        q_rows[:, h * DH : (h + 1) * DH] = q
        q16[pl.ds(h, rows, stride=heads), :] = q.astype(F32)

    tall = steps * heads
    half = tall // 2
    q_own[...] = q16[pl.ds(seq * half, half), :]
    lane = lax.broadcasted_iota(jnp.int32, (tall, DH), 1)
    many_head = lax.broadcasted_iota(jnp.int32, (group * tall, DH), 0) % heads
    many_lane = lax.broadcasted_iota(jnp.int32, (group * tall, DH), 1)
    for g in range(count):
        q = q16[g * group * tall : (g + 1) * group * tall, :]
        spread = jnp.concatenate([jnp.where(many_head == h, q, 0.0).astype(BF16) for h in range(heads)], axis=1)
        copies[2 * g].wait()
        fetch(1)
        scores = []
        for i in range(group):
            r = g * group + i
            score = lax.dot_general(
                spread[i * tall : (i + 1) * tall], ck_v[r], (((1,), (1,)), ((), ())), preferred_element_type=F32
            )
            scores.append(jnp.where(lane < len_s[r] - seq * block, score * SCALE, NEG))
        scores = jnp.concatenate(scores, axis=0)
        highest = jnp.max(scores, axis=-1, keepdims=True)
        weights = jnp.where(scores == NEG, 0.0, jnp.exp(scores - highest))
        total = jnp.sum(weights, axis=-1, keepdims=True)
        weights = weights.astype(BF16)
        copies[2 * g + 1].wait()
        fetch(1)
        pieces = split3(jnp.broadcast_to(highest, scores.shape)) + split3(jnp.broadcast_to(total, scores.shape))
        stats = pieces[5]
        for i in range(4, -1, -1):
            stats = jnp.where(many_lane == i, pieces[i], stats)
        stats = stats.astype(BF16)
        for i in range(group):
            r = g * group + i
            wide = jnp.dot(weights[i * tall : (i + 1) * tall], cv_v[r], preferred_element_type=F32)
            o = wide[:, 0:DH]
            for h in range(1, heads):
                o = jnp.where(many_head[0:tall] == h, wide[:, h * DH : (h + 1) * DH], o)
            for j in range(2):
                part_out[2 * r + j, 0:half, :] = o[j * half : (j + 1) * half].astype(BF16)
                part_out[2 * r + j, half : 2 * half, :] = stats[i * tall + j * half : i * tall + (j + 1) * half]


def merge_kernel(
    steps,
    got_ref, q_own, normed, cosine, sine, w_qkv, w_ref,
    out_ref,
    k16, v16, ctx_s,
):
    half = q_own.shape[0]
    heads = half // 2
    tall = 2 * half
    seq = lax.axis_index("seq")

    block = pl.multiple_of((seq // 4) * 8, 8)
    rows = normed[pl.ds(block, 8), :]
    keys = jnp.dot(rows, w_qkv[1], preferred_element_type=F32)
    values = jnp.dot(rows, w_qkv[2], preferred_element_type=F32)
    turns = (cosine[pl.ds(block, 8), :], sine[pl.ds(block, 8), :])
    for h in range(heads):
        span = slice(h * DH, (h + 1) * DH)
        k16[pl.ds(h, 8, stride=heads), :] = rounded(turn(keys[:, span], *turns))
        v16[pl.ds(h, 8, stride=heads), :] = rounded(values[:, span])
    q = q_own[...]
    step = (seq % 2) * 2 + lax.broadcasted_iota(jnp.int32, (half, 1), 0) // heads
    base = pl.multiple_of(((seq // 2) % 2) * tall, tall)
    scores = []
    values = []
    for s in range(steps):
        key = k16[pl.ds(base + s * heads, heads), :]
        value = v16[pl.ds(base + s * heads, heads), :]
        key = jnp.concatenate([key, key], axis=0)
        values.append(jnp.concatenate([value, value], axis=0))
        scores.append(jnp.sum(q * key, axis=-1, keepdims=True) * SCALE)
    fresh_high = scores[0]
    for s in range(1, steps):
        fresh_high = jnp.maximum(fresh_high, jnp.where(s <= step, scores[s], NEG))
    fresh_total = jnp.zeros_like(fresh_high)
    fresh = jnp.zeros((half, DH), F32)
    for s in range(steps):
        weight = jnp.where(s <= step, jnp.exp(scores[s] - fresh_high), 0.0)
        fresh_total = fresh_total + weight
        fresh = fresh + rounded(weight) * values[s]

    stats = got_ref[:, half : 2 * half, :].astype(F32)
    highest = (stats[:, :, 0:1] + stats[:, :, 1:2]) + stats[:, :, 2:3]
    total = (stats[:, :, 3:4] + stats[:, :, 4:5]) + stats[:, :, 5:6]
    top = jnp.maximum(jnp.max(highest, axis=0), fresh_high)
    factor = jnp.exp(highest - top[None])
    fresh_factor = jnp.exp(fresh_high - top)
    whole = jnp.sum(factor * total, axis=0) + fresh_factor * fresh_total
    o = jnp.sum(factor * got_ref[:, 0:half, :].astype(F32), axis=0) + fresh_factor * fresh
    ctx_s[...] = o / whole
    ctx = jnp.concatenate([ctx_s[pl.ds(h, 2, stride=heads), :] for h in range(heads)], axis=1)
    out_ref[...] = jnp.dot(ctx.astype(BF16), w_ref[...], preferred_element_type=F32)


def outputs_kernel(
    after_hbm, w_hbm, q_rows, normed, cosine, sine,
    q_out, k_out, v_out,
    w_v, sem_w,
):
    reqs, steps, width = q_out.shape
    copies = [pltpu.make_async_copy(w_hbm.at[1 + j], w_v.at[j], sem_w.at[j]) for j in range(2)]
    for c in copies:
        c.start()
    q_out[...] = q_rows[...].reshape(q_out.shape)
    for j, out in enumerate((k_out, v_out)):
        copies[j].wait()
        part = jnp.dot(normed[...], w_v[j], preferred_element_type=F32)
        for h in range(width // DH):
            v = part[:, h * DH : (h + 1) * DH]
            v = turn(v, cosine[...], sine[...]) if j == 0 else v
            out[:, :, h * DH : (h + 1) * DH] = v.reshape(reqs, steps, DH).astype(BF16)


def mlp_kernel(x_ref, gu_ref, wd_ref, a_ref, b_ref, c_ref, d_ref, middle_out, down_out):
    seq = lax.axis_index("seq")
    x = x_ref[seq // 2].astype(F32)
    x = jnp.where(seq % 2 == 0, x[0:2], x[2:4])
    middle = x + ((a_ref[...] + b_ref[...]) + (c_ref[...] + d_ref[...]))
    middle_out[...] = middle
    normed = norm_rows(middle).astype(BF16)
    gate = jnp.dot(normed, gu_ref[0], preferred_element_type=F32)
    up = jnp.dot(normed, gu_ref[1], preferred_element_type=F32)
    active = ((gate / (1.0 + jnp.exp(-gate))) * up).astype(BF16)
    down_out[...] = jnp.dot(active, wd_ref[...], preferred_element_type=F32)


def last_kernel(middle_ref, a_ref, b_ref, c_ref, d_ref, out_ref):
    cols = out_ref.shape[2]
    span = pl.ds(pl.multiple_of(lax.axis_index("mp") * cols, cols), cols)
    down = (a_ref[:, span] + b_ref[:, span]) + (c_ref[:, span] + d_ref[:, span])
    hidden = (middle_ref[:, span] + down).astype(BF16)
    out_ref[...] = jnp.broadcast_to(hidden[None], out_ref.shape)


def to_others(values, axis):
    size = lax.axis_size(axis)
    got = [None] * (size - 1)
    for k in range(size - 1, 0, -1):
        got[k - 1] = lax.ppermute(values[k - 1], axis, [(i, i ^ k) for i in range(size)])
    return got


def per_device(inputs, w_qkv, w_out, w_gate_up, w_down, cache_keys, cache_values, lengths):
    reqs, steps, model = inputs.shape
    block = cache_keys.shape[1]
    width = cache_keys.shape[2]
    heads = width // DH
    rows = reqs * steps
    tall = steps * heads
    n_seq = lax.axis_size("seq")
    n_mp = lax.axis_size("mp")
    assert rows == 2 * n_seq and steps == 4 and n_mp == 4 and tall == 16
    group = min(16, reqs)
    in_hbm = functools.partial(pltpu.with_memory_space_constraint, memory_space=pltpu.HBM)
    any_space = pl.BlockSpec(memory_space=pltpu.HBM)
    vmem = pl.BlockSpec(memory_space=pltpu.VMEM)
    part, q_rows, q_own, normed, cosine, sine = pl.pallas_call(
        functools.partial(cached_kernel, group, reqs, steps, block, width),
        out_shape=(
            jax.ShapeDtypeStruct((n_seq, tall, DH), BF16),
            jax.ShapeDtypeStruct((rows, width), BF16),
            jax.ShapeDtypeStruct((tall // 2, DH), F32),
            jax.ShapeDtypeStruct((rows, model), BF16),
            jax.ShapeDtypeStruct((rows, DH), F32),
            jax.ShapeDtypeStruct((rows, DH), F32),
        ),
        in_specs=[any_space] * 5,
        out_specs=(vmem,) * 6,
        scratch_shapes=[
            pltpu.SMEM((reqs,), jnp.int32),
            pltpu.VMEM(inputs.shape, BF16),
            pltpu.VMEM((model, width), BF16),
            pltpu.VMEM(cache_keys.shape, BF16),
            pltpu.VMEM(cache_values.shape, BF16),
            pltpu.VMEM((rows, model), F32),
            pltpu.VMEM((rows * heads, DH), F32),
            pltpu.SemaphoreType.DMA,
            pltpu.SemaphoreType.DMA,
            pltpu.SemaphoreType.DMA,
            pltpu.SemaphoreType.DMA((reqs // group,)),
            pltpu.SemaphoreType.DMA((reqs // group,)),
        ],
        compiler_params=pltpu.CompilerParams(vmem_limit_bytes=LIMIT << 20),
        name="cached_attention",
    )(in_hbm(lengths), in_hbm(inputs), in_hbm(w_qkv), in_hbm(cache_keys), in_hbm(cache_values))

    got = lax.all_to_all(part, "seq", 0, 0)

    mine = pl.pallas_call(
        functools.partial(merge_kernel, steps),
        out_shape=jax.ShapeDtypeStruct((2, model), F32),
        in_specs=[vmem] * 7,
        out_specs=vmem,
        scratch_shapes=[
            pltpu.VMEM((8 * heads, DH), F32),
            pltpu.VMEM((8 * heads, DH), F32),
            pltpu.VMEM((tall // 2, DH), F32),
        ],
        compiler_params=pltpu.CompilerParams(vmem_limit_bytes=8 << 20),
        name="merge_project",
    )(got, q_own, normed, cosine, sine, w_qkv, w_out)
    others = to_others([mine] * 3, "mp")

    piece = jax.ShapeDtypeStruct((reqs, steps, width), BF16)
    queries, new_keys, new_values = pl.pallas_call(
        outputs_kernel,
        out_shape=(piece,) * 3,
        in_specs=[any_space] * 2 + [vmem] * 4,
        out_specs=(vmem,) * 3,
        scratch_shapes=[pltpu.VMEM((2, model, width), BF16), pltpu.SemaphoreType.DMA((2,))],
        compiler_params=pltpu.CompilerParams(vmem_limit_bytes=12 << 20),
        name="projections",
    )(mine, in_hbm(w_qkv), q_rows, normed, cosine, sine)

    cols = model // n_mp
    rows2 = jax.ShapeDtypeStruct((2, model), F32)
    middle, down = pl.pallas_call(
        mlp_kernel,
        out_shape=(rows2,) * 2,
        in_specs=[vmem] * 7,
        out_specs=(vmem,) * 2,
        compiler_params=pltpu.CompilerParams(vmem_limit_bytes=8 << 20),
        name="mlp",
    )(inputs, w_gate_up, w_down, mine, *others)
    hidden = pl.pallas_call(
        last_kernel,
        out_shape=jax.ShapeDtypeStruct((n_seq, 2, cols), BF16),
        in_specs=[vmem] * 5,
        out_specs=vmem,
        compiler_params=pltpu.CompilerParams(vmem_limit_bytes=4 << 20),
        name="last_sum",
    )(middle, down, *to_others([down] * 3, "mp"))
    hidden = lax.all_to_all(hidden, "seq", 0, 0)
    return (hidden.reshape(reqs, steps, cols), queries, new_keys, new_values)


def solution(mesh):
    placed = (
        P(),
        P(None, None, "mp"),
        P("mp", None),
        P(None, None, "mp"),
        P("mp", None),
        P(None, "seq", "mp"),
        P(None, "seq", "mp"),
        P(),
    )
    return jax.shard_map(
        per_device,
        mesh=mesh,
        in_specs=placed,
        out_specs=(P(None, None, "mp"),) * 4,
        check_vma=False,
    )
```

```python
import functools

import jax
import jax.numpy as jnp
import numpy as np
from jax import lax
from jax.experimental import pallas as pl
from jax.experimental.pallas import tpu as pltpu
from jax.sharding import PartitionSpec as P

DH = 128
NEG = -1e30
EPS = 1e-05
SCALE = DH ** (-0.5)
F32 = jnp.float32
BF16 = jnp.bfloat16


def norm_rows(x):
    centred = x - jnp.mean(x, axis=-1, keepdims=True)
    variance = jnp.mean(centred * centred, axis=-1, keepdims=True)
    return centred * lax.rsqrt(variance + EPS)


def split3(v):
    a = v.astype(BF16).astype(F32)
    rest = v - a
    b = rest.astype(BF16).astype(F32)
    return a, b, rest - b


def frequencies():
    half = DH // 2
    values = np.float32(10000.0) ** (np.float32(-2.0) * np.arange(half, dtype=np.float32) / np.float32(DH))
    lane = lax.broadcasted_iota(jnp.int32, (8, DH), 1) % half
    freq = jnp.full((8, DH), float(values[0]), F32)
    for i in range(1, half):
        freq = jnp.where(lane == i, float(values[i]), freq)
    return freq


def turn(v, cosine, sine):
    return v * cosine + pltpu.roll(v, DH // 2, 1) * sine


def rounded(v):
    return v.astype(BF16).astype(F32)


def cached_kernel(
    group, reqs, steps, block, width,
    len_hbm, x_hbm, w_hbm, ck_hbm, cv_hbm,
    part_out, q_rows, q_own, normed_out, cos_out, sin_out,
    len_s, order_s, x_v, w_v, ck_v, cv_v, xs, q16, sem_l, sem_x, sem_w, sem_k, sem_v,
):
    heads = width // DH
    rows = reqs * steps
    tall = steps * heads
    half = tall // 2
    seq = lax.axis_index("seq")
    first = seq * block
    copy_l = pltpu.make_async_copy(len_hbm, len_s, sem_l)
    copy_l.start()
    copy_x = pltpu.make_async_copy(x_hbm, x_v, sem_x)
    copy_x.start()
    copy_w = pltpu.make_async_copy(w_hbm.at[0], w_v, sem_w)
    copy_w.start()

    copy_l.wait()
    count = jnp.int32(0)
    for r in range(reqs):
        live = len_s[r] > first
        order_s[jnp.where(live, count, reqs - 1 - r + count)] = r
        count = count + live.astype(jnp.int32)

    def copies(cache, held, sems, lo):
        return [
            pltpu.make_async_copy(cache.at[order_s[i]], held.at[i], sems.at[i]) for i in range(lo, lo + group)
        ]

    def fetch(*args):
        for c in copies(*args):
            c.start()

    def arrive(*args):
        for c in copies(*args):
            c.wait()

    fetch(ck_hbm, ck_v, sem_k, 0)

    freq = frequencies()
    step_of = (lax.broadcasted_iota(jnp.int32, (8, DH), 0) % steps).astype(F32)
    lane8 = lax.broadcasted_iota(jnp.int32, (8, DH), 1)
    upper = lax.broadcasted_iota(jnp.int32, (8, DH), 0) >= steps
    for r in range(0, reqs, 2):
        place = jnp.where(upper, len_s[r + 1], len_s[r]).astype(F32) + step_of
        angles = place * freq
        cos_out[r * steps : (r + 2) * steps, :] = jnp.cos(angles)
        sine = jnp.sin(angles)
        sin_out[r * steps : (r + 2) * steps, :] = jnp.where(lane8 < DH // 2, -sine, sine)

    lane = lax.broadcasted_iota(jnp.int32, (tall, DH), 1)
    empty = jnp.where(lane[0:half] == 0, NEG, 0.0).astype(BF16)
    for p in range(2 * reqs):
        part_out[p, 0:half, :] = jnp.zeros((half, DH), BF16)
        part_out[p, half : 2 * half, :] = empty

    copy_x.wait()
    fetch(cv_hbm, cv_v, sem_v, 0)
    for r in range(reqs):
        xs[pl.ds(r * steps, steps), :] = x_v[r].astype(F32)
    normed_out[...] = norm_rows(xs[...]).astype(BF16)

    copy_w.wait()
    part = jnp.dot(normed_out[...], w_v[...], preferred_element_type=F32)
    for h in range(heads):
        q = turn(part[:, h * DH : (h + 1) * DH], cos_out[...], sin_out[...]).astype(BF16)
        q_rows[:, h * DH : (h + 1) * DH] = q
        q16[pl.ds(h, rows, stride=heads), :] = q.astype(F32)
    q_own[...] = q16[pl.ds(seq * half, half), :]

    row_head = lax.broadcasted_iota(jnp.int32, (tall, DH), 0) % heads
    many_lane = lax.broadcasted_iota(jnp.int32, (group * tall, DH), 1)

    def attend(lo):
        arrive(ck_hbm, ck_v, sem_k, lo)
        scores = []
        for i in range(lo, lo + group):
            r = order_s[i]
            q = q16[pl.ds(pl.multiple_of(r * tall, tall), tall), :]
            spread = jnp.concatenate([jnp.where(row_head == h, q, 0.0).astype(BF16) for h in range(heads)], axis=1)
            score = lax.dot_general(spread, ck_v[i], (((1,), (1,)), ((), ())), preferred_element_type=F32)
            scores.append(jnp.where(lane < len_s[r] - first, score * SCALE, NEG))
        scores = jnp.concatenate(scores, axis=0)
        highest = jnp.max(scores, axis=-1, keepdims=True)
        weights = jnp.where(scores == NEG, 0.0, jnp.exp(scores - highest))
        total = jnp.sum(weights, axis=-1, keepdims=True)
        weights = weights.astype(BF16)
        pieces = split3(jnp.broadcast_to(highest, scores.shape)) + split3(jnp.broadcast_to(total, scores.shape))
        stats = pieces[5]
        for i in range(4, -1, -1):
            stats = jnp.where(many_lane == i, pieces[i], stats)
        stats = stats.astype(BF16)
        arrive(cv_hbm, cv_v, sem_v, lo)
        for i in range(lo, lo + group):
            r = order_s[i]
            at = (i - lo) * tall
            wide = jnp.dot(weights[at : at + tall], cv_v[i], preferred_element_type=F32)
            o = wide[:, 0:DH]
            for h in range(1, heads):
                o = jnp.where(row_head == h, wide[:, h * DH : (h + 1) * DH], o)
            for j in range(2):
                part_out[2 * r + j, 0:half, :] = o[j * half : (j + 1) * half].astype(BF16)
                part_out[2 * r + j, half : 2 * half, :] = stats[at + j * half : at + (j + 1) * half]

    attend(0)
    for lo in range(group, reqs, group):
        @pl.when(count > lo)
        def _():
            fetch(ck_hbm, ck_v, sem_k, lo)
            fetch(cv_hbm, cv_v, sem_v, lo)
            attend(lo)


def merge_kernel(
    steps,
    got_ref, q_own, normed, cosine, sine, w_qkv, w_ref,
    out_ref,
    k16, v16, ctx_s,
):
    half = q_own.shape[0]
    heads = half // 2
    tall = 2 * half
    seq = lax.axis_index("seq")

    block = pl.multiple_of((seq // 4) * 8, 8)
    rows = normed[pl.ds(block, 8), :]
    keys = jnp.dot(rows, w_qkv[1], preferred_element_type=F32)
    values = jnp.dot(rows, w_qkv[2], preferred_element_type=F32)
    turns = (cosine[pl.ds(block, 8), :], sine[pl.ds(block, 8), :])
    for h in range(heads):
        span = slice(h * DH, (h + 1) * DH)
        k16[pl.ds(h, 8, stride=heads), :] = rounded(turn(keys[:, span], *turns))
        v16[pl.ds(h, 8, stride=heads), :] = rounded(values[:, span])
    q = q_own[...]
    step = (seq % 2) * 2 + lax.broadcasted_iota(jnp.int32, (half, 1), 0) // heads
    base = pl.multiple_of(((seq // 2) % 2) * tall, tall)
    scores = []
    values = []
    for s in range(steps):
        key = k16[pl.ds(base + s * heads, heads), :]
        value = v16[pl.ds(base + s * heads, heads), :]
        key = jnp.concatenate([key, key], axis=0)
        values.append(jnp.concatenate([value, value], axis=0))
        scores.append(jnp.sum(q * key, axis=-1, keepdims=True) * SCALE)
    fresh_high = scores[0]
    for s in range(1, steps):
        fresh_high = jnp.maximum(fresh_high, jnp.where(s <= step, scores[s], NEG))
    fresh_total = jnp.zeros_like(fresh_high)
    fresh = jnp.zeros((half, DH), F32)
    for s in range(steps):
        weight = jnp.where(s <= step, jnp.exp(scores[s] - fresh_high), 0.0)
        fresh_total = fresh_total + weight
        fresh = fresh + rounded(weight) * values[s]

    stats = got_ref[:, half : 2 * half, :].astype(F32)
    highest = (stats[:, :, 0:1] + stats[:, :, 1:2]) + stats[:, :, 2:3]
    total = (stats[:, :, 3:4] + stats[:, :, 4:5]) + stats[:, :, 5:6]
    top = jnp.maximum(jnp.max(highest, axis=0), fresh_high)
    factor = jnp.exp(highest - top[None])
    fresh_factor = jnp.exp(fresh_high - top)
    whole = jnp.sum(factor * total, axis=0) + fresh_factor * fresh_total
    o = jnp.sum(factor * got_ref[:, 0:half, :].astype(F32), axis=0) + fresh_factor * fresh
    ctx_s[...] = o / whole
    ctx = jnp.concatenate([ctx_s[pl.ds(h, 2, stride=heads), :] for h in range(heads)], axis=1)
    out_ref[...] = jnp.dot(ctx.astype(BF16), w_ref[...], preferred_element_type=F32)


def outputs_kernel(
    after_hbm, w_hbm, q_rows, normed, cosine, sine,
    q_out, k_out, v_out,
    w_v, sem_w,
):
    reqs, steps, width = q_out.shape
    copies = [pltpu.make_async_copy(w_hbm.at[1 + j], w_v.at[j], sem_w.at[j]) for j in range(2)]
    for c in copies:
        c.start()
    q_out[...] = q_rows[...].reshape(q_out.shape)
    for j, out in enumerate((k_out, v_out)):
        copies[j].wait()
        part = jnp.dot(normed[...], w_v[j], preferred_element_type=F32)
        for h in range(width // DH):
            v = part[:, h * DH : (h + 1) * DH]
            v = turn(v, cosine[...], sine[...]) if j == 0 else v
            out[:, :, h * DH : (h + 1) * DH] = v.reshape(reqs, steps, DH).astype(BF16)


def mlp_kernel(x_ref, gu_ref, wd_ref, a_ref, b_ref, c_ref, d_ref, middle_out, down_out):
    seq = lax.axis_index("seq")
    x = x_ref[seq // 2].astype(F32)
    x = jnp.where(seq % 2 == 0, x[0:2], x[2:4])
    middle = x + ((a_ref[...] + b_ref[...]) + (c_ref[...] + d_ref[...]))
    middle_out[...] = middle
    normed = norm_rows(middle).astype(BF16)
    gate = jnp.dot(normed, gu_ref[0], preferred_element_type=F32)
    up = jnp.dot(normed, gu_ref[1], preferred_element_type=F32)
    active = ((gate / (1.0 + jnp.exp(-gate))) * up).astype(BF16)
    down_out[...] = jnp.dot(active, wd_ref[...], preferred_element_type=F32)


def last_kernel(middle_ref, a_ref, b_ref, c_ref, d_ref, out_ref):
    cols = out_ref.shape[2]
    span = pl.ds(pl.multiple_of(lax.axis_index("mp") * cols, cols), cols)
    down = (a_ref[:, span] + b_ref[:, span]) + (c_ref[:, span] + d_ref[:, span])
    hidden = (middle_ref[:, span] + down).astype(BF16)
    out_ref[...] = jnp.broadcast_to(hidden[None], out_ref.shape)


def to_others(values, axis):
    size = lax.axis_size(axis)
    got = [None] * (size - 1)
    for k in range(size - 1, 0, -1):
        got[k - 1] = lax.ppermute(values[k - 1], axis, [(i, i ^ k) for i in range(size)])
    return got


def per_device(inputs, w_qkv, w_out, w_gate_up, w_down, cache_keys, cache_values, lengths):
    reqs, steps, model = inputs.shape
    block = cache_keys.shape[1]
    width = cache_keys.shape[2]
    heads = width // DH
    rows = reqs * steps
    tall = steps * heads
    n_seq = lax.axis_size("seq")
    n_mp = lax.axis_size("mp")
    assert rows == 2 * n_seq and steps == 4 and n_mp == 4 and tall == 16
    group = max(reqs // 2, 1)
    in_hbm = functools.partial(pltpu.with_memory_space_constraint, memory_space=pltpu.HBM)
    any_space = pl.BlockSpec(memory_space=pltpu.HBM)
    vmem = pl.BlockSpec(memory_space=pltpu.VMEM)
    part, q_rows, q_own, normed, cosine, sine = pl.pallas_call(
        functools.partial(cached_kernel, group, reqs, steps, block, width),
        out_shape=(
            jax.ShapeDtypeStruct((n_seq, tall, DH), BF16),
            jax.ShapeDtypeStruct((rows, width), BF16),
            jax.ShapeDtypeStruct((tall // 2, DH), F32),
            jax.ShapeDtypeStruct((rows, model), BF16),
            jax.ShapeDtypeStruct((rows, DH), F32),
            jax.ShapeDtypeStruct((rows, DH), F32),
        ),
        in_specs=[any_space] * 5,
        out_specs=(vmem,) * 6,
        scratch_shapes=[
            pltpu.SMEM((reqs,), jnp.int32),
            pltpu.SMEM((reqs,), jnp.int32),
            pltpu.VMEM(inputs.shape, BF16),
            pltpu.VMEM((model, width), BF16),
            pltpu.VMEM(cache_keys.shape, BF16),
            pltpu.VMEM(cache_values.shape, BF16),
            pltpu.VMEM((rows, model), F32),
            pltpu.VMEM((rows * heads, DH), F32),
            pltpu.SemaphoreType.DMA,
            pltpu.SemaphoreType.DMA,
            pltpu.SemaphoreType.DMA,
            pltpu.SemaphoreType.DMA((reqs,)),
            pltpu.SemaphoreType.DMA((reqs,)),
        ],
        compiler_params=pltpu.CompilerParams(vmem_limit_bytes=48 << 20),
        name="cached_attention",
    )(in_hbm(lengths), in_hbm(inputs), in_hbm(w_qkv), in_hbm(cache_keys), in_hbm(cache_values))

    got = lax.all_to_all(part, "seq", 0, 0)

    mine = pl.pallas_call(
        functools.partial(merge_kernel, steps),
        out_shape=jax.ShapeDtypeStruct((2, model), F32),
        in_specs=[vmem] * 7,
        out_specs=vmem,
        scratch_shapes=[
            pltpu.VMEM((8 * heads, DH), F32),
            pltpu.VMEM((8 * heads, DH), F32),
            pltpu.VMEM((tall // 2, DH), F32),
        ],
        compiler_params=pltpu.CompilerParams(vmem_limit_bytes=8 << 20),
        name="merge_project",
    )(got, q_own, normed, cosine, sine, w_qkv, w_out)
    others = to_others([mine] * 3, "mp")

    piece = jax.ShapeDtypeStruct((reqs, steps, width), BF16)
    queries, new_keys, new_values = pl.pallas_call(
        outputs_kernel,
        out_shape=(piece,) * 3,
        in_specs=[any_space] * 2 + [vmem] * 4,
        out_specs=(vmem,) * 3,
        scratch_shapes=[pltpu.VMEM((2, model, width), BF16), pltpu.SemaphoreType.DMA((2,))],
        compiler_params=pltpu.CompilerParams(vmem_limit_bytes=12 << 20),
        name="projections",
    )(mine, in_hbm(w_qkv), q_rows, normed, cosine, sine)

    cols = model // n_mp
    rows2 = jax.ShapeDtypeStruct((2, model), F32)
    middle, down = pl.pallas_call(
        mlp_kernel,
        out_shape=(rows2,) * 2,
        in_specs=[vmem] * 7,
        out_specs=(vmem,) * 2,
        compiler_params=pltpu.CompilerParams(vmem_limit_bytes=8 << 20),
        name="mlp",
    )(inputs, w_gate_up, w_down, mine, *others)
    hidden = pl.pallas_call(
        last_kernel,
        out_shape=jax.ShapeDtypeStruct((n_seq, 2, cols), BF16),
        in_specs=[vmem] * 5,
        out_specs=vmem,
        compiler_params=pltpu.CompilerParams(vmem_limit_bytes=4 << 20),
        name="last_sum",
    )(middle, down, *to_others([down] * 3, "mp"))
    hidden = lax.all_to_all(hidden, "seq", 0, 0)
    return (hidden.reshape(reqs, steps, cols), queries, new_keys, new_values)


def solution(mesh):
    placed = (
        P(),
        P(None, None, "mp"),
        P("mp", None),
        P(None, None, "mp"),
        P("mp", None),
        P(None, "seq", "mp"),
        P(None, "seq", "mp"),
        P(),
    )
    return jax.shard_map(
        per_device,
        mesh=mesh,
        in_specs=placed,
        out_specs=(P(None, None, "mp"),) * 4,
        check_vma=False,
    )
```

```python
import functools

import jax
import jax.numpy as jnp
import numpy as np
from jax import lax
from jax.experimental import pallas as pl
from jax.experimental.pallas import tpu as pltpu
from jax.sharding import PartitionSpec as P

DH = 128
NEG = -1e30
EPS = 1e-05
SCALE = DH ** (-0.5)
F32 = jnp.float32
BF16 = jnp.bfloat16


def norm_rows(x):
    centred = x - jnp.mean(x, axis=-1, keepdims=True)
    variance = jnp.mean(centred * centred, axis=-1, keepdims=True)
    return centred * lax.rsqrt(variance + EPS)


def split3(v):
    a = v.astype(BF16).astype(F32)
    rest = v - a
    b = rest.astype(BF16).astype(F32)
    return a, b, rest - b


def frequencies():
    half = DH // 2
    values = np.float32(10000.0) ** (np.float32(-2.0) * np.arange(half, dtype=np.float32) / np.float32(DH))
    lane = lax.broadcasted_iota(jnp.int32, (8, DH), 1) % half
    freq = jnp.full((8, DH), float(values[0]), F32)
    for i in range(1, half):
        freq = jnp.where(lane == i, float(values[i]), freq)
    return freq


def turn(v, cosine, sine):
    return v * cosine + pltpu.roll(v, DH // 2, 1) * sine


def rounded(v):
    return v.astype(BF16).astype(F32)


def cached_kernel(
    group, reqs, steps, block, width,
    len_hbm, x_hbm, w_hbm, ck_hbm, cv_hbm,
    part_out, q_rows, q_own, normed_out, cos_out, sin_out,
    len_s, order_s, x_v, w_v, ck_v, cv_v, xs, q16, sem_l, sem_x, sem_w, sem_k, sem_v,
):
    heads = width // DH
    rows = reqs * steps
    tall = steps * heads
    half = tall // 2
    seq = lax.axis_index("seq")
    first = seq * block
    copy_l = pltpu.make_async_copy(len_hbm, len_s, sem_l)
    copy_l.start()
    copy_x = pltpu.make_async_copy(x_hbm, x_v, sem_x)
    copy_x.start()
    copy_w = pltpu.make_async_copy(w_hbm.at[0], w_v, sem_w)
    copy_w.start()

    copy_l.wait()
    count = jnp.int32(0)
    for r in range(reqs):
        live = len_s[r] > first
        order_s[jnp.where(live, count, reqs - 1 - r + count)] = r
        count = count + live.astype(jnp.int32)

    def copies(cache, held, sems, lo):
        return [
            pltpu.make_async_copy(cache.at[order_s[i]], held.at[i], sems.at[i]) for i in range(lo, lo + group)
        ]

    def fetch(*args):
        for c in copies(*args):
            c.start()

    def arrive(*args):
        for c in copies(*args):
            c.wait()

    fetch(ck_hbm, ck_v, sem_k, 0)

    freq = frequencies()
    step_of = (lax.broadcasted_iota(jnp.int32, (8, DH), 0) % steps).astype(F32)
    lane8 = lax.broadcasted_iota(jnp.int32, (8, DH), 1)
    upper = lax.broadcasted_iota(jnp.int32, (8, DH), 0) >= steps
    for r in range(0, reqs, 2):
        place = jnp.where(upper, len_s[r + 1], len_s[r]).astype(F32) + step_of
        angles = place * freq
        cos_out[r * steps : (r + 2) * steps, :] = jnp.cos(angles)
        sine = jnp.sin(angles)
        sin_out[r * steps : (r + 2) * steps, :] = jnp.where(lane8 < DH // 2, -sine, sine)

    lane = lax.broadcasted_iota(jnp.int32, (tall, DH), 1)
    empty = jnp.where(lane[0:half] == 0, NEG, 0.0).astype(BF16)
    for p in range(2 * reqs):
        part_out[p, 0:half, :] = jnp.zeros((half, DH), BF16)
        part_out[p, half : 2 * half, :] = empty

    copy_x.wait()
    fetch(cv_hbm, cv_v, sem_v, 0)
    for r in range(reqs):
        xs[pl.ds(r * steps, steps), :] = x_v[r].astype(F32)
    normed_out[...] = norm_rows(xs[...]).astype(BF16)

    copy_w.wait()
    part = jnp.dot(normed_out[...], w_v[...], preferred_element_type=F32)
    for h in range(heads):
        q = turn(part[:, h * DH : (h + 1) * DH], cos_out[...], sin_out[...]).astype(BF16)
        q_rows[:, h * DH : (h + 1) * DH] = q
        q16[pl.ds(h, rows, stride=heads), :] = q.astype(F32)
    q_own[...] = q16[pl.ds(seq * half, half), :]

    row_head = lax.broadcasted_iota(jnp.int32, (tall, DH), 0) % heads
    many_lane = lax.broadcasted_iota(jnp.int32, (group * tall, DH), 1)

    def attend(lo):
        arrive(ck_hbm, ck_v, sem_k, lo)
        scores = []
        for i in range(lo, lo + group):
            r = order_s[i]
            q = q16[pl.ds(pl.multiple_of(r * tall, tall), tall), :]
            spread = jnp.concatenate([jnp.where(row_head == h, q, 0.0).astype(BF16) for h in range(heads)], axis=1)
            score = lax.dot_general(spread, ck_v[i], (((1,), (1,)), ((), ())), preferred_element_type=F32)
            scores.append(jnp.where(lane < len_s[r] - first, score * SCALE, NEG))
        scores = jnp.concatenate(scores, axis=0)
        highest = jnp.max(scores, axis=-1, keepdims=True)
        weights = jnp.where(scores == NEG, 0.0, jnp.exp(scores - highest))
        total = jnp.sum(weights, axis=-1, keepdims=True)
        weights = weights.astype(BF16)
        pieces = split3(jnp.broadcast_to(highest, scores.shape)) + split3(jnp.broadcast_to(total, scores.shape))
        stats = pieces[5]
        for i in range(4, -1, -1):
            stats = jnp.where(many_lane == i, pieces[i], stats)
        stats = stats.astype(BF16)
        arrive(cv_hbm, cv_v, sem_v, lo)
        for i in range(lo, lo + group):
            r = order_s[i]
            at = (i - lo) * tall
            wide = jnp.dot(weights[at : at + tall], cv_v[i], preferred_element_type=F32)
            o = wide[:, 0:DH]
            for h in range(1, heads):
                o = jnp.where(row_head == h, wide[:, h * DH : (h + 1) * DH], o)
            for j in range(2):
                part_out[2 * r + j, 0:half, :] = o[j * half : (j + 1) * half].astype(BF16)
                part_out[2 * r + j, half : 2 * half, :] = stats[at + j * half : at + (j + 1) * half]

    attend(0)
    for lo in range(group, reqs, group):
        @pl.when(count > lo)
        def _():
            fetch(ck_hbm, ck_v, sem_k, lo)
            fetch(cv_hbm, cv_v, sem_v, lo)
            attend(lo)


def fresh_kernel(
    steps,
    w_hbm, proj_hbm, q_own, normed, cosine, sine,
    fresh_out, proj_out,
    w_v, k16, v16, sem_w, sem_p,
):
    half = q_own.shape[0]
    heads = half // 2
    tall = 2 * half
    seq = lax.axis_index("seq")
    copies = [pltpu.make_async_copy(w_hbm.at[1 + j], w_v.at[j], sem_w.at[j]) for j in range(2)]
    for c in copies:
        c.start()
    copy_p = pltpu.make_async_copy(proj_hbm, proj_out, sem_p)
    copy_p.start()
    block = pl.multiple_of((seq // 4) * 8, 8)
    rows = normed[pl.ds(block, 8), :]
    turns = (cosine[pl.ds(block, 8), :], sine[pl.ds(block, 8), :])
    for j, store in enumerate((k16, v16)):
        copies[j].wait()
        part = jnp.dot(rows, w_v[j], preferred_element_type=F32)
        for h in range(heads):
            v = part[:, h * DH : (h + 1) * DH]
            store[pl.ds(h, 8, stride=heads), :] = rounded(turn(v, *turns) if j == 0 else v)
    q = q_own[...]
    step = (seq % 2) * 2 + lax.broadcasted_iota(jnp.int32, (half, 1), 0) // heads
    base = pl.multiple_of(((seq // 2) % 2) * tall, tall)
    scores = []
    values = []
    for s in range(steps):
        key = k16[pl.ds(base + s * heads, heads), :]
        value = v16[pl.ds(base + s * heads, heads), :]
        key = jnp.concatenate([key, key], axis=0)
        values.append(jnp.concatenate([value, value], axis=0))
        scores.append(jnp.sum(q * key, axis=-1, keepdims=True) * SCALE)
    high = scores[0]
    for s in range(1, steps):
        high = jnp.maximum(high, jnp.where(s <= step, scores[s], NEG))
    total = jnp.zeros_like(high)
    o = jnp.zeros((half, DH), F32)
    for s in range(steps):
        weight = jnp.where(s <= step, jnp.exp(scores[s] - high), 0.0)
        total = total + weight
        o = o + rounded(weight) * values[s]
    fresh_out[0] = o
    fresh_out[1] = jnp.broadcast_to(high, o.shape)
    fresh_out[2] = jnp.broadcast_to(total, o.shape)
    copy_p.wait()


def merge_kernel(got_ref, fresh_ref, w_ref, out_ref, ctx_s):
    half = fresh_ref.shape[1]
    heads = half // 2
    fresh_high = fresh_ref[1][:, 0:1]
    stats = got_ref[:, half : 2 * half, :].astype(F32)
    highest = (stats[:, :, 0:1] + stats[:, :, 1:2]) + stats[:, :, 2:3]
    total = (stats[:, :, 3:4] + stats[:, :, 4:5]) + stats[:, :, 5:6]
    top = jnp.maximum(jnp.max(highest, axis=0), fresh_high)
    factor = jnp.exp(highest - top[None])
    fresh_factor = jnp.exp(fresh_high - top)
    whole = jnp.sum(factor * total, axis=0) + fresh_factor * fresh_ref[2][:, 0:1]
    o = jnp.sum(factor * got_ref[:, 0:half, :].astype(F32), axis=0) + fresh_factor * fresh_ref[0]
    ctx_s[...] = o / whole
    ctx = jnp.concatenate([ctx_s[pl.ds(h, 2, stride=heads), :] for h in range(heads)], axis=1)
    out_ref[...] = jnp.dot(ctx.astype(BF16), w_ref[...], preferred_element_type=F32)


def outputs_kernel(
    after_hbm, w_hbm, q_rows, normed, cosine, sine,
    q_out, k_out, v_out,
    w_v, sem_w,
):
    reqs, steps, width = q_out.shape
    copies = [pltpu.make_async_copy(w_hbm.at[1 + j], w_v.at[j], sem_w.at[j]) for j in range(2)]
    for c in copies:
        c.start()
    q_out[...] = q_rows[...].reshape(q_out.shape)
    for j, out in enumerate((k_out, v_out)):
        copies[j].wait()
        part = jnp.dot(normed[...], w_v[j], preferred_element_type=F32)
        for h in range(width // DH):
            v = part[:, h * DH : (h + 1) * DH]
            v = turn(v, cosine[...], sine[...]) if j == 0 else v
            out[:, :, h * DH : (h + 1) * DH] = v.reshape(reqs, steps, DH).astype(BF16)


def mlp_kernel(x_ref, gu_ref, wd_ref, a_ref, b_ref, c_ref, d_ref, middle_out, down_out):
    seq = lax.axis_index("seq")
    x = x_ref[seq // 2].astype(F32)
    x = jnp.where(seq % 2 == 0, x[0:2], x[2:4])
    middle = x + ((a_ref[...] + b_ref[...]) + (c_ref[...] + d_ref[...]))
    middle_out[...] = middle
    normed = norm_rows(middle).astype(BF16)
    gate = jnp.dot(normed, gu_ref[0], preferred_element_type=F32)
    up = jnp.dot(normed, gu_ref[1], preferred_element_type=F32)
    active = ((gate / (1.0 + jnp.exp(-gate))) * up).astype(BF16)
    down_out[...] = jnp.dot(active, wd_ref[...], preferred_element_type=F32)


def last_kernel(middle_ref, a_ref, b_ref, c_ref, d_ref, out_ref):
    cols = out_ref.shape[2]
    span = pl.ds(pl.multiple_of(lax.axis_index("mp") * cols, cols), cols)
    down = (a_ref[:, span] + b_ref[:, span]) + (c_ref[:, span] + d_ref[:, span])
    hidden = (middle_ref[:, span] + down).astype(BF16)
    out_ref[...] = jnp.broadcast_to(hidden[None], out_ref.shape)


def to_others(values, axis):
    size = lax.axis_size(axis)
    got = [None] * (size - 1)
    for k in range(size - 1, 0, -1):
        got[k - 1] = lax.ppermute(values[k - 1], axis, [(i, i ^ k) for i in range(size)])
    return got


def per_device(inputs, w_qkv, w_out, w_gate_up, w_down, cache_keys, cache_values, lengths):
    reqs, steps, model = inputs.shape
    block = cache_keys.shape[1]
    width = cache_keys.shape[2]
    heads = width // DH
    rows = reqs * steps
    tall = steps * heads
    n_seq = lax.axis_size("seq")
    n_mp = lax.axis_size("mp")
    assert rows == 2 * n_seq and steps == 4 and n_mp == 4 and tall == 16
    group = max(reqs // 2, 1)
    in_hbm = functools.partial(pltpu.with_memory_space_constraint, memory_space=pltpu.HBM)
    any_space = pl.BlockSpec(memory_space=pltpu.HBM)
    vmem = pl.BlockSpec(memory_space=pltpu.VMEM)
    part, q_rows, q_own, normed, cosine, sine = pl.pallas_call(
        functools.partial(cached_kernel, group, reqs, steps, block, width),
        out_shape=(
            jax.ShapeDtypeStruct((n_seq, tall, DH), BF16),
            jax.ShapeDtypeStruct((rows, width), BF16),
            jax.ShapeDtypeStruct((tall // 2, DH), F32),
            jax.ShapeDtypeStruct((rows, model), BF16),
            jax.ShapeDtypeStruct((rows, DH), F32),
            jax.ShapeDtypeStruct((rows, DH), F32),
        ),
        in_specs=[any_space] * 5,
        out_specs=(vmem,) * 6,
        scratch_shapes=[
            pltpu.SMEM((reqs,), jnp.int32),
            pltpu.SMEM((reqs,), jnp.int32),
            pltpu.VMEM(inputs.shape, BF16),
            pltpu.VMEM((model, width), BF16),
            pltpu.VMEM(cache_keys.shape, BF16),
            pltpu.VMEM(cache_values.shape, BF16),
            pltpu.VMEM((rows, model), F32),
            pltpu.VMEM((rows * heads, DH), F32),
            pltpu.SemaphoreType.DMA,
            pltpu.SemaphoreType.DMA,
            pltpu.SemaphoreType.DMA,
            pltpu.SemaphoreType.DMA((reqs,)),
            pltpu.SemaphoreType.DMA((reqs,)),
        ],
        compiler_params=pltpu.CompilerParams(vmem_limit_bytes=48 << 20),
        name="cached_attention",
    )(in_hbm(lengths), in_hbm(inputs), in_hbm(w_qkv), in_hbm(cache_keys), in_hbm(cache_values))

    got = lax.all_to_all(part, "seq", 0, 0)

    fresh, w_proj = pl.pallas_call(
        functools.partial(fresh_kernel, steps),
        out_shape=(jax.ShapeDtypeStruct((3, tall // 2, DH), F32), jax.ShapeDtypeStruct(w_out.shape, BF16)),
        in_specs=[any_space] * 2 + [vmem] * 4,
        out_specs=(vmem,) * 2,
        scratch_shapes=[
            pltpu.VMEM((2, model, width), BF16),
            pltpu.VMEM((8 * heads, DH), F32),
            pltpu.VMEM((8 * heads, DH), F32),
            pltpu.SemaphoreType.DMA((2,)),
            pltpu.SemaphoreType.DMA,
        ],
        compiler_params=pltpu.CompilerParams(vmem_limit_bytes=12 << 20),
        name="new_tokens",
    )(in_hbm(w_qkv), in_hbm(w_out), q_own, normed, cosine, sine)
    mine = pl.pallas_call(
        merge_kernel,
        out_shape=jax.ShapeDtypeStruct((2, model), F32),
        in_specs=[vmem] * 3,
        out_specs=vmem,
        scratch_shapes=[pltpu.VMEM((tall // 2, DH), F32)],
        compiler_params=pltpu.CompilerParams(vmem_limit_bytes=4 << 20),
        cost_estimate=pl.CostEstimate(flops=10**10, transcendentals=0, bytes_accessed=60 << 20),
        name="merge_project",
    )(got, fresh, w_proj)
    others = to_others([mine] * 3, "mp")

    piece = jax.ShapeDtypeStruct((reqs, steps, width), BF16)
    queries, new_keys, new_values = pl.pallas_call(
        outputs_kernel,
        out_shape=(piece,) * 3,
        in_specs=[any_space] * 2 + [vmem] * 4,
        out_specs=(vmem,) * 3,
        scratch_shapes=[pltpu.VMEM((2, model, width), BF16), pltpu.SemaphoreType.DMA((2,))],
        compiler_params=pltpu.CompilerParams(vmem_limit_bytes=12 << 20),
        name="projections",
    )(mine, in_hbm(w_qkv), q_rows, normed, cosine, sine)

    cols = model // n_mp
    rows2 = jax.ShapeDtypeStruct((2, model), F32)
    middle, down = pl.pallas_call(
        mlp_kernel,
        out_shape=(rows2,) * 2,
        in_specs=[vmem] * 7,
        out_specs=(vmem,) * 2,
        compiler_params=pltpu.CompilerParams(vmem_limit_bytes=8 << 20),
        name="mlp",
    )(inputs, w_gate_up, w_down, mine, *others)
    hidden = pl.pallas_call(
        last_kernel,
        out_shape=jax.ShapeDtypeStruct((n_seq, 2, cols), BF16),
        in_specs=[vmem] * 5,
        out_specs=vmem,
        compiler_params=pltpu.CompilerParams(vmem_limit_bytes=4 << 20),
        name="last_sum",
    )(middle, down, *to_others([down] * 3, "mp"))
    hidden = lax.all_to_all(hidden, "seq", 0, 0)
    return (hidden.reshape(reqs, steps, cols), queries, new_keys, new_values)


def solution(mesh):
    placed = (
        P(),
        P(None, None, "mp"),
        P("mp", None),
        P(None, None, "mp"),
        P("mp", None),
        P(None, "seq", "mp"),
        P(None, "seq", "mp"),
        P(),
    )
    return jax.shard_map(
        per_device,
        mesh=mesh,
        in_specs=placed,
        out_specs=(P(None, None, "mp"),) * 4,
        check_vma=False,
    )
```

```python
import functools

import jax
import jax.numpy as jnp
import numpy as np
from jax import lax
from jax.experimental import pallas as pl
from jax.experimental.pallas import tpu as pltpu
from jax.sharding import PartitionSpec as P

DH = 128
NEG = -1e30
EPS = 1e-05
SCALE = DH ** (-0.5)
F32 = jnp.float32
BF16 = jnp.bfloat16


def norm_rows(x):
    centred = x - jnp.mean(x, axis=-1, keepdims=True)
    variance = jnp.mean(centred * centred, axis=-1, keepdims=True)
    return centred * lax.rsqrt(variance + EPS)


def split3(v):
    a = v.astype(BF16).astype(F32)
    rest = v - a
    b = rest.astype(BF16).astype(F32)
    return a, b, rest - b


def frequencies():
    half = DH // 2
    values = np.float32(10000.0) ** (np.float32(-2.0) * np.arange(half, dtype=np.float32) / np.float32(DH))
    lane = lax.broadcasted_iota(jnp.int32, (8, DH), 1) % half
    freq = jnp.full((8, DH), float(values[0]), F32)
    for i in range(1, half):
        freq = jnp.where(lane == i, float(values[i]), freq)
    return freq


def turn(v, cosine, sine):
    return v * cosine + pltpu.roll(v, DH // 2, 1) * sine


def rounded(v):
    return v.astype(BF16).astype(F32)


def cached_kernel(
    group, reqs, steps, block, width,
    len_hbm, x_hbm, w_hbm, ck_hbm, cv_hbm,
    part_out, q_rows, q_own, normed_out, cos_out, sin_out,
    len_s, order_s, x_v, w_v, ck_v, cv_v, xs, q16, sem_l, sem_x, sem_w, sem_k, sem_v,
):
    heads = width // DH
    rows = reqs * steps
    tall = steps * heads
    half = tall // 2
    seq = lax.axis_index("seq")
    first = seq * block
    copy_l = pltpu.make_async_copy(len_hbm, len_s, sem_l)
    copy_l.start()
    copy_x = pltpu.make_async_copy(x_hbm, x_v, sem_x)
    copy_x.start()
    copy_w = pltpu.make_async_copy(w_hbm.at[0], w_v, sem_w)
    copy_w.start()

    copy_l.wait()
    count = jnp.int32(0)
    for r in range(reqs):
        live = len_s[r] > first
        order_s[jnp.where(live, count, reqs - 1 - r + count)] = r
        count = count + live.astype(jnp.int32)

    def copies(cache, held, sems, lo):
        return [
            pltpu.make_async_copy(cache.at[order_s[i]], held.at[i], sems.at[i]) for i in range(lo, lo + group)
        ]

    def fetch(*args):
        for c in copies(*args):
            c.start()

    def arrive(*args):
        for c in copies(*args):
            c.wait()

    fetch(ck_hbm, ck_v, sem_k, 0)

    freq = frequencies()
    step_of = (lax.broadcasted_iota(jnp.int32, (8, DH), 0) % steps).astype(F32)
    lane8 = lax.broadcasted_iota(jnp.int32, (8, DH), 1)
    upper = lax.broadcasted_iota(jnp.int32, (8, DH), 0) >= steps
    for r in range(0, reqs, 2):
        place = jnp.where(upper, len_s[r + 1], len_s[r]).astype(F32) + step_of
        angles = place * freq
        cos_out[r * steps : (r + 2) * steps, :] = jnp.cos(angles)
        sine = jnp.sin(angles)
        sin_out[r * steps : (r + 2) * steps, :] = jnp.where(lane8 < DH // 2, -sine, sine)

    lane = lax.broadcasted_iota(jnp.int32, (tall, DH), 1)
    empty = jnp.where(lane[0:heads] % (DH // 2) == 0, NEG, 0.0).astype(BF16)
    for p in range(2 * reqs):
        part_out[p, 0] = jnp.zeros((heads, DH), BF16)
        part_out[p, 1] = jnp.zeros((heads, DH), BF16)
        part_out[p, 2] = empty

    copy_x.wait()
    fetch(cv_hbm, cv_v, sem_v, 0)
    for r in range(reqs):
        xs[pl.ds(r * steps, steps), :] = x_v[r].astype(F32)
    normed_out[...] = norm_rows(xs[...]).astype(BF16)

    copy_w.wait()
    part = jnp.dot(normed_out[...], w_v[...], preferred_element_type=F32)
    for h in range(heads):
        q = turn(part[:, h * DH : (h + 1) * DH], cos_out[...], sin_out[...]).astype(BF16)
        q_rows[:, h * DH : (h + 1) * DH] = q
        q16[pl.ds(h, rows, stride=heads), :] = q.astype(F32)
    q_own[...] = q16[pl.ds(seq * half, half), :]

    row_head = lax.broadcasted_iota(jnp.int32, (tall, DH), 0) % heads
    many_lane = lax.broadcasted_iota(jnp.int32, (group * tall, DH), 1)

    def attend(lo):
        arrive(ck_hbm, ck_v, sem_k, lo)
        scores = []
        for i in range(lo, lo + group):
            r = order_s[i]
            q = q16[pl.ds(pl.multiple_of(r * tall, tall), tall), :]
            spread = jnp.concatenate([jnp.where(row_head == h, q, 0.0).astype(BF16) for h in range(heads)], axis=1)
            score = lax.dot_general(spread, ck_v[i], (((1,), (1,)), ((), ())), preferred_element_type=F32)
            scores.append(jnp.where(lane < len_s[r] - first, score * SCALE, NEG))
        scores = jnp.concatenate(scores, axis=0)
        highest = jnp.max(scores, axis=-1, keepdims=True)
        weights = jnp.where(scores == NEG, 0.0, jnp.exp(scores - highest))
        total = jnp.sum(weights, axis=-1, keepdims=True)
        weights = weights.astype(BF16)
        pieces = split3(jnp.broadcast_to(highest, scores.shape)) + split3(jnp.broadcast_to(total, scores.shape))
        stats = pieces[5]
        for i in range(4, -1, -1):
            stats = jnp.where(many_lane % (DH // 2) == i, pieces[i], stats)
        arrive(cv_hbm, cv_v, sem_v, lo)
        for i in range(lo, lo + group):
            r = order_s[i]
            at = (i - lo) * tall
            wide = jnp.dot(weights[at : at + tall], cv_v[i], preferred_element_type=F32)
            o = wide[:, 0:DH]
            for h in range(1, heads):
                o = jnp.where(row_head == h, wide[:, h * DH : (h + 1) * DH], o)
            for j in range(2):
                lo_row = 2 * j * heads
                for k in range(2):
                    part_out[2 * r + j, k] = o[lo_row + k * heads : lo_row + (k + 1) * heads].astype(BF16)
                pair = [stats[at + lo_row + k * heads : at + lo_row + (k + 1) * heads] for k in range(2)]
                part_out[2 * r + j, 2] = jnp.where(lane[0:heads] < DH // 2, pair[0], pair[1]).astype(BF16)

    attend(0)
    for lo in range(group, reqs, group):
        @pl.when(count > lo)
        def _():
            fetch(ck_hbm, ck_v, sem_k, lo)
            fetch(cv_hbm, cv_v, sem_v, lo)
            attend(lo)


def fresh_kernel(
    steps,
    w_hbm, proj_hbm, q_own, normed, cosine, sine,
    fresh_out, proj_out,
    w_v, k16, v16, sem_w, sem_p,
):
    half = q_own.shape[0]
    heads = half // 2
    tall = 2 * half
    seq = lax.axis_index("seq")
    copies = [pltpu.make_async_copy(w_hbm.at[1 + j], w_v.at[j], sem_w.at[j]) for j in range(2)]
    for c in copies:
        c.start()
    copy_p = pltpu.make_async_copy(proj_hbm, proj_out, sem_p)
    copy_p.start()
    block = pl.multiple_of((seq // 4) * 8, 8)
    rows = normed[pl.ds(block, 8), :]
    turns = (cosine[pl.ds(block, 8), :], sine[pl.ds(block, 8), :])
    for j, store in enumerate((k16, v16)):
        copies[j].wait()
        part = jnp.dot(rows, w_v[j], preferred_element_type=F32)
        for h in range(heads):
            v = part[:, h * DH : (h + 1) * DH]
            store[pl.ds(h, 8, stride=heads), :] = rounded(turn(v, *turns) if j == 0 else v)
    q = q_own[...]
    step = (seq % 2) * 2 + lax.broadcasted_iota(jnp.int32, (half, 1), 0) // heads
    base = pl.multiple_of(((seq // 2) % 2) * tall, tall)
    scores = []
    values = []
    for s in range(steps):
        key = k16[pl.ds(base + s * heads, heads), :]
        value = v16[pl.ds(base + s * heads, heads), :]
        key = jnp.concatenate([key, key], axis=0)
        values.append(jnp.concatenate([value, value], axis=0))
        scores.append(jnp.sum(q * key, axis=-1, keepdims=True) * SCALE)
    high = scores[0]
    for s in range(1, steps):
        high = jnp.maximum(high, jnp.where(s <= step, scores[s], NEG))
    total = jnp.zeros_like(high)
    o = jnp.zeros((half, DH), F32)
    for s in range(steps):
        weight = jnp.where(s <= step, jnp.exp(scores[s] - high), 0.0)
        total = total + weight
        o = o + rounded(weight) * values[s]
    fresh_out[0] = o
    fresh_out[1] = jnp.broadcast_to(high, o.shape)
    fresh_out[2] = jnp.broadcast_to(total, o.shape)
    copy_p.wait()


def merge_kernel(got_ref, fresh_ref, w_ref, out_ref, ctx_s):
    heads = got_ref.shape[2]
    stats = got_ref[:, 2].astype(F32)
    for k in range(2):
        span = slice(k * heads, (k + 1) * heads)
        fresh, fresh_high, fresh_total = fresh_ref[0][span], fresh_ref[1][span, 0:1], fresh_ref[2][span, 0:1]
        at = [stats[:, :, k * DH // 2 + i : k * DH // 2 + i + 1] for i in range(6)]
        highest = (at[0] + at[1]) + at[2]
        total = (at[3] + at[4]) + at[5]
        top = jnp.maximum(jnp.max(highest, axis=0), fresh_high)
        factor = jnp.exp(highest - top[None])
        fresh_factor = jnp.exp(fresh_high - top)
        whole = jnp.sum(factor * total, axis=0) + fresh_factor * fresh_total
        o = jnp.sum(factor * got_ref[:, k].astype(F32), axis=0) + fresh_factor * fresh
        ctx_s[span, :] = o / whole
    ctx = jnp.concatenate([ctx_s[pl.ds(h, 2, stride=heads), :] for h in range(heads)], axis=1)
    out_ref[...] = jnp.dot(ctx.astype(BF16), w_ref[...], preferred_element_type=F32)


def outputs_kernel(
    after_hbm, w_hbm, q_rows, normed, cosine, sine,
    q_out, k_out, v_out,
    w_v, sem_w,
):
    reqs, steps, width = q_out.shape
    copies = [pltpu.make_async_copy(w_hbm.at[1 + j], w_v.at[j], sem_w.at[j]) for j in range(2)]
    for c in copies:
        c.start()
    q_out[...] = q_rows[...].reshape(q_out.shape)
    for j, out in enumerate((k_out, v_out)):
        copies[j].wait()
        part = jnp.dot(normed[...], w_v[j], preferred_element_type=F32)
        for h in range(width // DH):
            v = part[:, h * DH : (h + 1) * DH]
            v = turn(v, cosine[...], sine[...]) if j == 0 else v
            out[:, :, h * DH : (h + 1) * DH] = v.reshape(reqs, steps, DH).astype(BF16)


def mlp_kernel(x_ref, gu_ref, wd_ref, a_ref, b_ref, c_ref, d_ref, middle_out, down_out):
    seq = lax.axis_index("seq")
    x = x_ref[seq // 2].astype(F32)
    x = jnp.where(seq % 2 == 0, x[0:2], x[2:4])
    middle = x + ((a_ref[...] + b_ref[...]) + (c_ref[...] + d_ref[...]))
    middle_out[...] = middle
    normed = norm_rows(middle).astype(BF16)
    gate = jnp.dot(normed, gu_ref[0], preferred_element_type=F32)
    up = jnp.dot(normed, gu_ref[1], preferred_element_type=F32)
    active = ((gate / (1.0 + jnp.exp(-gate))) * up).astype(BF16)
    down_out[...] = jnp.dot(active, wd_ref[...], preferred_element_type=F32)


def last_kernel(middle_ref, a_ref, b_ref, c_ref, d_ref, out_ref):
    cols = out_ref.shape[2]
    span = pl.ds(pl.multiple_of(lax.axis_index("mp") * cols, cols), cols)
    down = (a_ref[:, span] + b_ref[:, span]) + (c_ref[:, span] + d_ref[:, span])
    hidden = (middle_ref[:, span] + down).astype(BF16)
    out_ref[...] = jnp.broadcast_to(hidden[None], out_ref.shape)


def to_others(values, axis):
    size = lax.axis_size(axis)
    got = [None] * (size - 1)
    for k in range(size - 1, 0, -1):
        got[k - 1] = lax.ppermute(values[k - 1], axis, [(i, i ^ k) for i in range(size)])
    return got


def per_device(inputs, w_qkv, w_out, w_gate_up, w_down, cache_keys, cache_values, lengths):
    reqs, steps, model = inputs.shape
    block = cache_keys.shape[1]
    width = cache_keys.shape[2]
    heads = width // DH
    rows = reqs * steps
    tall = steps * heads
    n_seq = lax.axis_size("seq")
    n_mp = lax.axis_size("mp")
    assert rows == 2 * n_seq and steps == 4 and n_mp == 4 and tall == 16
    group = max(reqs // 2, 1)
    in_hbm = functools.partial(pltpu.with_memory_space_constraint, memory_space=pltpu.HBM)
    any_space = pl.BlockSpec(memory_space=pltpu.HBM)
    vmem = pl.BlockSpec(memory_space=pltpu.VMEM)
    part, q_rows, q_own, normed, cosine, sine = pl.pallas_call(
        functools.partial(cached_kernel, group, reqs, steps, block, width),
        out_shape=(
            jax.ShapeDtypeStruct((n_seq, 3, heads, DH), BF16),
            jax.ShapeDtypeStruct((rows, width), BF16),
            jax.ShapeDtypeStruct((tall // 2, DH), F32),
            jax.ShapeDtypeStruct((rows, model), BF16),
            jax.ShapeDtypeStruct((rows, DH), F32),
            jax.ShapeDtypeStruct((rows, DH), F32),
        ),
        in_specs=[any_space] * 5,
        out_specs=(vmem,) * 6,
        scratch_shapes=[
            pltpu.SMEM((reqs,), jnp.int32),
            pltpu.SMEM((reqs,), jnp.int32),
            pltpu.VMEM(inputs.shape, BF16),
            pltpu.VMEM((model, width), BF16),
            pltpu.VMEM(cache_keys.shape, BF16),
            pltpu.VMEM(cache_values.shape, BF16),
            pltpu.VMEM((rows, model), F32),
            pltpu.VMEM((rows * heads, DH), F32),
            pltpu.SemaphoreType.DMA,
            pltpu.SemaphoreType.DMA,
            pltpu.SemaphoreType.DMA,
            pltpu.SemaphoreType.DMA((reqs,)),
            pltpu.SemaphoreType.DMA((reqs,)),
        ],
        compiler_params=pltpu.CompilerParams(vmem_limit_bytes=48 << 20),
        name="cached_attention",
    )(in_hbm(lengths), in_hbm(inputs), in_hbm(w_qkv), in_hbm(cache_keys), in_hbm(cache_values))

    got = lax.all_to_all(part, "seq", 0, 0)

    fresh, w_proj = pl.pallas_call(
        functools.partial(fresh_kernel, steps),
        out_shape=(jax.ShapeDtypeStruct((3, tall // 2, DH), F32), jax.ShapeDtypeStruct(w_out.shape, BF16)),
        in_specs=[any_space] * 2 + [vmem] * 4,
        out_specs=(vmem,) * 2,
        scratch_shapes=[
            pltpu.VMEM((2, model, width), BF16),
            pltpu.VMEM((8 * heads, DH), F32),
            pltpu.VMEM((8 * heads, DH), F32),
            pltpu.SemaphoreType.DMA((2,)),
            pltpu.SemaphoreType.DMA,
        ],
        compiler_params=pltpu.CompilerParams(vmem_limit_bytes=12 << 20),
        name="new_tokens",
    )(in_hbm(w_qkv), in_hbm(w_out), q_own, normed, cosine, sine)
    mine = pl.pallas_call(
        merge_kernel,
        out_shape=jax.ShapeDtypeStruct((2, model), F32),
        in_specs=[vmem] * 3,
        out_specs=vmem,
        scratch_shapes=[pltpu.VMEM((tall // 2, DH), F32)],
        compiler_params=pltpu.CompilerParams(vmem_limit_bytes=4 << 20),
        cost_estimate=pl.CostEstimate(flops=10**10, transcendentals=0, bytes_accessed=60 << 20),
        name="merge_project",
    )(got, fresh, w_proj)
    others = to_others([mine] * 3, "mp")

    piece = jax.ShapeDtypeStruct((reqs, steps, width), BF16)
    queries, new_keys, new_values = pl.pallas_call(
        outputs_kernel,
        out_shape=(piece,) * 3,
        in_specs=[any_space] * 2 + [vmem] * 4,
        out_specs=(vmem,) * 3,
        scratch_shapes=[pltpu.VMEM((2, model, width), BF16), pltpu.SemaphoreType.DMA((2,))],
        compiler_params=pltpu.CompilerParams(vmem_limit_bytes=12 << 20),
        name="projections",
    )(mine, in_hbm(w_qkv), q_rows, normed, cosine, sine)

    cols = model // n_mp
    rows2 = jax.ShapeDtypeStruct((2, model), F32)
    middle, down = pl.pallas_call(
        mlp_kernel,
        out_shape=(rows2,) * 2,
        in_specs=[vmem] * 7,
        out_specs=(vmem,) * 2,
        compiler_params=pltpu.CompilerParams(vmem_limit_bytes=8 << 20),
        name="mlp",
    )(inputs, w_gate_up, w_down, mine, *others)
    hidden = pl.pallas_call(
        last_kernel,
        out_shape=jax.ShapeDtypeStruct((n_seq, 2, cols), BF16),
        in_specs=[vmem] * 5,
        out_specs=vmem,
        compiler_params=pltpu.CompilerParams(vmem_limit_bytes=4 << 20),
        name="last_sum",
    )(middle, down, *to_others([down] * 3, "mp"))
    hidden = lax.all_to_all(hidden, "seq", 0, 0)
    return (hidden.reshape(reqs, steps, cols), queries, new_keys, new_values)


def solution(mesh):
    placed = (
        P(),
        P(None, None, "mp"),
        P("mp", None),
        P(None, None, "mp"),
        P("mp", None),
        P(None, "seq", "mp"),
        P(None, "seq", "mp"),
        P(),
    )
    return jax.shard_map(
        per_device,
        mesh=mesh,
        in_specs=placed,
        out_specs=(P(None, None, "mp"),) * 4,
        check_vma=False,
    )
```

```python
import functools

import jax
import jax.numpy as jnp
import numpy as np
from jax import lax
from jax.experimental import pallas as pl
from jax.experimental.pallas import tpu as pltpu
from jax.sharding import PartitionSpec as P

DH = 128
NEG = -1e30
EPS = 1e-05
SCALE = DH ** (-0.5)
F32 = jnp.float32
BF16 = jnp.bfloat16


def norm_rows(x):
    centred = x - jnp.mean(x, axis=-1, keepdims=True)
    variance = jnp.mean(centred * centred, axis=-1, keepdims=True)
    return centred * lax.rsqrt(variance + EPS)


def split3(v):
    a = v.astype(BF16).astype(F32)
    rest = v - a
    b = rest.astype(BF16).astype(F32)
    return a, b, rest - b


def frequencies():
    half = DH // 2
    values = np.float32(10000.0) ** (np.float32(-2.0) * np.arange(half, dtype=np.float32) / np.float32(DH))
    lane = lax.broadcasted_iota(jnp.int32, (8, DH), 1) % half
    freq = jnp.full((8, DH), float(values[0]), F32)
    for i in range(1, half):
        freq = jnp.where(lane == i, float(values[i]), freq)
    return freq


def turn(v, cosine, sine):
    return v * cosine + pltpu.roll(v, DH // 2, 1) * sine


def rounded(v):
    return v.astype(BF16).astype(F32)


def cached_kernel(
    group, reqs, steps, block, width,
    len_hbm, x_hbm, w_hbm, ck_hbm, cv_hbm,
    part_out, q_rows, q_own, normed_out, cos_out, sin_out,
    len_s, order_s, x_v, w_v, ck_v, cv_v, xs, q16, sem_l, sem_x, sem_w, sem_k, sem_v,
):
    heads = width // DH
    rows = reqs * steps
    tall = steps * heads
    half = tall // 2
    seq = lax.axis_index("seq")
    first = seq * block
    copy_l = pltpu.make_async_copy(len_hbm, len_s, sem_l)
    copy_l.start()
    copy_x = pltpu.make_async_copy(x_hbm, x_v, sem_x)
    copy_x.start()
    copy_w = pltpu.make_async_copy(w_hbm.at[0], w_v, sem_w)
    copy_w.start()

    copy_l.wait()
    count = jnp.int32(0)
    for r in range(reqs):
        live = len_s[r] > first
        order_s[jnp.where(live, count, reqs - 1 - r + count)] = r
        count = count + live.astype(jnp.int32)

    def copies(cache, held, sems, lo):
        return [
            pltpu.make_async_copy(cache.at[order_s[i]], held.at[i], sems.at[i]) for i in range(lo, lo + group)
        ]

    def fetch(*args):
        for c in copies(*args):
            c.start()

    def arrive(*args):
        for c in copies(*args):
            c.wait()

    fetch(ck_hbm, ck_v, sem_k, 0)

    freq = frequencies()
    step_of = (lax.broadcasted_iota(jnp.int32, (8, DH), 0) % steps).astype(F32)
    lane8 = lax.broadcasted_iota(jnp.int32, (8, DH), 1)
    upper = lax.broadcasted_iota(jnp.int32, (8, DH), 0) >= steps
    for r in range(0, reqs, 2):
        place = jnp.where(upper, len_s[r + 1], len_s[r]).astype(F32) + step_of
        angles = place * freq
        cos_out[r * steps : (r + 2) * steps, :] = jnp.cos(angles)
        sine = jnp.sin(angles)
        sin_out[r * steps : (r + 2) * steps, :] = jnp.where(lane8 < DH // 2, -sine, sine)

    lane = lax.broadcasted_iota(jnp.int32, (tall, DH), 1)
    empty = jnp.where(lane[0:heads] % (DH // 2) == 0, NEG, 0.0).astype(BF16)
    for p in range(2 * reqs):
        part_out[p, 0] = jnp.zeros((heads, DH), BF16)
        part_out[p, 1] = jnp.zeros((heads, DH), BF16)
        part_out[p, 2] = empty

    copy_x.wait()
    fetch(cv_hbm, cv_v, sem_v, 0)
    for r in range(reqs):
        xs[pl.ds(r * steps, steps), :] = x_v[r].astype(F32)
    normed_out[...] = norm_rows(xs[...]).astype(BF16)

    copy_w.wait()
    part = jnp.dot(normed_out[...], w_v[...], preferred_element_type=F32)
    for h in range(heads):
        q = turn(part[:, h * DH : (h + 1) * DH], cos_out[...], sin_out[...]).astype(BF16)
        q_rows[:, h * DH : (h + 1) * DH] = q
        q16[pl.ds(h, rows, stride=heads), :] = q.astype(F32)
    q_own[...] = q16[pl.ds(seq * half, half), :]

    row_head = lax.broadcasted_iota(jnp.int32, (tall, DH), 0) % heads
    many_lane = lax.broadcasted_iota(jnp.int32, (group * tall, DH), 1)

    def attend(lo):
        arrive(ck_hbm, ck_v, sem_k, lo)
        scores = []
        for i in range(lo, lo + group):
            r = order_s[i]
            q = q16[pl.ds(pl.multiple_of(r * tall, tall), tall), :]
            spread = jnp.concatenate([jnp.where(row_head == h, q, 0.0).astype(BF16) for h in range(heads)], axis=1)
            score = lax.dot_general(spread, ck_v[i], (((1,), (1,)), ((), ())), preferred_element_type=F32)
            scores.append(jnp.where(lane < len_s[r] - first, score * SCALE, NEG))
        scores = jnp.concatenate(scores, axis=0)
        highest = jnp.max(scores, axis=-1, keepdims=True)
        weights = jnp.where(scores == NEG, 0.0, jnp.exp(scores - highest))
        total = jnp.sum(weights, axis=-1, keepdims=True)
        weights = weights.astype(BF16)
        pieces = split3(jnp.broadcast_to(highest, scores.shape)) + split3(jnp.broadcast_to(total, scores.shape))
        stats = pieces[5]
        for i in range(4, -1, -1):
            stats = jnp.where(many_lane % (DH // 2) == i, pieces[i], stats)
        arrive(cv_hbm, cv_v, sem_v, lo)
        for i in range(lo, lo + group):
            r = order_s[i]
            at = (i - lo) * tall
            wide = jnp.dot(weights[at : at + tall], cv_v[i], preferred_element_type=F32)
            o = wide[:, 0:DH]
            for h in range(1, heads):
                o = jnp.where(row_head == h, wide[:, h * DH : (h + 1) * DH], o)
            for j in range(2):
                lo_row = 2 * j * heads
                for k in range(2):
                    part_out[2 * r + j, k] = o[lo_row + k * heads : lo_row + (k + 1) * heads].astype(BF16)
                pair = [stats[at + lo_row + k * heads : at + lo_row + (k + 1) * heads] for k in range(2)]
                part_out[2 * r + j, 2] = jnp.where(lane[0:heads] < DH // 2, pair[0], pair[1]).astype(BF16)

    attend(0)
    for lo in range(group, reqs, group):
        @pl.when(count > lo)
        def _():
            fetch(ck_hbm, ck_v, sem_k, lo)
            fetch(cv_hbm, cv_v, sem_v, lo)
            attend(lo)


def fresh_kernel(
    steps,
    w_hbm, proj_hbm, q_own, normed, cosine, sine,
    fresh_out, proj_out,
    w_v, k16, v16, sem_w, sem_p,
):
    half = q_own.shape[0]
    heads = half // 2
    tall = 2 * half
    seq = lax.axis_index("seq")
    copies = [pltpu.make_async_copy(w_hbm.at[1 + j], w_v.at[j], sem_w.at[j]) for j in range(2)]
    for c in copies:
        c.start()
    copy_p = pltpu.make_async_copy(proj_hbm, proj_out, sem_p)
    copy_p.start()
    block = pl.multiple_of((seq // 4) * 8, 8)
    rows = normed[pl.ds(block, 8), :]
    turns = (cosine[pl.ds(block, 8), :], sine[pl.ds(block, 8), :])
    for j, store in enumerate((k16, v16)):
        copies[j].wait()
        part = jnp.dot(rows, w_v[j], preferred_element_type=F32)
        for h in range(heads):
            v = part[:, h * DH : (h + 1) * DH]
            store[pl.ds(h, 8, stride=heads), :] = rounded(turn(v, *turns) if j == 0 else v)
    q = q_own[...]
    step = (seq % 2) * 2 + lax.broadcasted_iota(jnp.int32, (half, 1), 0) // heads
    base = pl.multiple_of(((seq // 2) % 2) * tall, tall)
    scores = []
    values = []
    for s in range(steps):
        key = k16[pl.ds(base + s * heads, heads), :]
        value = v16[pl.ds(base + s * heads, heads), :]
        key = jnp.concatenate([key, key], axis=0)
        values.append(jnp.concatenate([value, value], axis=0))
        scores.append(jnp.sum(q * key, axis=-1, keepdims=True) * SCALE)
    high = scores[0]
    for s in range(1, steps):
        high = jnp.maximum(high, jnp.where(s <= step, scores[s], NEG))
    total = jnp.zeros_like(high)
    o = jnp.zeros((half, DH), F32)
    for s in range(steps):
        weight = jnp.where(s <= step, jnp.exp(scores[s] - high), 0.0)
        total = total + weight
        o = o + rounded(weight) * values[s]
    fresh_out[0] = o
    fresh_out[1] = jnp.broadcast_to(high, o.shape)
    fresh_out[2] = jnp.broadcast_to(total, o.shape)
    copy_p.wait()


def merge_kernel(got_ref, fresh_ref, w_ref, out_ref, ctx_s):
    heads = got_ref.shape[2]
    stats = got_ref[:, 2].astype(F32)
    for k in range(2):
        span = slice(k * heads, (k + 1) * heads)
        fresh, fresh_high, fresh_total = fresh_ref[0][span], fresh_ref[1][span, 0:1], fresh_ref[2][span, 0:1]
        at = [stats[:, :, k * DH // 2 + i : k * DH // 2 + i + 1] for i in range(6)]
        highest = (at[0] + at[1]) + at[2]
        total = (at[3] + at[4]) + at[5]
        top = jnp.maximum(jnp.max(highest, axis=0), fresh_high)
        factor = jnp.exp(highest - top[None])
        fresh_factor = jnp.exp(fresh_high - top)
        whole = jnp.sum(factor * total, axis=0) + fresh_factor * fresh_total
        o = jnp.sum(factor * got_ref[:, k].astype(F32), axis=0) + fresh_factor * fresh
        ctx_s[span, :] = o / whole
    ctx = jnp.concatenate([ctx_s[pl.ds(h, 2, stride=heads), :] for h in range(heads)], axis=1)
    out_ref[...] = jnp.dot(ctx.astype(BF16), w_ref[...], preferred_element_type=F32)


def outputs_kernel(
    after_hbm, w_hbm, q_rows, normed, cosine, sine,
    q_out, k_out, v_out,
    w_v, sem_w,
):
    reqs, steps, width = q_out.shape
    copies = [pltpu.make_async_copy(w_hbm.at[1 + j], w_v.at[j], sem_w.at[j]) for j in range(2)]
    for c in copies:
        c.start()
    q_out[...] = q_rows[...].reshape(q_out.shape)
    for j, out in enumerate((k_out, v_out)):
        copies[j].wait()
        part = jnp.dot(normed[...], w_v[j], preferred_element_type=F32)
        for h in range(width // DH):
            v = part[:, h * DH : (h + 1) * DH]
            v = turn(v, cosine[...], sine[...]) if j == 0 else v
            out[:, :, h * DH : (h + 1) * DH] = v.reshape(reqs, steps, DH).astype(BF16)


def mlp_kernel(x_ref, gu_ref, wd_ref, a_ref, b_ref, c_ref, d_ref, middle_out, down_out):
    seq = lax.axis_index("seq")
    x = x_ref[seq // 2].astype(F32)
    x = jnp.where(seq % 2 == 0, x[0:2], x[2:4])
    middle = x + ((a_ref[...] + b_ref[...]) + (c_ref[...] + d_ref[...]))
    middle_out[...] = middle
    normed = norm_rows(middle).astype(BF16)
    gate = jnp.dot(normed, gu_ref[0], preferred_element_type=F32)
    up = jnp.dot(normed, gu_ref[1], preferred_element_type=F32)
    active = ((gate / (1.0 + jnp.exp(-gate))) * up).astype(BF16)
    down_out[...] = jnp.dot(active, wd_ref[...], preferred_element_type=F32)


def last_kernel(middle_ref, a_ref, b_ref, c_ref, d_ref, out_ref):
    cols = out_ref.shape[2]
    span = pl.ds(pl.multiple_of(lax.axis_index("mp") * cols, cols), cols)
    down = (a_ref[:, span] + b_ref[:, span]) + (c_ref[:, span] + d_ref[:, span])
    hidden = (middle_ref[:, span] + down).astype(BF16)
    out_ref[...] = jnp.broadcast_to(hidden[None], out_ref.shape)


def to_others(values, axis):
    size = lax.axis_size(axis)
    got = [None] * (size - 1)
    for k in range(size - 1, 0, -1):
        got[k - 1] = lax.ppermute(values[k - 1], axis, [(i, i ^ k) for i in range(size)])
    return got


def per_device(inputs, w_qkv, w_out, w_gate_up, w_down, cache_keys, cache_values, lengths):
    reqs, steps, model = inputs.shape
    block = cache_keys.shape[1]
    width = cache_keys.shape[2]
    heads = width // DH
    rows = reqs * steps
    tall = steps * heads
    n_seq = lax.axis_size("seq")
    n_mp = lax.axis_size("mp")
    assert rows == 2 * n_seq and steps == 4 and n_mp == 4 and tall == 16
    group = max(reqs // 2, 1)
    in_hbm = functools.partial(pltpu.with_memory_space_constraint, memory_space=pltpu.HBM)
    any_space = pl.BlockSpec(memory_space=pltpu.HBM)
    vmem = pl.BlockSpec(memory_space=pltpu.VMEM)
    part, q_rows, q_own, normed, cosine, sine = pl.pallas_call(
        functools.partial(cached_kernel, group, reqs, steps, block, width),
        out_shape=(
            jax.ShapeDtypeStruct((n_seq, 3, heads, DH), BF16),
            jax.ShapeDtypeStruct((rows, width), BF16),
            jax.ShapeDtypeStruct((tall // 2, DH), F32),
            jax.ShapeDtypeStruct((rows, model), BF16),
            jax.ShapeDtypeStruct((rows, DH), F32),
            jax.ShapeDtypeStruct((rows, DH), F32),
        ),
        in_specs=[any_space] * 5,
        out_specs=(vmem,) * 6,
        scratch_shapes=[
            pltpu.SMEM((reqs,), jnp.int32),
            pltpu.SMEM((reqs,), jnp.int32),
            pltpu.VMEM(inputs.shape, BF16),
            pltpu.VMEM((model, width), BF16),
            pltpu.VMEM(cache_keys.shape, BF16),
            pltpu.VMEM(cache_values.shape, BF16),
            pltpu.VMEM((rows, model), F32),
            pltpu.VMEM((rows * heads, DH), F32),
            pltpu.SemaphoreType.DMA,
            pltpu.SemaphoreType.DMA,
            pltpu.SemaphoreType.DMA,
            pltpu.SemaphoreType.DMA((reqs,)),
            pltpu.SemaphoreType.DMA((reqs,)),
        ],
        compiler_params=pltpu.CompilerParams(vmem_limit_bytes=48 << 20),
        name="cached_attention",
    )(in_hbm(lengths), in_hbm(inputs), in_hbm(w_qkv), in_hbm(cache_keys), in_hbm(cache_values))

    got = lax.all_to_all(part, "seq", 0, 0)

    fresh, w_proj = pl.pallas_call(
        functools.partial(fresh_kernel, steps),
        out_shape=(jax.ShapeDtypeStruct((3, tall // 2, DH), F32), jax.ShapeDtypeStruct(w_out.shape, BF16)),
        in_specs=[any_space] * 2 + [vmem] * 4,
        out_specs=(vmem,) * 2,
        scratch_shapes=[
            pltpu.VMEM((2, model, width), BF16),
            pltpu.VMEM((8 * heads, DH), F32),
            pltpu.VMEM((8 * heads, DH), F32),
            pltpu.SemaphoreType.DMA((2,)),
            pltpu.SemaphoreType.DMA,
        ],
        compiler_params=pltpu.CompilerParams(vmem_limit_bytes=12 << 20),
        name="new_tokens",
    )(in_hbm(w_qkv), in_hbm(w_out), q_own, normed, cosine, sine)
    mine = pl.pallas_call(
        merge_kernel,
        out_shape=jax.ShapeDtypeStruct((2, model), F32),
        in_specs=[vmem] * 3,
        out_specs=vmem,
        scratch_shapes=[pltpu.VMEM((tall // 2, DH), F32)],
        compiler_params=pltpu.CompilerParams(vmem_limit_bytes=4 << 20),
        cost_estimate=pl.CostEstimate(flops=10**10, transcendentals=0, bytes_accessed=60 << 20),
        name="merge_project",
    )(got, fresh, w_proj)
    others = to_others([mine] * 3, "mp")

    piece = jax.ShapeDtypeStruct((reqs, steps, width), BF16)
    queries, new_keys, new_values = pl.pallas_call(
        outputs_kernel,
        out_shape=(piece,) * 3,
        in_specs=[any_space] * 2 + [vmem] * 4,
        out_specs=(vmem,) * 3,
        scratch_shapes=[pltpu.VMEM((2, model, width), BF16), pltpu.SemaphoreType.DMA((2,))],
        compiler_params=pltpu.CompilerParams(vmem_limit_bytes=12 << 20),
        name="projections",
    )(mine, in_hbm(w_qkv), q_rows, normed, cosine, sine)

    cols = model // n_mp
    rows2 = jax.ShapeDtypeStruct((2, model), F32)
    middle, down = pl.pallas_call(
        mlp_kernel,
        out_shape=(rows2,) * 2,
        in_specs=[vmem] * 7,
        out_specs=(vmem,) * 2,
        compiler_params=pltpu.CompilerParams(vmem_limit_bytes=8 << 20),
        name="mlp",
    )(inputs, w_gate_up, w_down, mine, others[0], others[2], others[1])
    back = to_others([down] * 3, "mp")
    hidden = pl.pallas_call(
        last_kernel,
        out_shape=jax.ShapeDtypeStruct((n_seq, 2, cols), BF16),
        in_specs=[vmem] * 5,
        out_specs=vmem,
        compiler_params=pltpu.CompilerParams(vmem_limit_bytes=4 << 20),
        name="last_sum",
    )(middle, down, back[0], back[2], back[1])
    hidden = lax.all_to_all(hidden, "seq", 0, 0)
    return (hidden.reshape(reqs, steps, cols), queries, new_keys, new_values)


def solution(mesh):
    placed = (
        P(),
        P(None, None, "mp"),
        P("mp", None),
        P(None, None, "mp"),
        P("mp", None),
        P(None, "seq", "mp"),
        P(None, "seq", "mp"),
        P(),
    )
    return jax.shard_map(
        per_device,
        mesh=mesh,
        in_specs=placed,
        out_specs=(P(None, None, "mp"),) * 4,
        check_vma=False,
    )
```

```python
import functools

import jax
import jax.numpy as jnp
import numpy as np
from jax import lax
from jax.experimental import pallas as pl
from jax.experimental.pallas import tpu as pltpu
from jax.sharding import PartitionSpec as P

DH = 128
NEG = -1e30
EPS = 1e-05
SCALE = DH ** (-0.5)
F32 = jnp.float32
BF16 = jnp.bfloat16


def norm_rows(x):
    centred = x - jnp.mean(x, axis=-1, keepdims=True)
    variance = jnp.mean(centred * centred, axis=-1, keepdims=True)
    return centred * lax.rsqrt(variance + EPS)


def split3(v):
    a = v.astype(BF16).astype(F32)
    rest = v - a
    b = rest.astype(BF16).astype(F32)
    return a, b, rest - b


def frequencies():
    half = DH // 2
    values = np.float32(10000.0) ** (np.float32(-2.0) * np.arange(half, dtype=np.float32) / np.float32(DH))
    lane = lax.broadcasted_iota(jnp.int32, (8, DH), 1) % half
    freq = jnp.full((8, DH), float(values[0]), F32)
    for i in range(1, half):
        freq = jnp.where(lane == i, float(values[i]), freq)
    return freq


def turn(v, cosine, sine):
    return v * cosine + pltpu.roll(v, DH // 2, 1) * sine


def rounded(v):
    return v.astype(BF16).astype(F32)


def cached_kernel(
    group, reqs, steps, block, width,
    len_hbm, x_hbm, w_hbm, ck_hbm, cv_hbm,
    part_out, q_rows, q_own, normed_out, cos_out, sin_out,
    len_s, order_s, x_v, w_v, ck_v, cv_v, xs, q16, sem_l, sem_x, sem_w, sem_k, sem_v,
):
    heads = width // DH
    rows = reqs * steps
    tall = steps * heads
    half = tall // 2
    seq = lax.axis_index("seq")
    first = seq * block
    copy_l = pltpu.make_async_copy(len_hbm, len_s, sem_l)
    copy_l.start()
    copy_x = pltpu.make_async_copy(x_hbm, x_v, sem_x)
    copy_x.start()
    copy_w = pltpu.make_async_copy(w_hbm.at[0], w_v, sem_w)
    copy_w.start()

    copy_l.wait()
    count = jnp.int32(0)
    for r in range(reqs):
        live = len_s[r] > first
        order_s[jnp.where(live, count, reqs - 1 - r + count)] = r
        count = count + live.astype(jnp.int32)

    def copies(cache, held, sems, lo):
        return [
            pltpu.make_async_copy(cache.at[order_s[i]], held.at[i], sems.at[i]) for i in range(lo, lo + group)
        ]

    def fetch(*args):
        for c in copies(*args):
            c.start()

    def arrive(*args):
        for c in copies(*args):
            c.wait()

    fetch(ck_hbm, ck_v, sem_k, 0)

    freq = frequencies()
    step_of = (lax.broadcasted_iota(jnp.int32, (8, DH), 0) % steps).astype(F32)
    lane8 = lax.broadcasted_iota(jnp.int32, (8, DH), 1)
    upper = lax.broadcasted_iota(jnp.int32, (8, DH), 0) >= steps
    for r in range(0, reqs, 2):
        place = jnp.where(upper, len_s[r + 1], len_s[r]).astype(F32) + step_of
        angles = place * freq
        cos_out[r * steps : (r + 2) * steps, :] = jnp.cos(angles)
        sine = jnp.sin(angles)
        sin_out[r * steps : (r + 2) * steps, :] = jnp.where(lane8 < DH // 2, -sine, sine)

    lane = lax.broadcasted_iota(jnp.int32, (tall, DH), 1)
    empty = jnp.where(lane[0:heads] % (DH // 2) == 0, NEG, 0.0).astype(BF16)
    for p in range(2 * reqs):
        part_out[p, 0] = jnp.zeros((heads, DH), BF16)
        part_out[p, 1] = jnp.zeros((heads, DH), BF16)
        part_out[p, 2] = empty

    copy_x.wait()
    fetch(cv_hbm, cv_v, sem_v, 0)
    for r in range(reqs):
        xs[pl.ds(r * steps, steps), :] = x_v[r].astype(F32)
    normed_out[...] = norm_rows(xs[...]).astype(BF16)

    copy_w.wait()
    part = jnp.dot(normed_out[...], w_v[...], preferred_element_type=F32)
    for h in range(heads):
        q = turn(part[:, h * DH : (h + 1) * DH], cos_out[...], sin_out[...]).astype(BF16)
        q_rows[:, h * DH : (h + 1) * DH] = q
        q16[pl.ds(h, rows, stride=heads), :] = q.astype(F32)
    q_own[...] = q16[pl.ds(seq * half, half), :]

    row_head = lax.broadcasted_iota(jnp.int32, (tall, DH), 0) % heads
    many_lane = lax.broadcasted_iota(jnp.int32, (group * tall, DH), 1)

    def attend(lo):
        arrive(ck_hbm, ck_v, sem_k, lo)
        scores = []
        for i in range(lo, lo + group):
            r = order_s[i]
            q = q16[pl.ds(pl.multiple_of(r * tall, tall), tall), :]
            spread = jnp.concatenate([jnp.where(row_head == h, q, 0.0).astype(BF16) for h in range(heads)], axis=1)
            score = lax.dot_general(spread, ck_v[i], (((1,), (1,)), ((), ())), preferred_element_type=F32)
            scores.append(jnp.where(lane < len_s[r] - first, score * SCALE, NEG))
        scores = jnp.concatenate(scores, axis=0)
        highest = jnp.max(scores, axis=-1, keepdims=True)
        weights = jnp.where(scores == NEG, 0.0, jnp.exp(scores - highest))
        total = jnp.sum(weights, axis=-1, keepdims=True)
        weights = weights.astype(BF16)
        pieces = split3(jnp.broadcast_to(highest, scores.shape)) + split3(jnp.broadcast_to(total, scores.shape))
        stats = pieces[5]
        for i in range(4, -1, -1):
            stats = jnp.where(many_lane % (DH // 2) == i, pieces[i], stats)
        arrive(cv_hbm, cv_v, sem_v, lo)
        for i in range(lo, lo + group):
            r = order_s[i]
            at = (i - lo) * tall
            wide = jnp.dot(weights[at : at + tall], cv_v[i], preferred_element_type=F32)
            o = wide[:, 0:DH]
            for h in range(1, heads):
                o = jnp.where(row_head == h, wide[:, h * DH : (h + 1) * DH], o)
            for j in range(2):
                lo_row = 2 * j * heads
                for k in range(2):
                    part_out[2 * r + j, k] = o[lo_row + k * heads : lo_row + (k + 1) * heads].astype(BF16)
                pair = [stats[at + lo_row + k * heads : at + lo_row + (k + 1) * heads] for k in range(2)]
                part_out[2 * r + j, 2] = jnp.where(lane[0:heads] < DH // 2, pair[0], pair[1]).astype(BF16)

    attend(0)
    for lo in range(group, reqs, group):
        @pl.when(count > lo)
        def _():
            fetch(ck_hbm, ck_v, sem_k, lo)
            fetch(cv_hbm, cv_v, sem_v, lo)
            attend(lo)


def fresh_kernel(
    w_hbm, proj_hbm, q_rows, q_own, normed, cosine, sine,
    q_out, k_out, v_out, fresh_out, proj_out,
    w_v, k_s, v_s, k16, v16, sem_w, sem_p,
):
    reqs, steps, width = q_out.shape
    half = q_own.shape[0]
    heads = half // 2
    tall = 2 * half
    seq = lax.axis_index("seq")
    copies = [pltpu.make_async_copy(w_hbm.at[1 + j], w_v.at[j], sem_w.at[j]) for j in range(2)]
    for c in copies:
        c.start()
    copy_p = pltpu.make_async_copy(proj_hbm, proj_out, sem_p)
    copy_p.start()
    q_out[...] = q_rows[...].reshape(q_out.shape)
    block = pl.multiple_of((seq // 4) * 8, 8)
    for j, (out, whole, store) in enumerate(((k_out, k_s, k16), (v_out, v_s, v16))):
        copies[j].wait()
        part = jnp.dot(normed[...], w_v[j], preferred_element_type=F32)
        for h in range(heads):
            span = slice(h * DH, (h + 1) * DH)
            v = part[:, span]
            v = (turn(v, cosine[...], sine[...]) if j == 0 else v).astype(BF16)
            out[:, :, span] = v.reshape(reqs, steps, DH)
            whole[:, span] = v.astype(F32)
        for h in range(heads):
            store[pl.ds(h, 8, stride=heads), :] = whole[pl.ds(block, 8), h * DH : (h + 1) * DH]
    q = q_own[...]
    step = (seq % 2) * 2 + lax.broadcasted_iota(jnp.int32, (half, 1), 0) // heads
    base = pl.multiple_of(((seq // 2) % 2) * tall, tall)
    scores = []
    values = []
    for s in range(steps):
        key = k16[pl.ds(base + s * heads, heads), :]
        value = v16[pl.ds(base + s * heads, heads), :]
        key = jnp.concatenate([key, key], axis=0)
        values.append(jnp.concatenate([value, value], axis=0))
        scores.append(jnp.sum(q * key, axis=-1, keepdims=True) * SCALE)
    high = scores[0]
    for s in range(1, steps):
        high = jnp.maximum(high, jnp.where(s <= step, scores[s], NEG))
    total = jnp.zeros_like(high)
    o = jnp.zeros((half, DH), F32)
    for s in range(steps):
        weight = jnp.where(s <= step, jnp.exp(scores[s] - high), 0.0)
        total = total + weight
        o = o + rounded(weight) * values[s]
    fresh_out[0] = o
    fresh_out[1] = jnp.broadcast_to(high, o.shape)
    fresh_out[2] = jnp.broadcast_to(total, o.shape)
    copy_p.wait()


def merge_kernel(got_ref, fresh_ref, w_ref, out_ref, ctx_s):
    heads = got_ref.shape[2]
    stats = got_ref[:, 2].astype(F32)
    for k in range(2):
        span = slice(k * heads, (k + 1) * heads)
        fresh, fresh_high, fresh_total = fresh_ref[0][span], fresh_ref[1][span, 0:1], fresh_ref[2][span, 0:1]
        at = [stats[:, :, k * DH // 2 + i : k * DH // 2 + i + 1] for i in range(6)]
        highest = (at[0] + at[1]) + at[2]
        total = (at[3] + at[4]) + at[5]
        top = jnp.maximum(jnp.max(highest, axis=0), fresh_high)
        factor = jnp.exp(highest - top[None])
        fresh_factor = jnp.exp(fresh_high - top)
        whole = jnp.sum(factor * total, axis=0) + fresh_factor * fresh_total
        o = jnp.sum(factor * got_ref[:, k].astype(F32), axis=0) + fresh_factor * fresh
        ctx_s[span, :] = o / whole
    ctx = jnp.concatenate([ctx_s[pl.ds(h, 2, stride=heads), :] for h in range(heads)], axis=1)
    out_ref[...] = jnp.dot(ctx.astype(BF16), w_ref[...], preferred_element_type=F32)


def mlp_kernel(x_ref, gu_ref, wd_ref, a_ref, b_ref, c_ref, d_ref, middle_out, down_out):
    seq = lax.axis_index("seq")
    x = x_ref[seq // 2].astype(F32)
    x = jnp.where(seq % 2 == 0, x[0:2], x[2:4])
    middle = x + ((a_ref[...] + b_ref[...]) + (c_ref[...] + d_ref[...]))
    middle_out[...] = middle
    normed = norm_rows(middle).astype(BF16)
    gate = jnp.dot(normed, gu_ref[0], preferred_element_type=F32)
    up = jnp.dot(normed, gu_ref[1], preferred_element_type=F32)
    active = ((gate / (1.0 + jnp.exp(-gate))) * up).astype(BF16)
    down_out[...] = jnp.dot(active, wd_ref[...], preferred_element_type=F32)


def last_kernel(middle_ref, a_ref, b_ref, c_ref, d_ref, out_ref):
    cols = out_ref.shape[2]
    span = pl.ds(pl.multiple_of(lax.axis_index("mp") * cols, cols), cols)
    down = (a_ref[:, span] + b_ref[:, span]) + (c_ref[:, span] + d_ref[:, span])
    hidden = (middle_ref[:, span] + down).astype(BF16)
    out_ref[...] = jnp.broadcast_to(hidden[None], out_ref.shape)


def to_others(values, axis):
    size = lax.axis_size(axis)
    got = [None] * (size - 1)
    for k in range(size - 1, 0, -1):
        got[k - 1] = lax.ppermute(values[k - 1], axis, [(i, i ^ k) for i in range(size)])
    return got


def per_device(inputs, w_qkv, w_out, w_gate_up, w_down, cache_keys, cache_values, lengths):
    reqs, steps, model = inputs.shape
    block = cache_keys.shape[1]
    width = cache_keys.shape[2]
    heads = width // DH
    rows = reqs * steps
    tall = steps * heads
    n_seq = lax.axis_size("seq")
    n_mp = lax.axis_size("mp")
    assert rows == 2 * n_seq and steps == 4 and n_mp == 4 and tall == 16
    group = max(reqs // 2, 1)
    in_hbm = functools.partial(pltpu.with_memory_space_constraint, memory_space=pltpu.HBM)
    any_space = pl.BlockSpec(memory_space=pltpu.HBM)
    vmem = pl.BlockSpec(memory_space=pltpu.VMEM)
    part, q_rows, q_own, normed, cosine, sine = pl.pallas_call(
        functools.partial(cached_kernel, group, reqs, steps, block, width),
        out_shape=(
            jax.ShapeDtypeStruct((n_seq, 3, heads, DH), BF16),
            jax.ShapeDtypeStruct((rows, width), BF16),
            jax.ShapeDtypeStruct((tall // 2, DH), F32),
            jax.ShapeDtypeStruct((rows, model), BF16),
            jax.ShapeDtypeStruct((rows, DH), F32),
            jax.ShapeDtypeStruct((rows, DH), F32),
        ),
        in_specs=[any_space] * 5,
        out_specs=(vmem,) * 6,
        scratch_shapes=[
            pltpu.SMEM((reqs,), jnp.int32),
            pltpu.SMEM((reqs,), jnp.int32),
            pltpu.VMEM(inputs.shape, BF16),
            pltpu.VMEM((model, width), BF16),
            pltpu.VMEM(cache_keys.shape, BF16),
            pltpu.VMEM(cache_values.shape, BF16),
            pltpu.VMEM((rows, model), F32),
            pltpu.VMEM((rows * heads, DH), F32),
            pltpu.SemaphoreType.DMA,
            pltpu.SemaphoreType.DMA,
            pltpu.SemaphoreType.DMA,
            pltpu.SemaphoreType.DMA((reqs,)),
            pltpu.SemaphoreType.DMA((reqs,)),
        ],
        compiler_params=pltpu.CompilerParams(vmem_limit_bytes=48 << 20),
        name="cached_attention",
    )(in_hbm(lengths), in_hbm(inputs), in_hbm(w_qkv), in_hbm(cache_keys), in_hbm(cache_values))

    got = lax.all_to_all(part, "seq", 0, 0)

    piece = jax.ShapeDtypeStruct((reqs, steps, width), BF16)
    queries, new_keys, new_values, fresh, w_proj = pl.pallas_call(
        fresh_kernel,
        out_shape=(
            piece, piece, piece,
            jax.ShapeDtypeStruct((3, tall // 2, DH), F32),
            jax.ShapeDtypeStruct(w_out.shape, BF16),
        ),
        in_specs=[any_space] * 2 + [vmem] * 5,
        out_specs=(vmem,) * 5,
        scratch_shapes=[
            pltpu.VMEM((2, model, width), BF16),
            pltpu.VMEM((rows, width), F32),
            pltpu.VMEM((rows, width), F32),
            pltpu.VMEM((8 * heads, DH), F32),
            pltpu.VMEM((8 * heads, DH), F32),
            pltpu.SemaphoreType.DMA((2,)),
            pltpu.SemaphoreType.DMA,
        ],
        compiler_params=pltpu.CompilerParams(vmem_limit_bytes=14 << 20),
        name="new_tokens",
    )(in_hbm(w_qkv), in_hbm(w_out), q_rows, q_own, normed, cosine, sine)
    mine = pl.pallas_call(
        merge_kernel,
        out_shape=jax.ShapeDtypeStruct((2, model), F32),
        in_specs=[vmem] * 3,
        out_specs=vmem,
        scratch_shapes=[pltpu.VMEM((tall // 2, DH), F32)],
        compiler_params=pltpu.CompilerParams(vmem_limit_bytes=4 << 20),
        cost_estimate=pl.CostEstimate(flops=10**10, transcendentals=0, bytes_accessed=60 << 20),
        name="merge_project",
    )(got, fresh, w_proj)
    others = to_others([mine] * 3, "mp")

    cols = model // n_mp
    rows2 = jax.ShapeDtypeStruct((2, model), F32)
    middle, down = pl.pallas_call(
        mlp_kernel,
        out_shape=(rows2,) * 2,
        in_specs=[vmem] * 7,
        out_specs=(vmem,) * 2,
        compiler_params=pltpu.CompilerParams(vmem_limit_bytes=8 << 20),
        name="mlp",
    )(inputs, w_gate_up, w_down, mine, *others)
    hidden = pl.pallas_call(
        last_kernel,
        out_shape=jax.ShapeDtypeStruct((n_seq, 2, cols), BF16),
        in_specs=[vmem] * 5,
        out_specs=vmem,
        compiler_params=pltpu.CompilerParams(vmem_limit_bytes=4 << 20),
        name="last_sum",
    )(middle, down, *to_others([down] * 3, "mp"))
    hidden = lax.all_to_all(hidden, "seq", 0, 0)
    return (hidden.reshape(reqs, steps, cols), queries, new_keys, new_values)


def solution(mesh):
    placed = (
        P(),
        P(None, None, "mp"),
        P("mp", None),
        P(None, None, "mp"),
        P("mp", None),
        P(None, "seq", "mp"),
        P(None, "seq", "mp"),
        P(),
    )
    return jax.shard_map(
        per_device,
        mesh=mesh,
        in_specs=placed,
        out_specs=(P(None, None, "mp"),) * 4,
        check_vma=False,
    )
```

```python
import functools

import jax
import jax.numpy as jnp
import numpy as np
from jax import lax
from jax.experimental import pallas as pl
from jax.experimental.pallas import tpu as pltpu
from jax.sharding import PartitionSpec as P

DH = 128
NEG = -1e30
EPS = 1e-05
SCALE = DH ** (-0.5)
F32 = jnp.float32
BF16 = jnp.bfloat16


def norm_rows(x):
    centred = x - jnp.mean(x, axis=-1, keepdims=True)
    variance = jnp.mean(centred * centred, axis=-1, keepdims=True)
    return centred * lax.rsqrt(variance + EPS)


def split3(v):
    a = v.astype(BF16).astype(F32)
    rest = v - a
    b = rest.astype(BF16).astype(F32)
    return a, b, rest - b


def frequencies():
    half = DH // 2
    values = np.float32(10000.0) ** (np.float32(-2.0) * np.arange(half, dtype=np.float32) / np.float32(DH))
    lane = lax.broadcasted_iota(jnp.int32, (8, DH), 1) % half
    freq = jnp.full((8, DH), float(values[0]), F32)
    for i in range(1, half):
        freq = jnp.where(lane == i, float(values[i]), freq)
    return freq


def turn(v, cosine, sine):
    return v * cosine + pltpu.roll(v, DH // 2, 1) * sine


def rounded(v):
    return v.astype(BF16).astype(F32)


def cached_kernel(
    group, reqs, steps, block, width,
    len_hbm, x_hbm, w_hbm, ck_hbm, cv_hbm,
    part_out, q_rows, q_own, normed_out, cos_out, sin_out,
    len_s, order_s, x_v, w_v, ck_v, cv_v, xs, q16, sem_l, sem_x, sem_w, sem_k, sem_v,
):
    heads = width // DH
    rows = reqs * steps
    tall = steps * heads
    half = tall // 2
    seq = lax.axis_index("seq")
    first = seq * block
    copy_l = pltpu.make_async_copy(len_hbm, len_s, sem_l)
    copy_l.start()
    copy_x = pltpu.make_async_copy(x_hbm, x_v, sem_x)
    copy_x.start()
    copy_w = pltpu.make_async_copy(w_hbm.at[0], w_v, sem_w)
    copy_w.start()

    copy_l.wait()
    count = jnp.int32(0)
    for r in range(reqs):
        live = len_s[r] > first
        order_s[jnp.where(live, count, reqs - 1 - r + count)] = r
        count = count + live.astype(jnp.int32)

    def copies(cache, held, sems, lo):
        return [
            pltpu.make_async_copy(cache.at[order_s[i]], held.at[i], sems.at[i]) for i in range(lo, lo + group)
        ]

    def fetch(*args):
        for c in copies(*args):
            c.start()

    def arrive(*args):
        for c in copies(*args):
            c.wait()

    fetch(ck_hbm, ck_v, sem_k, 0)

    freq = frequencies()
    step_of = (lax.broadcasted_iota(jnp.int32, (8, DH), 0) % steps).astype(F32)
    lane8 = lax.broadcasted_iota(jnp.int32, (8, DH), 1)
    upper = lax.broadcasted_iota(jnp.int32, (8, DH), 0) >= steps
    for r in range(0, reqs, 2):
        place = jnp.where(upper, len_s[r + 1], len_s[r]).astype(F32) + step_of
        angles = place * freq
        cos_out[r * steps : (r + 2) * steps, :] = jnp.cos(angles)
        sine = jnp.sin(angles)
        sin_out[r * steps : (r + 2) * steps, :] = jnp.where(lane8 < DH // 2, -sine, sine)

    lane = lax.broadcasted_iota(jnp.int32, (tall, DH), 1)
    empty = jnp.where(lane[0:heads] % (DH // 2) == 0, NEG, 0.0).astype(BF16)
    for p in range(2 * reqs):
        part_out[p, 0] = jnp.zeros((heads, DH), BF16)
        part_out[p, 1] = jnp.zeros((heads, DH), BF16)
        part_out[p, 2] = empty

    copy_x.wait()
    fetch(cv_hbm, cv_v, sem_v, 0)
    for r in range(reqs):
        xs[pl.ds(r * steps, steps), :] = x_v[r].astype(F32)
    normed_out[...] = norm_rows(xs[...]).astype(BF16)

    copy_w.wait()
    part = jnp.dot(normed_out[...], w_v[...], preferred_element_type=F32)
    for h in range(heads):
        q = turn(part[:, h * DH : (h + 1) * DH], cos_out[...], sin_out[...]).astype(BF16)
        q_rows[:, h * DH : (h + 1) * DH] = q
        q16[pl.ds(h, rows, stride=heads), :] = q.astype(F32)
    q_own[...] = q16[pl.ds(seq * half, half), :]

    row_head = lax.broadcasted_iota(jnp.int32, (tall, DH), 0) % heads
    many_lane = lax.broadcasted_iota(jnp.int32, (group * tall, DH), 1)

    def attend(lo):
        arrive(ck_hbm, ck_v, sem_k, lo)
        scores = []
        for i in range(lo, lo + group):
            r = order_s[i]
            q = q16[pl.ds(pl.multiple_of(r * tall, tall), tall), :]
            spread = jnp.concatenate([jnp.where(row_head == h, q, 0.0).astype(BF16) for h in range(heads)], axis=1)
            score = lax.dot_general(spread, ck_v[i], (((1,), (1,)), ((), ())), preferred_element_type=F32)
            scores.append(jnp.where(lane < len_s[r] - first, score * SCALE, NEG))
        scores = jnp.concatenate(scores, axis=0)
        highest = jnp.max(scores, axis=-1, keepdims=True)
        weights = jnp.where(scores == NEG, 0.0, jnp.exp(scores - highest))
        total = jnp.sum(weights, axis=-1, keepdims=True)
        weights = weights.astype(BF16)
        pieces = split3(jnp.broadcast_to(highest, scores.shape)) + split3(jnp.broadcast_to(total, scores.shape))
        stats = pieces[5]
        for i in range(4, -1, -1):
            stats = jnp.where(many_lane % (DH // 2) == i, pieces[i], stats)
        arrive(cv_hbm, cv_v, sem_v, lo)
        for i in range(lo, lo + group):
            r = order_s[i]
            at = (i - lo) * tall
            wide = jnp.dot(weights[at : at + tall], cv_v[i], preferred_element_type=F32)
            o = wide[:, 0:DH]
            for h in range(1, heads):
                o = jnp.where(row_head == h, wide[:, h * DH : (h + 1) * DH], o)
            for j in range(2):
                lo_row = 2 * j * heads
                for k in range(2):
                    part_out[2 * r + j, k] = o[lo_row + k * heads : lo_row + (k + 1) * heads].astype(BF16)
                pair = [stats[at + lo_row + k * heads : at + lo_row + (k + 1) * heads] for k in range(2)]
                part_out[2 * r + j, 2] = jnp.where(lane[0:heads] < DH // 2, pair[0], pair[1]).astype(BF16)

    attend(0)
    for lo in range(group, reqs, group):
        @pl.when(count > lo)
        def _():
            fetch(ck_hbm, ck_v, sem_k, lo)
            fetch(cv_hbm, cv_v, sem_v, lo)
            attend(lo)


def fresh_kernel(
    w_hbm, proj_hbm, q_rows, q_own, normed, cosine, sine,
    q_out, k_out, v_out, fresh_out, proj_out,
    w_v, k_s, v_s, k16, v16, sem_w, sem_p,
):
    reqs, steps, width = q_out.shape
    half = q_own.shape[0]
    heads = half // 2
    tall = 2 * half
    seq = lax.axis_index("seq")
    copies = [pltpu.make_async_copy(w_hbm.at[1 + j], w_v.at[j], sem_w.at[j]) for j in range(2)]
    for c in copies:
        c.start()
    copy_p = pltpu.make_async_copy(proj_hbm, proj_out, sem_p)
    copy_p.start()
    q_out[...] = q_rows[...].reshape(q_out.shape)
    block = pl.multiple_of((seq // 4) * 8, 8)
    for j, (out, whole, store) in enumerate(((k_out, k_s, k16), (v_out, v_s, v16))):
        copies[j].wait()
        part = jnp.dot(normed[...], w_v[j], preferred_element_type=F32)
        for h in range(heads):
            span = slice(h * DH, (h + 1) * DH)
            v = part[:, span]
            v = (turn(v, cosine[...], sine[...]) if j == 0 else v).astype(BF16)
            out[:, :, span] = v.reshape(reqs, steps, DH)
            whole[:, span] = v.astype(F32)
        for h in range(heads):
            store[pl.ds(h, 8, stride=heads), :] = whole[pl.ds(block, 8), h * DH : (h + 1) * DH]
    q = q_own[...]
    step = (seq % 2) * 2 + lax.broadcasted_iota(jnp.int32, (half, 1), 0) // heads
    base = pl.multiple_of(((seq // 2) % 2) * tall, tall)
    scores = []
    values = []
    for s in range(steps):
        key = k16[pl.ds(base + s * heads, heads), :]
        value = v16[pl.ds(base + s * heads, heads), :]
        key = jnp.concatenate([key, key], axis=0)
        values.append(jnp.concatenate([value, value], axis=0))
        scores.append(jnp.sum(q * key, axis=-1, keepdims=True) * SCALE)
    high = scores[0]
    for s in range(1, steps):
        high = jnp.maximum(high, jnp.where(s <= step, scores[s], NEG))
    total = jnp.zeros_like(high)
    o = jnp.zeros((half, DH), F32)
    for s in range(steps):
        weight = jnp.where(s <= step, jnp.exp(scores[s] - high), 0.0)
        total = total + weight
        o = o + rounded(weight) * values[s]
    fresh_out[0] = o
    fresh_out[1] = jnp.broadcast_to(high, o.shape)
    fresh_out[2] = jnp.broadcast_to(total, o.shape)
    copy_p.wait()


def merge_kernel(got_ref, fresh_ref, w_ref, out_ref, ctx_s):
    heads = got_ref.shape[2]
    stats = got_ref[:, 2].astype(F32)
    for k in range(2):
        span = slice(k * heads, (k + 1) * heads)
        fresh, fresh_high, fresh_total = fresh_ref[0][span], fresh_ref[1][span, 0:1], fresh_ref[2][span, 0:1]
        at = [stats[:, :, k * DH // 2 + i : k * DH // 2 + i + 1] for i in range(6)]
        highest = (at[0] + at[1]) + at[2]
        total = (at[3] + at[4]) + at[5]
        top = jnp.maximum(jnp.max(highest, axis=0), fresh_high)
        factor = jnp.exp(highest - top[None])
        fresh_factor = jnp.exp(fresh_high - top)
        whole = jnp.sum(factor * total, axis=0) + fresh_factor * fresh_total
        o = jnp.sum(factor * got_ref[:, k].astype(F32), axis=0) + fresh_factor * fresh
        ctx_s[span, :] = o / whole
    ctx = jnp.concatenate([ctx_s[pl.ds(h, 2, stride=heads), :] for h in range(heads)], axis=1)
    out_ref[...] = jnp.dot(ctx.astype(BF16), w_ref[...], preferred_element_type=F32)


def mlp_kernel(x_ref, gu_ref, wd_ref, a_ref, b_ref, c_ref, d_ref, middle_out, down_out):
    seq = lax.axis_index("seq")
    x = x_ref[seq // 2].astype(F32)
    x = jnp.where(seq % 2 == 0, x[0:2], x[2:4])
    middle = x + ((a_ref[...] + b_ref[...]) + (c_ref[...] + d_ref[...]))
    middle_out[...] = middle
    normed = norm_rows(middle).astype(BF16)
    gate = jnp.dot(normed, gu_ref[0], preferred_element_type=F32)
    up = jnp.dot(normed, gu_ref[1], preferred_element_type=F32)
    active = ((gate / (1.0 + jnp.exp(-gate))) * up).astype(BF16)
    down_out[...] = jnp.dot(active, wd_ref[...], preferred_element_type=F32)


def last_kernel(middle_ref, a_ref, b_ref, c_ref, d_ref, out_ref):
    cols = out_ref.shape[2]
    span = pl.ds(pl.multiple_of(lax.axis_index("mp") * cols, cols), cols)
    down = (a_ref[:, span] + b_ref[:, span]) + (c_ref[:, span] + d_ref[:, span])
    hidden = (middle_ref[:, span] + down).astype(BF16)
    out_ref[...] = jnp.broadcast_to(hidden[None], out_ref.shape)


def to_others(values, axis):
    size = lax.axis_size(axis)
    got = [None] * (size - 1)
    for k in range(size - 1, 0, -1):
        got[k - 1] = lax.ppermute(values[k - 1], axis, [(i, i ^ k) for i in range(size)])
    return got


def per_device(inputs, w_qkv, w_out, w_gate_up, w_down, cache_keys, cache_values, lengths):
    reqs, steps, model = inputs.shape
    block = cache_keys.shape[1]
    width = cache_keys.shape[2]
    heads = width // DH
    rows = reqs * steps
    tall = steps * heads
    n_seq = lax.axis_size("seq")
    n_mp = lax.axis_size("mp")
    assert rows == 2 * n_seq and steps == 4 and n_mp == 4 and tall == 16
    group = max(reqs // 2, 1)
    in_hbm = functools.partial(pltpu.with_memory_space_constraint, memory_space=pltpu.HBM)
    any_space = pl.BlockSpec(memory_space=pltpu.HBM)
    vmem = pl.BlockSpec(memory_space=pltpu.VMEM)
    part, q_rows, q_own, normed, cosine, sine = pl.pallas_call(
        functools.partial(cached_kernel, group, reqs, steps, block, width),
        out_shape=(
            jax.ShapeDtypeStruct((n_seq, 3, heads, DH), BF16),
            jax.ShapeDtypeStruct((rows, width), BF16),
            jax.ShapeDtypeStruct((tall // 2, DH), F32),
            jax.ShapeDtypeStruct((rows, model), BF16),
            jax.ShapeDtypeStruct((rows, DH), F32),
            jax.ShapeDtypeStruct((rows, DH), F32),
        ),
        in_specs=[any_space] * 5,
        out_specs=(vmem,) * 6,
        scratch_shapes=[
            pltpu.SMEM((reqs,), jnp.int32),
            pltpu.SMEM((reqs,), jnp.int32),
            pltpu.VMEM(inputs.shape, BF16),
            pltpu.VMEM((model, width), BF16),
            pltpu.VMEM(cache_keys.shape, BF16),
            pltpu.VMEM(cache_values.shape, BF16),
            pltpu.VMEM((rows, model), F32),
            pltpu.VMEM((rows * heads, DH), F32),
            pltpu.SemaphoreType.DMA,
            pltpu.SemaphoreType.DMA,
            pltpu.SemaphoreType.DMA,
            pltpu.SemaphoreType.DMA((reqs,)),
            pltpu.SemaphoreType.DMA((reqs,)),
        ],
        compiler_params=pltpu.CompilerParams(vmem_limit_bytes=48 << 20),
        name="cached_attention",
    )(in_hbm(lengths), in_hbm(inputs), in_hbm(w_qkv), in_hbm(cache_keys), in_hbm(cache_values))

    got = lax.all_to_all(part, "seq", 0, 0)

    piece = jax.ShapeDtypeStruct((reqs, steps, width), BF16)
    queries, new_keys, new_values, fresh, w_proj = pl.pallas_call(
        fresh_kernel,
        out_shape=(
            piece, piece, piece,
            jax.ShapeDtypeStruct((3, tall // 2, DH), F32),
            jax.ShapeDtypeStruct(w_out.shape, BF16),
        ),
        in_specs=[any_space] * 2 + [vmem] * 5,
        out_specs=(vmem,) * 5,
        scratch_shapes=[
            pltpu.VMEM((2, model, width), BF16),
            pltpu.VMEM((rows, width), F32),
            pltpu.VMEM((rows, width), F32),
            pltpu.VMEM((8 * heads, DH), F32),
            pltpu.VMEM((8 * heads, DH), F32),
            pltpu.SemaphoreType.DMA((2,)),
            pltpu.SemaphoreType.DMA,
        ],
        compiler_params=pltpu.CompilerParams(vmem_limit_bytes=14 << 20),
        name="new_tokens",
    )(in_hbm(w_qkv), in_hbm(w_out), q_rows, q_own, normed, cosine, sine)
    mine = pl.pallas_call(
        merge_kernel,
        out_shape=jax.ShapeDtypeStruct((2, model), F32),
        in_specs=[vmem] * 3,
        out_specs=vmem,
        scratch_shapes=[pltpu.VMEM((tall // 2, DH), F32)],
        compiler_params=pltpu.CompilerParams(vmem_limit_bytes=4 << 20),
        cost_estimate=pl.CostEstimate(flops=10**10, transcendentals=0, bytes_accessed=60 << 20),
        name="merge_project",
    )(got, fresh, w_proj)
    others = to_others([mine] * 3, "mp")

    cols = model // n_mp
    rows2 = jax.ShapeDtypeStruct((2, model), F32)
    middle, down = pl.pallas_call(
        mlp_kernel,
        out_shape=(rows2,) * 2,
        in_specs=[vmem] * 7,
        out_specs=(vmem,) * 2,
        compiler_params=pltpu.CompilerParams(vmem_limit_bytes=8 << 20),
        name="mlp",
    )(inputs, w_gate_up, w_down, mine, *others[::-1])
    hidden = pl.pallas_call(
        last_kernel,
        out_shape=jax.ShapeDtypeStruct((n_seq, 2, cols), BF16),
        in_specs=[vmem] * 5,
        out_specs=vmem,
        compiler_params=pltpu.CompilerParams(vmem_limit_bytes=4 << 20),
        name="last_sum",
    )(middle, down, *to_others([down] * 3, "mp")[::-1])
    hidden = lax.all_to_all(hidden, "seq", 0, 0)
    return (hidden.reshape(reqs, steps, cols), queries, new_keys, new_values)


def solution(mesh):
    placed = (
        P(),
        P(None, None, "mp"),
        P("mp", None),
        P(None, None, "mp"),
        P("mp", None),
        P(None, "seq", "mp"),
        P(None, "seq", "mp"),
        P(),
    )
    return jax.shard_map(
        per_device,
        mesh=mesh,
        in_specs=placed,
        out_specs=(P(None, None, "mp"),) * 4,
        check_vma=False,
    )
```

```python
import functools

import jax
import jax.numpy as jnp
import numpy as np
from jax import lax
from jax.experimental import pallas as pl
from jax.experimental.pallas import tpu as pltpu
from jax.sharding import PartitionSpec as P

DH = 128
NEG = -1e30
EPS = 1e-05
SCALE = DH ** (-0.5)
F32 = jnp.float32
BF16 = jnp.bfloat16


def norm_rows(x):
    centred = x - jnp.mean(x, axis=-1, keepdims=True)
    variance = jnp.mean(centred * centred, axis=-1, keepdims=True)
    return centred * lax.rsqrt(variance + EPS)


def split3(v):
    a = v.astype(BF16).astype(F32)
    rest = v - a
    b = rest.astype(BF16).astype(F32)
    return a, b, rest - b


def frequencies():
    half = DH // 2
    values = np.float32(10000.0) ** (np.float32(-2.0) * np.arange(half, dtype=np.float32) / np.float32(DH))
    lane = lax.broadcasted_iota(jnp.int32, (8, DH), 1) % half
    freq = jnp.full((8, DH), float(values[0]), F32)
    for i in range(1, half):
        freq = jnp.where(lane == i, float(values[i]), freq)
    return freq


def turn(v, cosine, sine):
    return v * cosine + pltpu.roll(v, DH // 2, 1) * sine


def rounded(v):
    return v.astype(BF16).astype(F32)


def cached_kernel(
    group, reqs, steps, block, width,
    len_hbm, x_hbm, w_hbm, ck_hbm, cv_hbm,
    part_out, q_rows, q_own, normed_out, cos_out, sin_out,
    len_s, order_s, x_v, w_v, ck_v, cv_v, xs, q16, sem_l, sem_x, sem_w, sem_k, sem_v,
):
    heads = width // DH
    rows = reqs * steps
    tall = steps * heads
    half = tall // 2
    seq = lax.axis_index("seq")
    first = seq * block
    copy_l = pltpu.make_async_copy(len_hbm, len_s, sem_l)
    copy_l.start()
    copy_x = pltpu.make_async_copy(x_hbm, x_v, sem_x)
    copy_x.start()
    copy_w = pltpu.make_async_copy(w_hbm.at[0], w_v, sem_w)
    copy_w.start()

    copy_l.wait()
    count = jnp.int32(0)
    for r in range(reqs):
        live = len_s[r] > first
        order_s[jnp.where(live, count, reqs - 1 - r + count)] = r
        count = count + live.astype(jnp.int32)

    def copies(cache, held, sems, lo):
        return [
            pltpu.make_async_copy(cache.at[order_s[i]], held.at[i], sems.at[i]) for i in range(lo, lo + group)
        ]

    def fetch(*args):
        for c in copies(*args):
            c.start()

    def arrive(*args):
        for c in copies(*args):
            c.wait()

    fetch(ck_hbm, ck_v, sem_k, 0)

    freq = frequencies()
    step_of = (lax.broadcasted_iota(jnp.int32, (8, DH), 0) % steps).astype(F32)
    lane8 = lax.broadcasted_iota(jnp.int32, (8, DH), 1)
    upper = lax.broadcasted_iota(jnp.int32, (8, DH), 0) >= steps
    for r in range(0, reqs, 2):
        place = jnp.where(upper, len_s[r + 1], len_s[r]).astype(F32) + step_of
        angles = place * freq
        cos_out[r * steps : (r + 2) * steps, :] = jnp.cos(angles)
        sine = jnp.sin(angles)
        sin_out[r * steps : (r + 2) * steps, :] = jnp.where(lane8 < DH // 2, -sine, sine)

    lane = lax.broadcasted_iota(jnp.int32, (tall, DH), 1)
    empty = jnp.where(lane[0:heads] % (DH // 2) == 0, NEG, 0.0).astype(BF16)
    for p in range(2 * reqs):
        part_out[p, 0] = jnp.zeros((heads, DH), BF16)
        part_out[p, 1] = jnp.zeros((heads, DH), BF16)
        part_out[p, 2] = empty

    copy_x.wait()
    fetch(cv_hbm, cv_v, sem_v, 0)
    for r in range(reqs):
        xs[pl.ds(r * steps, steps), :] = x_v[r].astype(F32)
    normed_out[...] = norm_rows(xs[...]).astype(BF16)

    copy_w.wait()
    part = jnp.dot(normed_out[...], w_v[...], preferred_element_type=F32)
    for h in range(heads):
        q = turn(part[:, h * DH : (h + 1) * DH], cos_out[...], sin_out[...]).astype(BF16)
        q_rows[:, h * DH : (h + 1) * DH] = q
        q16[pl.ds(h, rows, stride=heads), :] = q.astype(F32)
    q_own[...] = q16[pl.ds(seq * half, half), :]

    row_head = lax.broadcasted_iota(jnp.int32, (tall, DH), 0) % heads
    many_lane = lax.broadcasted_iota(jnp.int32, (group * tall, DH), 1)

    def attend(lo):
        arrive(ck_hbm, ck_v, sem_k, lo)
        scores = []
        for i in range(lo, lo + group):
            r = order_s[i]
            q = q16[pl.ds(pl.multiple_of(r * tall, tall), tall), :]
            spread = jnp.concatenate([jnp.where(row_head == h, q, 0.0).astype(BF16) for h in range(heads)], axis=1)
            score = lax.dot_general(spread, ck_v[i], (((1,), (1,)), ((), ())), preferred_element_type=F32)
            scores.append(jnp.where(lane < len_s[r] - first, score * SCALE, NEG))
        scores = jnp.concatenate(scores, axis=0)
        highest = jnp.max(scores, axis=-1, keepdims=True)
        weights = jnp.where(scores == NEG, 0.0, jnp.exp(scores - highest))
        total = jnp.sum(weights, axis=-1, keepdims=True)
        weights = weights.astype(BF16)
        pieces = split3(jnp.broadcast_to(highest, scores.shape)) + split3(jnp.broadcast_to(total, scores.shape))
        stats = pieces[5]
        for i in range(4, -1, -1):
            stats = jnp.where(many_lane % (DH // 2) == i, pieces[i], stats)
        arrive(cv_hbm, cv_v, sem_v, lo)
        for i in range(lo, lo + group):
            r = order_s[i]
            at = (i - lo) * tall
            wide = jnp.dot(weights[at : at + tall], cv_v[i], preferred_element_type=F32)
            o = wide[:, 0:DH]
            for h in range(1, heads):
                o = jnp.where(row_head == h, wide[:, h * DH : (h + 1) * DH], o)
            for j in range(2):
                lo_row = 2 * j * heads
                for k in range(2):
                    part_out[2 * r + j, k] = o[lo_row + k * heads : lo_row + (k + 1) * heads].astype(BF16)
                pair = [stats[at + lo_row + k * heads : at + lo_row + (k + 1) * heads] for k in range(2)]
                part_out[2 * r + j, 2] = jnp.where(lane[0:heads] < DH // 2, pair[0], pair[1]).astype(BF16)

    attend(0)
    for lo in range(group, reqs, group):
        @pl.when(count > lo)
        def _():
            fetch(ck_hbm, ck_v, sem_k, lo)
            fetch(cv_hbm, cv_v, sem_v, lo)
            attend(lo)


def fresh_kernel(
    w_hbm, proj_hbm, q_rows, q_own, normed, cosine, sine,
    q_out, k_out, v_out, fresh_out, proj_out,
    w_v, k_s, v_s, k16, v16, sem_w, sem_p,
):
    reqs, steps, width = q_out.shape
    half = q_own.shape[0]
    heads = half // 2
    tall = 2 * half
    seq = lax.axis_index("seq")
    copies = [pltpu.make_async_copy(w_hbm.at[1 + j], w_v.at[j], sem_w.at[j]) for j in range(2)]
    for c in copies:
        c.start()
    copy_p = pltpu.make_async_copy(proj_hbm, proj_out, sem_p)
    copy_p.start()
    q_out[...] = q_rows[...].reshape(q_out.shape)
    block = pl.multiple_of((seq // 4) * 8, 8)
    for j, (out, whole, store) in enumerate(((k_out, k_s, k16), (v_out, v_s, v16))):
        copies[j].wait()
        part = jnp.dot(normed[...], w_v[j], preferred_element_type=F32)
        for h in range(heads):
            span = slice(h * DH, (h + 1) * DH)
            v = part[:, span]
            v = (turn(v, cosine[...], sine[...]) if j == 0 else v).astype(BF16)
            out[:, :, span] = v.reshape(reqs, steps, DH)
            whole[:, span] = v.astype(F32)
        for h in range(heads):
            store[pl.ds(h, 8, stride=heads), :] = whole[pl.ds(block, 8), h * DH : (h + 1) * DH]
    q = q_own[...]
    step = (seq % 2) * 2 + lax.broadcasted_iota(jnp.int32, (half, 1), 0) // heads
    base = pl.multiple_of(((seq // 2) % 2) * tall, tall)
    scores = []
    values = []
    for s in range(steps):
        key = k16[pl.ds(base + s * heads, heads), :]
        value = v16[pl.ds(base + s * heads, heads), :]
        key = jnp.concatenate([key, key], axis=0)
        values.append(jnp.concatenate([value, value], axis=0))
        scores.append(jnp.sum(q * key, axis=-1, keepdims=True) * SCALE)
    high = scores[0]
    for s in range(1, steps):
        high = jnp.maximum(high, jnp.where(s <= step, scores[s], NEG))
    total = jnp.zeros_like(high)
    o = jnp.zeros((half, DH), F32)
    for s in range(steps):
        weight = jnp.where(s <= step, jnp.exp(scores[s] - high), 0.0)
        total = total + weight
        o = o + rounded(weight) * values[s]
    fresh_out[0] = o
    fresh_out[1] = jnp.broadcast_to(high, o.shape)
    fresh_out[2] = jnp.broadcast_to(total, o.shape)
    copy_p.wait()


def merge_kernel(got_ref, fresh_ref, w_ref, out_ref, ctx_s):
    heads = got_ref.shape[2]
    stats = got_ref[:, 2].astype(F32)
    for k in range(2):
        span = slice(k * heads, (k + 1) * heads)
        fresh, fresh_high, fresh_total = fresh_ref[0][span], fresh_ref[1][span, 0:1], fresh_ref[2][span, 0:1]
        at = [stats[:, :, k * DH // 2 + i : k * DH // 2 + i + 1] for i in range(6)]
        highest = (at[0] + at[1]) + at[2]
        total = (at[3] + at[4]) + at[5]
        top = jnp.maximum(jnp.max(highest, axis=0), fresh_high)
        factor = jnp.exp(highest - top[None])
        fresh_factor = jnp.exp(fresh_high - top)
        whole = jnp.sum(factor * total, axis=0) + fresh_factor * fresh_total
        o = jnp.sum(factor * got_ref[:, k].astype(F32), axis=0) + fresh_factor * fresh
        ctx_s[span, :] = o / whole
    ctx = jnp.concatenate([ctx_s[pl.ds(h, 2, stride=heads), :] for h in range(heads)], axis=1)
    out_ref[...] = jnp.dot(ctx.astype(BF16), w_ref[...], preferred_element_type=F32)


def mlp_kernel(x_ref, gu_ref, wd_ref, near_ref, far_ref, middle_out, down_out):
    seq = lax.axis_index("seq")
    x = x_ref[seq // 2].astype(F32)
    x = jnp.where(seq % 2 == 0, x[0:2], x[2:4])
    middle = x + (near_ref[...] + far_ref[...])
    middle_out[...] = middle
    normed = norm_rows(middle).astype(BF16)
    gate = jnp.dot(normed, gu_ref[0], preferred_element_type=F32)
    up = jnp.dot(normed, gu_ref[1], preferred_element_type=F32)
    active = ((gate / (1.0 + jnp.exp(-gate))) * up).astype(BF16)
    down_out[...] = jnp.dot(active, wd_ref[...], preferred_element_type=F32)


def last_kernel(middle_ref, near_ref, far_ref, out_ref):
    cols = out_ref.shape[2]
    span = pl.ds(pl.multiple_of(lax.axis_index("mp") * cols, cols), cols)
    down = near_ref[:, span] + far_ref[:, span]
    hidden = (middle_ref[:, span] + down).astype(BF16)
    out_ref[...] = jnp.broadcast_to(hidden[None], out_ref.shape)


def halves(v, axis):
    size = lax.axis_size(axis)
    near = v + lax.ppermute(v, axis, [(i, i ^ 1) for i in range(size)])
    return near, lax.ppermute(near, axis, [(i, i ^ 2) for i in range(size)])


def per_device(inputs, w_qkv, w_out, w_gate_up, w_down, cache_keys, cache_values, lengths):
    reqs, steps, model = inputs.shape
    block = cache_keys.shape[1]
    width = cache_keys.shape[2]
    heads = width // DH
    rows = reqs * steps
    tall = steps * heads
    n_seq = lax.axis_size("seq")
    n_mp = lax.axis_size("mp")
    assert rows == 2 * n_seq and steps == 4 and n_mp == 4 and tall == 16
    group = max(reqs // 2, 1)
    in_hbm = functools.partial(pltpu.with_memory_space_constraint, memory_space=pltpu.HBM)
    any_space = pl.BlockSpec(memory_space=pltpu.HBM)
    vmem = pl.BlockSpec(memory_space=pltpu.VMEM)
    part, q_rows, q_own, normed, cosine, sine = pl.pallas_call(
        functools.partial(cached_kernel, group, reqs, steps, block, width),
        out_shape=(
            jax.ShapeDtypeStruct((n_seq, 3, heads, DH), BF16),
            jax.ShapeDtypeStruct((rows, width), BF16),
            jax.ShapeDtypeStruct((tall // 2, DH), F32),
            jax.ShapeDtypeStruct((rows, model), BF16),
            jax.ShapeDtypeStruct((rows, DH), F32),
            jax.ShapeDtypeStruct((rows, DH), F32),
        ),
        in_specs=[any_space] * 5,
        out_specs=(vmem,) * 6,
        scratch_shapes=[
            pltpu.SMEM((reqs,), jnp.int32),
            pltpu.SMEM((reqs,), jnp.int32),
            pltpu.VMEM(inputs.shape, BF16),
            pltpu.VMEM((model, width), BF16),
            pltpu.VMEM(cache_keys.shape, BF16),
            pltpu.VMEM(cache_values.shape, BF16),
            pltpu.VMEM((rows, model), F32),
            pltpu.VMEM((rows * heads, DH), F32),
            pltpu.SemaphoreType.DMA,
            pltpu.SemaphoreType.DMA,
            pltpu.SemaphoreType.DMA,
            pltpu.SemaphoreType.DMA((reqs,)),
            pltpu.SemaphoreType.DMA((reqs,)),
        ],
        compiler_params=pltpu.CompilerParams(vmem_limit_bytes=48 << 20),
        name="cached_attention",
    )(in_hbm(lengths), in_hbm(inputs), in_hbm(w_qkv), in_hbm(cache_keys), in_hbm(cache_values))

    got = lax.all_to_all(part, "seq", 0, 0)

    piece = jax.ShapeDtypeStruct((reqs, steps, width), BF16)
    queries, new_keys, new_values, fresh, w_proj = pl.pallas_call(
        fresh_kernel,
        out_shape=(
            piece, piece, piece,
            jax.ShapeDtypeStruct((3, tall // 2, DH), F32),
            jax.ShapeDtypeStruct(w_out.shape, BF16),
        ),
        in_specs=[any_space] * 2 + [vmem] * 5,
        out_specs=(vmem,) * 5,
        scratch_shapes=[
            pltpu.VMEM((2, model, width), BF16),
            pltpu.VMEM((rows, width), F32),
            pltpu.VMEM((rows, width), F32),
            pltpu.VMEM((8 * heads, DH), F32),
            pltpu.VMEM((8 * heads, DH), F32),
            pltpu.SemaphoreType.DMA((2,)),
            pltpu.SemaphoreType.DMA,
        ],
        compiler_params=pltpu.CompilerParams(vmem_limit_bytes=14 << 20),
        name="new_tokens",
    )(in_hbm(w_qkv), in_hbm(w_out), q_rows, q_own, normed, cosine, sine)
    mine = pl.pallas_call(
        merge_kernel,
        out_shape=jax.ShapeDtypeStruct((2, model), F32),
        in_specs=[vmem] * 3,
        out_specs=vmem,
        scratch_shapes=[pltpu.VMEM((tall // 2, DH), F32)],
        compiler_params=pltpu.CompilerParams(vmem_limit_bytes=4 << 20),
        cost_estimate=pl.CostEstimate(flops=10**10, transcendentals=0, bytes_accessed=60 << 20),
        name="merge_project",
    )(got, fresh, w_proj)

    cols = model // n_mp
    rows2 = jax.ShapeDtypeStruct((2, model), F32)
    middle, down = pl.pallas_call(
        mlp_kernel,
        out_shape=(rows2,) * 2,
        in_specs=[vmem] * 5,
        out_specs=(vmem,) * 2,
        compiler_params=pltpu.CompilerParams(vmem_limit_bytes=8 << 20),
        name="mlp",
    )(inputs, w_gate_up, w_down, *halves(mine, "mp"))
    hidden = pl.pallas_call(
        last_kernel,
        out_shape=jax.ShapeDtypeStruct((n_seq, 2, cols), BF16),
        in_specs=[vmem] * 3,
        out_specs=vmem,
        compiler_params=pltpu.CompilerParams(vmem_limit_bytes=4 << 20),
        name="last_sum",
    )(middle, *halves(down, "mp"))
    hidden = lax.all_to_all(hidden, "seq", 0, 0)
    return (hidden.reshape(reqs, steps, cols), queries, new_keys, new_values)


def solution(mesh):
    placed = (
        P(),
        P(None, None, "mp"),
        P("mp", None),
        P(None, None, "mp"),
        P("mp", None),
        P(None, "seq", "mp"),
        P(None, "seq", "mp"),
        P(),
    )
    return jax.shard_map(
        per_device,
        mesh=mesh,
        in_specs=placed,
        out_specs=(P(None, None, "mp"),) * 4,
        check_vma=False,
    )
```

```python
import functools

import jax
import jax.numpy as jnp
import numpy as np
from jax import lax
from jax.experimental import pallas as pl
from jax.experimental.pallas import tpu as pltpu
from jax.sharding import PartitionSpec as P

DH = 128
NEG = -1e30
EPS = 1e-05
SCALE = DH ** (-0.5)
F32 = jnp.float32
BF16 = jnp.bfloat16


def norm_rows(x):
    centred = x - jnp.mean(x, axis=-1, keepdims=True)
    variance = jnp.mean(centred * centred, axis=-1, keepdims=True)
    return centred * lax.rsqrt(variance + EPS)


def split3(v):
    a = v.astype(BF16).astype(F32)
    rest = v - a
    b = rest.astype(BF16).astype(F32)
    return a, b, rest - b


def frequencies():
    half = DH // 2
    values = np.float32(10000.0) ** (np.float32(-2.0) * np.arange(half, dtype=np.float32) / np.float32(DH))
    lane = lax.broadcasted_iota(jnp.int32, (8, DH), 1) % half
    freq = jnp.full((8, DH), float(values[0]), F32)
    for i in range(1, half):
        freq = jnp.where(lane == i, float(values[i]), freq)
    return freq


def turn(v, cosine, sine):
    return v * cosine + pltpu.roll(v, DH // 2, 1) * sine


def rounded(v):
    return v.astype(BF16).astype(F32)


def cached_kernel(
    group, reqs, steps, block, width,
    len_hbm, x_hbm, w_hbm, ck_hbm, cv_hbm,
    part_out, q_rows, q_own, normed_out, cos_out, sin_out,
    len_s, order_s, x_v, w_v, ck_v, cv_v, xs, q16, sem_l, sem_x, sem_w, sem_k, sem_v,
):
    heads = width // DH
    rows = reqs * steps
    tall = steps * heads
    half = tall // 2
    seq = lax.axis_index("seq")
    first = seq * block
    copy_l = pltpu.make_async_copy(len_hbm, len_s, sem_l)
    copy_l.start()
    copy_x = pltpu.make_async_copy(x_hbm, x_v, sem_x)
    copy_x.start()
    depth = w_v.shape[0] // 2
    copies_w = [
        pltpu.make_async_copy(w_hbm.at[0, pl.ds(i * depth, depth)], w_v.at[pl.ds(i * depth, depth)], sem_w.at[i])
        for i in range(2)
    ]
    for c in copies_w:
        c.start()

    copy_l.wait()
    count = jnp.int32(0)
    for r in range(reqs):
        live = len_s[r] > first
        order_s[jnp.where(live, count, reqs - 1 - r + count)] = r
        count = count + live.astype(jnp.int32)

    def copies(cache, held, sems, lo):
        return [
            pltpu.make_async_copy(cache.at[order_s[i]], held.at[i], sems.at[i]) for i in range(lo, lo + group)
        ]

    def fetch(*args):
        for c in copies(*args):
            c.start()

    def arrive(*args):
        for c in copies(*args):
            c.wait()

    fetch(ck_hbm, ck_v, sem_k, 0)

    freq = frequencies()
    step_of = (lax.broadcasted_iota(jnp.int32, (8, DH), 0) % steps).astype(F32)
    lane8 = lax.broadcasted_iota(jnp.int32, (8, DH), 1)
    upper = lax.broadcasted_iota(jnp.int32, (8, DH), 0) >= steps
    for r in range(0, reqs, 2):
        place = jnp.where(upper, len_s[r + 1], len_s[r]).astype(F32) + step_of
        angles = place * freq
        cos_out[r * steps : (r + 2) * steps, :] = jnp.cos(angles)
        sine = jnp.sin(angles)
        sin_out[r * steps : (r + 2) * steps, :] = jnp.where(lane8 < DH // 2, -sine, sine)

    lane = lax.broadcasted_iota(jnp.int32, (tall, DH), 1)
    empty = jnp.where(lane[0:heads] % (DH // 2) == 0, NEG, 0.0).astype(BF16)
    for p in range(2 * reqs):
        part_out[p, 0] = jnp.zeros((heads, DH), BF16)
        part_out[p, 1] = jnp.zeros((heads, DH), BF16)
        part_out[p, 2] = empty

    copy_x.wait()
    fetch(cv_hbm, cv_v, sem_v, 0)
    for r in range(reqs):
        xs[pl.ds(r * steps, steps), :] = x_v[r].astype(F32)
    normed_out[...] = norm_rows(xs[...]).astype(BF16)

    copies_w[0].wait()
    part = jnp.dot(normed_out[:, :depth], w_v[:depth], preferred_element_type=F32)
    copies_w[1].wait()
    part = part + jnp.dot(normed_out[:, depth:], w_v[depth:], preferred_element_type=F32)
    for h in range(heads):
        q = turn(part[:, h * DH : (h + 1) * DH], cos_out[...], sin_out[...]).astype(BF16)
        q_rows[:, h * DH : (h + 1) * DH] = q
        q16[pl.ds(h, rows, stride=heads), :] = q.astype(F32)
    q_own[...] = q16[pl.ds(seq * half, half), :]

    row_head = lax.broadcasted_iota(jnp.int32, (tall, DH), 0) % heads
    many_lane = lax.broadcasted_iota(jnp.int32, (group * tall, DH), 1)

    def attend(lo):
        arrive(ck_hbm, ck_v, sem_k, lo)
        scores = []
        for i in range(lo, lo + group):
            r = order_s[i]
            q = q16[pl.ds(pl.multiple_of(r * tall, tall), tall), :]
            spread = jnp.concatenate([jnp.where(row_head == h, q, 0.0).astype(BF16) for h in range(heads)], axis=1)
            score = lax.dot_general(spread, ck_v[i], (((1,), (1,)), ((), ())), preferred_element_type=F32)
            scores.append(jnp.where(lane < len_s[r] - first, score * SCALE, NEG))
        scores = jnp.concatenate(scores, axis=0)
        highest = jnp.max(scores, axis=-1, keepdims=True)
        weights = jnp.where(scores == NEG, 0.0, jnp.exp(scores - highest))
        total = jnp.sum(weights, axis=-1, keepdims=True)
        weights = weights.astype(BF16)
        pieces = split3(jnp.broadcast_to(highest, scores.shape)) + split3(jnp.broadcast_to(total, scores.shape))
        stats = pieces[5]
        for i in range(4, -1, -1):
            stats = jnp.where(many_lane % (DH // 2) == i, pieces[i], stats)
        arrive(cv_hbm, cv_v, sem_v, lo)
        for i in range(lo, lo + group):
            r = order_s[i]
            at = (i - lo) * tall
            wide = jnp.dot(weights[at : at + tall], cv_v[i], preferred_element_type=F32)
            o = wide[:, 0:DH]
            for h in range(1, heads):
                o = jnp.where(row_head == h, wide[:, h * DH : (h + 1) * DH], o)
            for j in range(2):
                lo_row = 2 * j * heads
                for k in range(2):
                    part_out[2 * r + j, k] = o[lo_row + k * heads : lo_row + (k + 1) * heads].astype(BF16)
                pair = [stats[at + lo_row + k * heads : at + lo_row + (k + 1) * heads] for k in range(2)]
                part_out[2 * r + j, 2] = jnp.where(lane[0:heads] < DH // 2, pair[0], pair[1]).astype(BF16)

    attend(0)
    for lo in range(group, reqs, group):
        @pl.when(count > lo)
        def _():
            fetch(ck_hbm, ck_v, sem_k, lo)
            fetch(cv_hbm, cv_v, sem_v, lo)
            attend(lo)


def fresh_kernel(
    w_hbm, proj_hbm, q_rows, q_own, normed, cosine, sine,
    q_out, k_out, v_out, fresh_out, proj_out,
    w_v, k_s, v_s, k16, v16, sem_w, sem_p,
):
    reqs, steps, width = q_out.shape
    half = q_own.shape[0]
    heads = half // 2
    tall = 2 * half
    seq = lax.axis_index("seq")
    copies = [pltpu.make_async_copy(w_hbm.at[1 + j], w_v.at[j], sem_w.at[j]) for j in range(2)]
    for c in copies:
        c.start()
    copy_p = pltpu.make_async_copy(proj_hbm, proj_out, sem_p)
    copy_p.start()
    q_out[...] = q_rows[...].reshape(q_out.shape)
    block = pl.multiple_of((seq // 4) * 8, 8)
    for j, (out, whole, store) in enumerate(((k_out, k_s, k16), (v_out, v_s, v16))):
        copies[j].wait()
        part = jnp.dot(normed[...], w_v[j], preferred_element_type=F32)
        for h in range(heads):
            span = slice(h * DH, (h + 1) * DH)
            v = part[:, span]
            v = (turn(v, cosine[...], sine[...]) if j == 0 else v).astype(BF16)
            out[:, :, span] = v.reshape(reqs, steps, DH)
            whole[:, span] = v.astype(F32)
        for h in range(heads):
            store[pl.ds(h, 8, stride=heads), :] = whole[pl.ds(block, 8), h * DH : (h + 1) * DH]
    q = q_own[...]
    step = (seq % 2) * 2 + lax.broadcasted_iota(jnp.int32, (half, 1), 0) // heads
    base = pl.multiple_of(((seq // 2) % 2) * tall, tall)
    scores = []
    values = []
    for s in range(steps):
        key = k16[pl.ds(base + s * heads, heads), :]
        value = v16[pl.ds(base + s * heads, heads), :]
        key = jnp.concatenate([key, key], axis=0)
        values.append(jnp.concatenate([value, value], axis=0))
        scores.append(jnp.sum(q * key, axis=-1, keepdims=True) * SCALE)
    high = scores[0]
    for s in range(1, steps):
        high = jnp.maximum(high, jnp.where(s <= step, scores[s], NEG))
    total = jnp.zeros_like(high)
    o = jnp.zeros((half, DH), F32)
    for s in range(steps):
        weight = jnp.where(s <= step, jnp.exp(scores[s] - high), 0.0)
        total = total + weight
        o = o + rounded(weight) * values[s]
    fresh_out[0] = o
    fresh_out[1] = jnp.broadcast_to(high, o.shape)
    fresh_out[2] = jnp.broadcast_to(total, o.shape)
    copy_p.wait()


def merge_kernel(got_ref, fresh_ref, w_ref, out_ref, ctx_s):
    heads = got_ref.shape[2]
    stats = got_ref[:, 2].astype(F32)
    for k in range(2):
        span = slice(k * heads, (k + 1) * heads)
        fresh, fresh_high, fresh_total = fresh_ref[0][span], fresh_ref[1][span, 0:1], fresh_ref[2][span, 0:1]
        at = [stats[:, :, k * DH // 2 + i : k * DH // 2 + i + 1] for i in range(6)]
        highest = (at[0] + at[1]) + at[2]
        total = (at[3] + at[4]) + at[5]
        top = jnp.maximum(jnp.max(highest, axis=0), fresh_high)
        factor = jnp.exp(highest - top[None])
        fresh_factor = jnp.exp(fresh_high - top)
        whole = jnp.sum(factor * total, axis=0) + fresh_factor * fresh_total
        o = jnp.sum(factor * got_ref[:, k].astype(F32), axis=0) + fresh_factor * fresh
        ctx_s[span, :] = o / whole
    ctx = jnp.concatenate([ctx_s[pl.ds(h, 2, stride=heads), :] for h in range(heads)], axis=1)
    out_ref[...] = jnp.dot(ctx.astype(BF16), w_ref[...], preferred_element_type=F32)


def mlp_kernel(x_ref, gu_ref, wd_ref, near_ref, far_ref, middle_out, down_out):
    seq = lax.axis_index("seq")
    x = x_ref[seq // 2].astype(F32)
    x = jnp.where(seq % 2 == 0, x[0:2], x[2:4])
    middle = x + (near_ref[...] + far_ref[...])
    middle_out[...] = middle
    normed = norm_rows(middle).astype(BF16)
    gate = jnp.dot(normed, gu_ref[0], preferred_element_type=F32)
    up = jnp.dot(normed, gu_ref[1], preferred_element_type=F32)
    active = ((gate / (1.0 + jnp.exp(-gate))) * up).astype(BF16)
    down_out[...] = jnp.dot(active, wd_ref[...], preferred_element_type=F32)


def last_kernel(middle_ref, near_ref, far_ref, out_ref):
    cols = out_ref.shape[2]
    span = pl.ds(pl.multiple_of(lax.axis_index("mp") * cols, cols), cols)
    down = near_ref[:, span] + far_ref[:, span]
    hidden = (middle_ref[:, span] + down).astype(BF16)
    out_ref[...] = jnp.broadcast_to(hidden[None], out_ref.shape)


def halves(v, axis):
    size = lax.axis_size(axis)
    near = v + lax.ppermute(v, axis, [(i, i ^ 1) for i in range(size)])
    return near, lax.ppermute(near, axis, [(i, i ^ 2) for i in range(size)])


def per_device(inputs, w_qkv, w_out, w_gate_up, w_down, cache_keys, cache_values, lengths):
    reqs, steps, model = inputs.shape
    block = cache_keys.shape[1]
    width = cache_keys.shape[2]
    heads = width // DH
    rows = reqs * steps
    tall = steps * heads
    n_seq = lax.axis_size("seq")
    n_mp = lax.axis_size("mp")
    assert rows == 2 * n_seq and steps == 4 and n_mp == 4 and tall == 16
    group = max(reqs // 2, 1)
    in_hbm = functools.partial(pltpu.with_memory_space_constraint, memory_space=pltpu.HBM)
    any_space = pl.BlockSpec(memory_space=pltpu.HBM)
    vmem = pl.BlockSpec(memory_space=pltpu.VMEM)
    part, q_rows, q_own, normed, cosine, sine = pl.pallas_call(
        functools.partial(cached_kernel, group, reqs, steps, block, width),
        out_shape=(
            jax.ShapeDtypeStruct((n_seq, 3, heads, DH), BF16),
            jax.ShapeDtypeStruct((rows, width), BF16),
            jax.ShapeDtypeStruct((tall // 2, DH), F32),
            jax.ShapeDtypeStruct((rows, model), BF16),
            jax.ShapeDtypeStruct((rows, DH), F32),
            jax.ShapeDtypeStruct((rows, DH), F32),
        ),
        in_specs=[any_space] * 5,
        out_specs=(vmem,) * 6,
        scratch_shapes=[
            pltpu.SMEM((reqs,), jnp.int32),
            pltpu.SMEM((reqs,), jnp.int32),
            pltpu.VMEM(inputs.shape, BF16),
            pltpu.VMEM((model, width), BF16),
            pltpu.VMEM(cache_keys.shape, BF16),
            pltpu.VMEM(cache_values.shape, BF16),
            pltpu.VMEM((rows, model), F32),
            pltpu.VMEM((rows * heads, DH), F32),
            pltpu.SemaphoreType.DMA,
            pltpu.SemaphoreType.DMA,
            pltpu.SemaphoreType.DMA((2,)),
            pltpu.SemaphoreType.DMA((reqs,)),
            pltpu.SemaphoreType.DMA((reqs,)),
        ],
        compiler_params=pltpu.CompilerParams(vmem_limit_bytes=48 << 20),
        name="cached_attention",
    )(in_hbm(lengths), in_hbm(inputs), in_hbm(w_qkv), in_hbm(cache_keys), in_hbm(cache_values))

    got = lax.all_to_all(part, "seq", 0, 0)

    piece = jax.ShapeDtypeStruct((reqs, steps, width), BF16)
    queries, new_keys, new_values, fresh, w_proj = pl.pallas_call(
        fresh_kernel,
        out_shape=(
            piece, piece, piece,
            jax.ShapeDtypeStruct((3, tall // 2, DH), F32),
            jax.ShapeDtypeStruct(w_out.shape, BF16),
        ),
        in_specs=[any_space] * 2 + [vmem] * 5,
        out_specs=(vmem,) * 5,
        scratch_shapes=[
            pltpu.VMEM((2, model, width), BF16),
            pltpu.VMEM((rows, width), F32),
            pltpu.VMEM((rows, width), F32),
            pltpu.VMEM((8 * heads, DH), F32),
            pltpu.VMEM((8 * heads, DH), F32),
            pltpu.SemaphoreType.DMA((2,)),
            pltpu.SemaphoreType.DMA,
        ],
        compiler_params=pltpu.CompilerParams(vmem_limit_bytes=14 << 20),
        name="new_tokens",
    )(in_hbm(w_qkv), in_hbm(w_out), q_rows, q_own, normed, cosine, sine)
    mine = pl.pallas_call(
        merge_kernel,
        out_shape=jax.ShapeDtypeStruct((2, model), F32),
        in_specs=[vmem] * 3,
        out_specs=vmem,
        scratch_shapes=[pltpu.VMEM((tall // 2, DH), F32)],
        compiler_params=pltpu.CompilerParams(vmem_limit_bytes=4 << 20),
        cost_estimate=pl.CostEstimate(flops=10**10, transcendentals=0, bytes_accessed=60 << 20),
        name="merge_project",
    )(got, fresh, w_proj)

    cols = model // n_mp
    rows2 = jax.ShapeDtypeStruct((2, model), F32)
    middle, down = pl.pallas_call(
        mlp_kernel,
        out_shape=(rows2,) * 2,
        in_specs=[vmem] * 5,
        out_specs=(vmem,) * 2,
        compiler_params=pltpu.CompilerParams(vmem_limit_bytes=8 << 20),
        name="mlp",
    )(inputs, w_gate_up, w_down, *halves(mine, "mp"))
    hidden = pl.pallas_call(
        last_kernel,
        out_shape=jax.ShapeDtypeStruct((n_seq, 2, cols), BF16),
        in_specs=[vmem] * 3,
        out_specs=vmem,
        compiler_params=pltpu.CompilerParams(vmem_limit_bytes=4 << 20),
        name="last_sum",
    )(middle, *halves(down, "mp"))
    hidden = lax.all_to_all(hidden, "seq", 0, 0)
    return (hidden.reshape(reqs, steps, cols), queries, new_keys, new_values)


def solution(mesh):
    placed = (
        P(),
        P(None, None, "mp"),
        P("mp", None),
        P(None, None, "mp"),
        P("mp", None),
        P(None, "seq", "mp"),
        P(None, "seq", "mp"),
        P(),
    )
    return jax.shard_map(
        per_device,
        mesh=mesh,
        in_specs=placed,
        out_specs=(P(None, None, "mp"),) * 4,
        check_vma=False,
    )
```
